32 devices in a mesh: dp: 4 (over y, core), ctx: 4 (over z), tensor: 2 (over x).
Axes of the slice: x: 2, y: 2, z: 4, core: 2. Of those that a mesh axis runs over, the one named last changes fastest.
Arguments:
- block_input: float32 [1536, 12, 768], P(('ctx', 'tensor'), 'dp'), may hold values from -6 to 6
- out_cotangent: float32 [1536, 12, 768], P(('ctx', 'tensor'), 'dp'), may hold values from -6 to 6
- qkv_weight: float32 [768, 3, 768], P(('dp', 'ctx'), None, 'tensor'), may hold values from -0.21875 to 0.21875
- proj_weight: float32 [768, 768], P(('dp', 'ctx'), 'tensor'), may hold values from -4 to 4
- up_weight: float32 [768, 3072], P(('dp', 'ctx'), 'tensor'), may hold values from -0.21875 to 0.21875
- down_weight: float32 [768, 3072], P(('dp', 'ctx'), 'tensor'), may hold values from -0.109375 to 0.109375
- norm_gains: float32 [2, 768], P(None, ('dp', 'ctx')), may hold values from 0.1 to 1.9
- shift_terms: float32 [4, 768], P(None, ('dp', 'ctx')), may hold values from -1.5 to 1.5
- qv_bias: float32 [2, 12, 64], P(None, 'tensor', ('dp', 'ctx')), may hold values from -1.5 to 1.5
- up_bias: float32 [24, 128], P('tensor', ('dp', 'ctx')), may hold values from -1.5 to 1.5
- qkv_first: float32 [768, 3, 768], P(('dp', 'ctx'), None, 'tensor'), may hold values from -64 to 64
- qkv_second: float32 [768, 3, 768], P(('dp', 'ctx'), None, 'tensor'), may hold values from 13824 to 55296
- proj_first: float32 [768, 768], P(('dp', 'ctx'), 'tensor'), may hold values from -20 to 20
- proj_second: float32 [768, 768], P(('dp', 'ctx'), 'tensor'), may hold values from 44.2368 to 176.9472
- up_first: float32 [768, 3072], P(('dp', 'ctx'), 'tensor'), may hold values from -40 to 40
- up_second: float32 [768, 3072], P(('dp', 'ctx'), 'tensor'), may hold values from 129.024 to 516.096
- down_first: float32 [768, 3072], P(('dp', 'ctx'), 'tensor'), may hold values from -40 to 40
- down_second: float32 [768, 3072], P(('dp', 'ctx'), 'tensor'), may hold values from 221.184 to 884.736
- gains_first: float32 [2, 768], P(None, ('dp', 'ctx'))
- gains_second: float32 [2, 768], P(None, ('dp', 'ctx'))
- shifts_first: float32 [4, 768], P(None, ('dp', 'ctx'))
- shifts_second: float32 [4, 768], P(None, ('dp', 'ctx'))
- qv_bias_first: float32 [2, 12, 64], P(None, 'tensor', ('dp', 'ctx')), may hold values from -64 to 64
- qv_bias_second: float32 [2, 12, 64], P(None, 'tensor', ('dp', 'ctx')), may hold values from 1382400 to 5529600
- up_bias_first: float32 [24, 128], P('tensor', ('dp', 'ctx')), may hold values from -40 to 40
- up_bias_second: float32 [24, 128], P('tensor', ('dp', 'ctx')), may hold values from 23.04 to 92.16
Outputs:
- block_output: float32 [1536, 12, 768], P(('ctx', 'tensor'), 'dp')
- input_grad: float32 [1536, 12, 768], P(('ctx', 'tensor'), 'dp')
- qkv_grad: float32 [768, 3, 768], P(('dp', 'ctx'), None, 'tensor')
- proj_grad: float32 [768, 768], P(('dp', 'ctx'), 'tensor')
- up_weight_gradient: float32 [768, 3072], P(('dp', 'ctx'), 'tensor')
- down_weight_gradient: float32 [768, 3072], P(('dp', 'ctx'), 'tensor')
- gains_grad: float32 [2, 768], P(None, ('dp', 'ctx'))
- shifts_grad: float32 [4, 768], P(None, ('dp', 'ctx'))
- qv_bias_grad: float32 [2, 12, 64], P(None, 'tensor', ('dp', 'ctx'))
- up_bias_grad: float32 [24, 128], P('tensor', ('dp', 'ctx'))
- qkv_new: float32 [768, 3, 768], P(('dp', 'ctx'), None, 'tensor')
- proj_new: float32 [768, 768], P(('dp', 'ctx'), 'tensor')
- up_new: float32 [768, 3072], P(('dp', 'ctx'), 'tensor')
- down_new: float32 [768, 3072], P(('dp', 'ctx'), 'tensor')
- gains_new: float32 [2, 768], P(None, ('dp', 'ctx'))
- shifts_new: float32 [4, 768], P(None, ('dp', 'ctx'))
- qv_bias_new: float32 [2, 12, 64], P(None, 'tensor', ('dp', 'ctx'))
- up_bias_new: float32 [24, 128], P('tensor', ('dp', 'ctx'))
- qkv_first_next: float32 [768, 3, 768], P(('dp', 'ctx'), None, 'tensor')
- qkv_second_next: float32 [768, 3, 768], P(('dp', 'ctx'), None, 'tensor')
- proj_first_next: float32 [768, 768], P(('dp', 'ctx'), 'tensor')
- proj_second_next: float32 [768, 768], P(('dp', 'ctx'), 'tensor')
- up_first_next: float32 [768, 3072], P(('dp', 'ctx'), 'tensor')
- up_second_next: float32 [768, 3072], P(('dp', 'ctx'), 'tensor')
- down_first_next: float32 [768, 3072], P(('dp', 'ctx'), 'tensor')
- down_second_next: float32 [768, 3072], P(('dp', 'ctx'), 'tensor')
- gains_first_next: float32 [2, 768], P(None, ('dp', 'ctx'))
- gains_second_next: float32 [2, 768], P(None, ('dp', 'ctx'))
- shifts_first_next: float32 [4, 768], P(None, ('dp', 'ctx'))
- shifts_second_next: float32 [4, 768], P(None, ('dp', 'ctx'))
- qv_bias_first_next: float32 [2, 12, 64], P(None, 'tensor', ('dp', 'ctx'))
- qv_bias_second_next: float32 [2, 12, 64], P(None, 'tensor', ('dp', 'ctx'))
- up_bias_first_next: float32 [24, 128], P('tensor', ('dp', 'ctx'))
- up_bias_second_next: float32 [24, 128], P('tensor', ('dp', 'ctx'))
The draws below stay inside these ranges and needn't reach their ends.
All inputs are finite; a program needn't handle non-finite values.
Results may differ from the reference program's by a relative error of at most 0.014.
Values may be sent and summed in bfloat16 or wider, within the bound.
A program may use at most 256 MiB of HBM per device.

```python
import math
import jax
import jax.numpy as jnp
from jax import lax

D = 768
HEADS = 12
HD = 64
FF = 3072
STEP = 4
FRAMES = 1536
CLIPS_ALL = 12


def gains_rows():
    return jnp.array([8.0 * CLIPS_ALL * D, 2.0 * FRAMES * CLIPS_ALL], jnp.float32)


def shifts_rows():
    return jnp.array([8.0 * CLIPS_ALL * D, 2.0 * FRAMES * CLIPS_ALL, 1.0 * FRAMES * CLIPS_ALL, 1.0 * FRAMES * CLIPS_ALL], jnp.float32)


def first_draw(key, row_sizes):
    values = jnp.clip(jax.random.normal(key, (row_sizes.shape[0], D), jnp.float32), -6.0, 6.0)
    return values * (0.07 * jnp.sqrt(row_sizes))[:, None]


def second_draw(key, row_sizes, level):
    factor = jnp.exp(jax.random.uniform(key, (row_sizes.shape[0], D), jnp.float32, 0.0, 1.3862944))
    return factor * (level * row_sizes)[:, None]


def draw_gains_first(key, part):
    return first_draw(key, gains_rows())


def draw_gains_second(key, part):
    return second_draw(key, gains_rows(), 0.2)


def draw_shifts_first(key, part):
    return first_draw(key, shifts_rows())


def draw_shifts_second(key, part):
    return second_draw(key, shifts_rows(), 1.0)


def level_of(key, extent, split, least, largest):
    gain = 1.0
    for position, parts in split:
        draws = jax.random.uniform(jax.random.fold_in(jax.random.fold_in(key, 6), position), (parts,), jnp.float32, least / len(split), largest / len(split))
        gain = gain * jnp.repeat(jnp.exp(draws), extent[position] // parts).reshape((-1,) + (1,) * (len(extent) - 1 - position))
    return gain


def gaussian(key, shape, width, limit, cuts=(), kind=jnp.bfloat16):
    factor_of = level_of(key, shape, cuts, -0.22, 0.18) if cuts else 1.0
    result = jax.random.normal(key, shape, jnp.float32) * width * factor_of
    return jnp.minimum(jnp.maximum(result, -limit), limit).astype(kind)


def setup_inputs(seed: int = 0) -> dict:
    key_of = jax.random.split(jax.random.key(seed), 27)
    block_input = gaussian(key_of[0], (FRAMES, CLIPS_ALL, D), 1.0, 6.0, ((0, 8), (1, 4)), jnp.float32)
    out_cotangent = gaussian(key_of[1], (FRAMES, CLIPS_ALL, D), 1.0, 6.0, ((0, 8), (1, 4)), jnp.float32)
    qkv_weight = gaussian(key_of[2], (D, 3, D), D ** -0.5, 0.21875, ((0, 16), (2, 2)), jnp.float32)
    proj_weight = gaussian(key_of[3], (D, D), 1.0, 4.0, ((0, 16), (1, 2)), jnp.float32)
    up_weight = gaussian(key_of[4], (D, FF), D ** -0.5, 0.21875, ((0, 16), (1, 2)), jnp.float32)
    down_weight = gaussian(key_of[5], (D, FF), FF ** -0.5, 0.109375, ((0, 16), (1, 2)), jnp.float32)
    norm_gains = jnp.clip(1.0 + 0.18 * jax.random.normal(key_of[6], (2, D), jnp.float32), 0.1, 1.9)
    shift_terms = gaussian(key_of[7], (4, D), 0.3, 1.5, ((1, 16),), jnp.float32)
    qv_bias = gaussian(key_of[8], (2, HEADS, HD), 0.3, 1.5, ((1, 2), (2, 16)), jnp.float32)
    up_bias = gaussian(key_of[9], (FF // 128, 128), 0.3, 1.5, ((0, 2), (1, 16)), jnp.float32)
    qkv_first = gaussian(key_of[10], (D, 3, D), (0.12 * (CLIPS_ALL * D) ** 0.5), 64.0, ((0, 16), (2, 2)), jnp.float32)
    qkv_second = jnp.clip(jnp.exp(math.log(55296.0) - 1.3862944 * jax.random.uniform(key_of[11], (D, 3, D), jnp.float32) ** level_of(key_of[11], (D, 3, D), ((0, 16), (2, 2)), -0.2, 0.2)), 13824.0, 55296.0)
    proj_first = gaussian(key_of[12], (D, D), (0.024 * (FRAMES * CLIPS_ALL) ** 0.5), 20.0, ((0, 16), (1, 2)), jnp.float32)
    proj_second = jnp.clip(jnp.exp(math.log(176.9472) - 1.3862944 * jax.random.uniform(key_of[13], (D, D), jnp.float32) ** level_of(key_of[13], (D, D), ((0, 16), (1, 2)), -0.2, 0.2)), 44.2368, 176.9472)
    up_first = gaussian(key_of[14], (D, FF), (0.05 * (FRAMES * CLIPS_ALL) ** 0.5), 40.0, ((0, 16), (1, 2)), jnp.float32)
    up_second = jnp.clip(jnp.exp(math.log(516.096) - 1.3862944 * jax.random.uniform(key_of[15], (D, FF), jnp.float32) ** level_of(key_of[15], (D, FF), ((0, 16), (1, 2)), -0.2, 0.2)), 129.024, 516.096)
    down_first = gaussian(key_of[16], (D, FF), (0.046 * (FRAMES * CLIPS_ALL) ** 0.5), 40.0, ((0, 16), (1, 2)), jnp.float32)
    down_second = jnp.clip(jnp.exp(math.log(884.736) - 1.3862944 * jax.random.uniform(key_of[17], (D, FF), jnp.float32) ** level_of(key_of[17], (D, FF), ((0, 16), (1, 2)), -0.2, 0.2)), 221.184, 884.736)
    gains_first = draw_gains_first(jax.random.fold_in(key_of[26], 71), 0)
    gains_second = draw_gains_second(jax.random.fold_in(key_of[26], 71), 0)
    shifts_first = draw_shifts_first(jax.random.fold_in(key_of[26], 71), 0)
    shifts_second = draw_shifts_second(jax.random.fold_in(key_of[26], 71), 0)
    qv_bias_first = gaussian(key_of[22], (2, HEADS, HD), (0.12 * (CLIPS_ALL * D) ** 0.5), 64.0, ((1, 2), (2, 16)), jnp.float32)
    qv_bias_second = jnp.clip(jnp.exp(math.log(5529600) - 1.3862944 * jax.random.uniform(key_of[23], (2, HEADS, HD), jnp.float32) ** level_of(key_of[23], (2, HEADS, HD), ((1, 2), (2, 16)), -0.2, 0.2)), 1382400, 5529600)
    up_bias_first = gaussian(key_of[24], (FF // 128, 128), (0.05 * (FRAMES * CLIPS_ALL) ** 0.5), 40.0, ((0, 2), (1, 16)), jnp.float32)
    up_bias_second = jnp.clip(jnp.exp(math.log(92.16) - 1.3862944 * jax.random.uniform(key_of[25], (FF // 128, 128), jnp.float32) ** level_of(key_of[25], (FF // 128, 128), ((0, 2), (1, 16)), -0.2, 0.2)), 23.04, 92.16)
    return dict(block_input=block_input, out_cotangent=out_cotangent, qkv_weight=qkv_weight, proj_weight=proj_weight, up_weight=up_weight, down_weight=down_weight, norm_gains=norm_gains, shift_terms=shift_terms, qv_bias=qv_bias, up_bias=up_bias, qkv_first=qkv_first, qkv_second=qkv_second, proj_first=proj_first, proj_second=proj_second, up_first=up_first, up_second=up_second, down_first=down_first, down_second=down_second, gains_first=gains_first, gains_second=gains_second, shifts_first=shifts_first, shifts_second=shifts_second, qv_bias_first=qv_bias_first, qv_bias_second=qv_bias_second, up_bias_first=up_bias_first, up_bias_second=up_bias_second)


eps_norm = 1e-05
beta_one = 0.9
beta_two = 0.98
eps_adam = 1e-06
rate_qkv = 0.6
rate_proj = 1.2
rate_up = 0.1
rate_down = 0.15
rate_gains = 4.0
rate_shifts = 8.0
rate_query_bias = 20.0
rate_up_bias = 0.4
decay_rate = 0.01
root_half = 0.7071067811865476
density_scale = 0.3989422804014327

def rounded(values_in):
    return lax.optimization_barrier(values_in.astype(jnp.bfloat16)).astype(jnp.float32)

def normalize(values_in, gain_row, shift_row):
    center = values_in - lax.optimization_barrier(jnp.mean(values_in, axis=-1, keepdims=True))
    inv_scale = lax.rsqrt(lax.optimization_barrier(jnp.mean(center * center, axis=-1, keepdims=True)) + eps_norm)
    normed = center * inv_scale
    return (normed, inv_scale, rounded(normed * gain_row + shift_row))

def normalize_back(grad_in, normed, inv_scale, gain_row):
    inner_term = grad_in * gain_row
    inner_term = inner_term - lax.optimization_barrier(jnp.mean(inner_term, axis=-1, keepdims=True)) - normed * lax.optimization_barrier(jnp.mean(inner_term * normed, axis=-1, keepdims=True))
    return inv_scale * inner_term

def gelu_value(hidden):
    return 0.5 * hidden * (1.0 + jax.scipy.special.erf(hidden * root_half))

def gelu_slope(hidden):
    return 0.5 * (1.0 + jax.scipy.special.erf(hidden * root_half)) + hidden * density_scale * jnp.exp(-0.5 * hidden * hidden)

def adam_step(current, moment_one, moment_two, gradient, rate_value, decay_value):
    one_next = beta_one * moment_one + (1.0 - beta_one) * gradient
    two_next = beta_two * moment_two + (1.0 - beta_two) * gradient * gradient
    step_ratio = one_next / (1.0 - beta_one ** STEP) / (jnp.sqrt(two_next / (1.0 - beta_two ** STEP)) + eps_adam)
    return (current - rate_value * (step_ratio + decay_value * current), one_next, two_next)

def add_pair(left_value, right_value):
    return left_value + right_value

def matmul(left_value, right_value):
    return jnp.dot(left_value, right_value, preferred_element_type=jnp.float32)

def layer_clip(weights, block_rows, cot_rows):
    weight_query, weight_key, weight_value, weight_proj, weight_up, weight_down, gain_one, gain_two, shift_one, shift_two, bias_proj, bias_down, bias_query, bias_value, expand_bias = weights
    frame_count = block_rows.shape[0]
    score_scale = HD ** (-0.5)
    normed_one, inv_one, act_one = normalize(block_rows, gain_one, shift_one)
    queries = rounded(matmul(act_one, weight_query) + bias_query)
    keys_rows = rounded(matmul(act_one, weight_key))
    value_rows = rounded(matmul(act_one, weight_value) + bias_value)
    query_heads = queries.reshape(frame_count, HEADS, HD)
    key_heads = keys_rows.reshape(frame_count, HEADS, HD)
    value_heads = value_rows.reshape(frame_count, HEADS, HD)
    scores = jnp.einsum('qhe,khe->hqk', query_heads, key_heads) * score_scale
    row_top = lax.optimization_barrier(jnp.max(scores, axis=-1, keepdims=True))
    exp_terms = jnp.exp(scores - row_top)
    row_total = lax.optimization_barrier(jnp.sum(exp_terms, axis=-1, keepdims=True))
    log_total = row_top + jnp.log(row_total)
    mix_sum = jnp.einsum('hqk,khe->qhe', exp_terms, value_heads) / jnp.transpose(row_total, (1, 0, 2))
    attended = rounded(mix_sum.reshape(frame_count, D))
    residual = block_rows + (matmul(attended, weight_proj.T) + bias_proj)
    normed_two, inv_two, second_activation = normalize(residual, gain_two, shift_two)
    hidden = matmul(second_activation, weight_up) + expand_bias
    active_mask = rounded(gelu_value(hidden))
    block_out = residual + (matmul(active_mask, weight_down.T) + bias_down)
    grad_half = rounded(cot_rows)
    down_weight_gradient = matmul(grad_half.T, active_mask)
    hidden_grad = matmul(grad_half, weight_down) * gelu_slope(hidden)
    hidden_local_part = rounded(hidden_grad)
    up_weight_gradient = matmul(second_activation.T, hidden_local_part)
    act_two_grad = matmul(hidden_local_part, weight_up.T)
    resid_grad = cot_rows + normalize_back(act_two_grad, normed_two, inv_two, gain_two)
    resid_half = rounded(resid_grad)
    proj_grad = matmul(resid_half.T, attended)
    mixed_grad = rounded(matmul(resid_half, weight_proj)).reshape(frame_count, HEADS, HD)
    delta_sum = jnp.transpose(lax.optimization_barrier(jnp.sum(mixed_grad * attended.reshape(frame_count, HEADS, HD), axis=-1)))[:, :, None]
    prob_rows = jnp.exp(scores - log_total)
    value_grad = jnp.einsum('hqk,qhe->khe', rounded(prob_rows), mixed_grad).reshape(frame_count, D)
    score_grad = rounded(prob_rows * (jnp.einsum('qhe,khe->hqk', mixed_grad, value_heads) - delta_sum))
    query_grad = (jnp.einsum('hqk,khe->qhe', score_grad, key_heads) * score_scale).reshape(frame_count, D)
    key_grad = (jnp.einsum('hqk,qhe->khe', score_grad, query_heads) * score_scale).reshape(frame_count, D)
    query_half = rounded(query_grad)
    key_half = rounded(key_grad)
    value_half = rounded(value_grad)
    qkv_grad = jnp.stack([matmul(act_one.T, query_half), matmul(act_one.T, key_half), matmul(act_one.T, value_half)], axis=1)
    act_one_grad = matmul(query_half, weight_query.T) + matmul(key_half, weight_key.T) + matmul(value_half, weight_value.T)
    input_grad = resid_grad + normalize_back(act_one_grad, normed_one, inv_one, gain_one)
    gains_grad = jnp.stack([lax.optimization_barrier(jnp.sum(act_one_grad * normed_one, axis=0)), lax.optimization_barrier(jnp.sum(act_two_grad * normed_two, axis=0))])
    shifts_grad = jnp.stack([lax.optimization_barrier(jnp.sum(act_one_grad, axis=0)), lax.optimization_barrier(jnp.sum(act_two_grad, axis=0)), lax.optimization_barrier(jnp.sum(resid_grad, axis=0)), lax.optimization_barrier(jnp.sum(cot_rows, axis=0))])
    qv_grad = jnp.stack([lax.optimization_barrier(jnp.sum(query_grad, axis=0)), lax.optimization_barrier(jnp.sum(value_grad, axis=0))])
    up_bias_grad = lax.optimization_barrier(jnp.sum(hidden_grad, axis=0))
    return (block_out, input_grad, (qkv_grad, proj_grad, up_weight_gradient, down_weight_gradient, gains_grad, shifts_grad, qv_grad, up_bias_grad))

def reference(block_input, out_cotangent, qkv_weight, proj_weight, up_weight, down_weight, norm_gains, shift_terms, qv_bias, up_bias, qkv_first, qkv_second, proj_first, proj_second, up_first, up_second, down_first, down_second, gains_first, gains_second, shifts_first, shifts_second, qv_bias_first, qv_bias_second, up_bias_first, up_bias_second):
    qkv_half = rounded(qkv_weight)
    gains_half = rounded(norm_gains)
    shifts_half = rounded(shift_terms)
    qv_half = rounded(qv_bias).reshape(2, D)
    weights = (qkv_half[:, 0], qkv_half[:, 1], qkv_half[:, 2], rounded(proj_weight), rounded(up_weight), rounded(down_weight), gains_half[0], gains_half[1], shifts_half[0], shifts_half[1], shifts_half[2], shifts_half[3], qv_half[0], qv_half[1], rounded(up_bias).reshape(FF))

    def step_clip(totals, clip_rows):
        block_out, input_grad, grads = layer_clip(weights, clip_rows[0], clip_rows[1])
        return (jax.tree.map(add_pair, totals, grads), (block_out, input_grad))
    float_type = block_input.dtype
    zero_grads = (jnp.zeros((D, 3, D), float_type), jnp.zeros((D, D), float_type), jnp.zeros((D, FF), float_type), jnp.zeros((D, FF), float_type), jnp.zeros((2, D), float_type), jnp.zeros((4, D), float_type), jnp.zeros((2, D), float_type), jnp.zeros((FF,), float_type))
    totals, (outputs, input_grads) = lax.scan(step_clip, zero_grads, (jnp.moveaxis(block_input, 1, 0), jnp.moveaxis(out_cotangent, 1, 0)))
    qkv_grad, proj_grad, up_weight_gradient, down_weight_gradient, gains_grad, shifts_grad, qv_flat, up_flat = totals
    qv_bias_grad = qv_flat.reshape(2, HEADS, HD)
    up_bias_grad = up_flat.reshape(FF // 128, 128)
    qkv_new, qkv_first_next, qkv_second_next = adam_step(qkv_weight, qkv_first, qkv_second, qkv_grad, rate_qkv, decay_rate)
    proj_new, proj_first_next, proj_second_next = adam_step(proj_weight, proj_first, proj_second, proj_grad, rate_proj, decay_rate)
    up_new, up_first_next, up_second_next = adam_step(up_weight, up_first, up_second, up_weight_gradient, rate_up, decay_rate)
    down_new, down_first_next, down_second_next = adam_step(down_weight, down_first, down_second, down_weight_gradient, rate_down, decay_rate)
    gains_new, gains_first_next, gains_second_next = adam_step(norm_gains, gains_first, gains_second, gains_grad, rate_gains, 0.0)
    shifts_new, shifts_first_next, shifts_second_next = adam_step(shift_terms, shifts_first, shifts_second, shifts_grad, rate_shifts, 0.0)
    qv_bias_new, qv_bias_first_next, qv_bias_second_next = adam_step(qv_bias, qv_bias_first, qv_bias_second, qv_bias_grad, rate_query_bias, 0.0)
    up_bias_new, up_bias_first_next, up_bias_second_next = adam_step(up_bias, up_bias_first, up_bias_second, up_bias_grad, rate_up_bias, 0.0)
    return (jnp.moveaxis(outputs, 0, 1), jnp.moveaxis(input_grads, 0, 1), qkv_grad, proj_grad, up_weight_gradient, down_weight_gradient, gains_grad, shifts_grad, qv_bias_grad, up_bias_grad, qkv_new, proj_new, up_new, down_new, gains_new, shifts_new, qv_bias_new, up_bias_new, qkv_first_next, qkv_second_next, proj_first_next, proj_second_next, up_first_next, up_second_next, down_first_next, down_second_next, gains_first_next, gains_second_next, shifts_first_next, shifts_second_next, qv_bias_first_next, qv_bias_second_next, up_bias_first_next, up_bias_second_next)
```

```python
import functools
import math

import jax
import jax.numpy as jnp
from jax import lax
from jax.experimental import pallas as pl
from jax.experimental.pallas import tpu as pltpu
from jax.sharding import PartitionSpec as P

HD = 64
STEP = 4
F32 = jnp.float32
BF = jnp.bfloat16

eps_norm = 1e-05
beta_one = 0.9
beta_two = 0.98
eps_adam = 1e-06
rate_qkv = 0.6
rate_proj = 1.2
rate_up = 0.1
rate_down = 0.15
rate_gains = 4.0
rate_shifts = 8.0
rate_query_bias = 20.0
rate_up_bias = 0.4
decay_rate = 0.01
root_half = 0.7071067811865476
density_scale = 0.3989422804014327
score_scale = HD ** (-0.5)
MIB = 2**20


def params(limit_mib):
    return pltpu.CompilerParams(vmem_limit_bytes=limit_mib * MIB)


def mm(a, b):
    return lax.dot_general(a, b, (((1,), (0,)), ((), ())), preferred_element_type=F32)


def mm_nt(a, b):
    return lax.dot_general(a, b, (((1,), (1,)), ((), ())), preferred_element_type=F32)


def row_mean(v):
    return jnp.mean(v, axis=-1, keepdims=True)


def normed_rows(v):
    center = v - row_mean(v)
    inv = lax.rsqrt(row_mean(center * center) + eps_norm)
    return center * inv, inv


def adam_step(current, moment_one, moment_two, gradient, rate_value, decay_value):
    one_next = beta_one * moment_one + (1.0 - beta_one) * gradient
    two_next = beta_two * moment_two + (1.0 - beta_two) * gradient * gradient
    step_ratio = (
        one_next / (1.0 - beta_one**STEP) / (jnp.sqrt(two_next / (1.0 - beta_two**STEP)) + eps_adam)
    )
    return (current - rate_value * (step_ratio + decay_value * current), one_next, two_next)


def qkv_kernel(own_ref, other_ref, w_ref, rows_ref, bias_ref, q_ref, kv_ref):
    gain, shift = rows_ref[0:1, :], rows_ref[1:2, :]
    bias_q, bias_v = bias_ref[0:1, :], bias_ref[1:2, :]
    half = own_ref.shape[0]
    width = q_ref.shape[1]
    for i, ref in enumerate((own_ref, other_ref)):
        normed, _ = normed_rows(ref[...].astype(F32))
        act = (normed * gain + shift).astype(BF)
        out = mm(act, w_ref[...])
        rows = pl.ds(i * half, half)
        q = (out[:, :width] + bias_q).astype(BF)
        q_ref[rows, :] = (q.astype(F32) * score_scale).astype(BF)
        kv_ref[rows, :width] = out[:, width : 2 * width].astype(BF)
        kv_ref[rows, width:] = (out[:, 2 * width :] + bias_v).astype(BF)


def qkv_call(own, other, weight, rows, bias):
    half, _ = own.shape
    width = weight.shape[1] // 3
    return pl.pallas_call(
        qkv_kernel,
        out_shape=(
            jax.ShapeDtypeStruct((2 * half, width), BF),
            jax.ShapeDtypeStruct((2 * half, 2 * width), BF),
        ),
        compiler_params=params(32),
        cost_estimate=pl.CostEstimate(
            flops=2 * 2 * half * weight.size, bytes_accessed=4 * MIB, transcendentals=0
        ),
        name="project_qkv",
    )(own, other, weight, rows, bias)


def head_mask(shape, h):
    lane = lax.broadcasted_iota(jnp.int32, shape, 1)
    return (lane >= HD) if h else (lane < HD)


def pick(v, h):
    return jnp.where(head_mask(v.shape, h), v, jnp.zeros_like(v))


def attend_kernel(q_ref, *refs):
    k_refs, v_refs = refs[0:4], refs[4:8]
    own_ref, send_ref, lse_ref, s_scr = refs[8:]
    half = own_ref.shape[0]
    q = q_ref[...]
    n = k_refs[0].shape[0]
    v_t = [r[...].T for r in v_refs]
    parts = []
    for h in range(2):
        qh = pick(q, h)
        tops = []
        for i in range(4):
            s = mm_nt(k_refs[i][...], qh)
            s_scr[h, pl.ds(i * n, n), :] = s
            tops.append(jnp.max(s, axis=0, keepdims=True))
        top = functools.reduce(jnp.maximum, tops)
        total = jnp.zeros_like(top)
        mix = jnp.zeros((HD, q.shape[0]), F32)
        for i in range(4):
            e = jnp.exp(s_scr[h, pl.ds(i * n, n), :] - top)
            total = total + jnp.sum(e, axis=0, keepdims=True)
            mix = mix + mm(v_t[i][h * HD : (h + 1) * HD, :], e.astype(BF))
        parts.append(mix / total)
        lse_ref[0, h : h + 1, :] = top + jnp.log(total)
    o = jnp.concatenate(parts, axis=0).T.astype(BF)
    own_ref[...] = o[:half]
    send_ref[...] = o[half:]


def attend_call(q, pieces):
    rows, width = q.shape
    pairs = width // 128
    n = pieces[0].shape[0]
    half = rows // 2
    k_spec = pl.BlockSpec((n, 128), lambda p: (0, p))
    v_spec = pl.BlockSpec((n, 128), lambda p: (0, p + pairs))
    return pl.pallas_call(
        attend_kernel,
        grid=(pairs,),
        in_specs=[pl.BlockSpec((rows, 128), lambda p: (0, p))] + [k_spec] * 4 + [v_spec] * 4,
        out_specs=[
            pl.BlockSpec((half, 128), lambda p: (0, p)),
            pl.BlockSpec((half, 128), lambda p: (0, p)),
            pl.BlockSpec((1, 2, rows), lambda p: (p, 0, 0)),
        ],
        out_shape=(
            jax.ShapeDtypeStruct((half, width), BF),
            jax.ShapeDtypeStruct((half, width), BF),
            jax.ShapeDtypeStruct((pairs, 2, rows), F32),
        ),
        scratch_shapes=[pltpu.VMEM((2, 4 * n, rows), F32)],
        compiler_params=params(40),
        cost_estimate=pl.CostEstimate(
            flops=16 * rows * 4 * n * width,
            bytes_accessed=4 * MIB,
            transcendentals=pairs * 2 * rows * 4 * n,
        ),
        name="attend",
    )(q, *pieces, *pieces)


def attend_back_kernel(*refs):
    q_ref, do_own_ref, do_got_ref, o_own_ref, o_send_ref, lse_ref = refs[:6]
    k_refs, v_refs = refs[6:10], refs[10:14]
    dq_ref = refs[14]
    dk_refs, dv_refs = refs[15:19], refs[19:23]
    q = q_ref[...]
    do = jnp.concatenate([do_own_ref[...], do_got_ref[...]], axis=0)
    o = jnp.concatenate([o_own_ref[...], o_send_ref[...]], axis=0)
    prod_t = (do.astype(F32) * o.astype(F32)).T
    q_heads = [pick(q, h) for h in range(2)]
    do_heads = [pick(do, h) for h in range(2)]
    deltas = [
        jnp.sum(prod_t[h * HD : (h + 1) * HD, :], axis=0, keepdims=True) for h in range(2)
    ]
    lses = [lse_ref[0, h : h + 1, :] for h in range(2)]
    dq_t = [jnp.zeros((HD, q.shape[0]), F32) for _ in range(2)]
    for i in range(4):
        k = k_refs[i][...]
        v = v_refs[i][...]
        k_t = k.T
        dk = jnp.zeros(k.shape, F32)
        dv = jnp.zeros(k.shape, F32)
        for h in range(2):
            p = jnp.exp(mm_nt(k, q_heads[h]) - lses[h])
            dv = dv + mm(p.astype(BF), do_heads[h])
            ds = (p * (mm_nt(v, do_heads[h]) - deltas[h])).astype(BF)
            dk = dk + mm(ds, q_heads[h])
            dq_t[h] = dq_t[h] + mm(k_t[h * HD : (h + 1) * HD, :], ds)
        dk_refs[i][...] = dk.astype(BF)
        dv_refs[i][...] = dv.astype(BF)
    dq_ref[...] = (jnp.concatenate(dq_t, axis=0).T * score_scale).astype(BF)


def attend_back_call(q, do_own, do_got, o_own, o_send, lse, pieces):
    rows, width = q.shape
    pairs = width // 128
    n = pieces[0].shape[0]
    half = rows // 2
    full = pl.BlockSpec((rows, 128), lambda p: (0, p))
    part = pl.BlockSpec((half, 128), lambda p: (0, p))
    k_spec = pl.BlockSpec((n, 128), lambda p: (0, p))
    v_spec = pl.BlockSpec((n, 128), lambda p: (0, p + pairs))
    out = pl.pallas_call(
        attend_back_kernel,
        grid=(pairs,),
        in_specs=[full, part, part, part, part, pl.BlockSpec((1, 2, rows), lambda p: (p, 0, 0))]
        + [k_spec] * 4
        + [v_spec] * 4,
        out_specs=[full] + [k_spec] * 8,
        out_shape=(jax.ShapeDtypeStruct((rows, width), BF),)
        + (jax.ShapeDtypeStruct((n, width), BF),) * 8,
        compiler_params=params(40),
        cost_estimate=pl.CostEstimate(
            flops=40 * rows * 4 * n * width,
            bytes_accessed=8 * MIB,
            transcendentals=pairs * 2 * rows * 4 * n,
        ),
        name="attend_back",
    )(q, do_own, do_got, o_own, o_send, lse, *pieces, *pieces)
    return out[0], out[1:5], out[5:9]


def ffn_kernel(clips, *refs):
    o_own, o_got = refs[0:clips], refs[clips : 2 * clips]
    x_ref, gy_ref, wo_ref, up_ref, dn_ref, b1_ref, rows_ref = refs[2 * clips : 2 * clips + 7]
    outs = refs[2 * clips + 7 :]
    y_ref, d1_ref = outs[0:2]
    do_own, do_send = outs[2 : 2 + clips], outs[2 + clips : 2 + 2 * clips]
    dup_ref, ddn_ref, dwo_ref, sums_ref, db1_ref = outs[2 + 2 * clips : 7 + 2 * clips]
    proj_scr, c_scr, ct_scr, gyt_scr, y_scr, dc_scr = outs[7 + 2 * clips :]
    half = o_own[0].shape[0]
    j = pl.program_id(0)
    gain, shift = rows_ref[0:1, :], rows_ref[1:2, :]
    bias_o, bias_2 = rows_ref[2:3, :], rows_ref[3:4, :]

    @pl.when(j == 0)
    def _():
        for i in range(clips):
            rows = pl.ds(i * half, half)
            proj = mm_nt(o_own[i][...], wo_ref[0]) + mm_nt(o_got[i][...], wo_ref[1]) + bias_o
            proj_scr[rows, :] = proj
            normed, _ = normed_rows(x_ref[rows, :].astype(F32) + proj)
            c_scr[rows, :] = (normed * gain + shift).astype(BF)
        ct_scr[...] = c_scr[...].T
        gyt_scr[...] = gy_ref[...].T
        y_scr[...] = jnp.zeros_like(y_scr)
        dc_scr[...] = jnp.zeros_like(dc_scr)

    up = up_ref[0]
    dn = dn_ref[0]
    f = mm(c_scr[...], up) + b1_ref[0]
    cdf = 0.5 * (1.0 + lax.erf(f * root_half))
    u = (f * cdf).astype(BF)
    slope = cdf + f * (density_scale * jnp.exp(-0.5 * f * f))
    df = mm(gy_ref[...], dn) * slope
    dfb = df.astype(BF)
    db1_ref[0] = jnp.sum(df, axis=0, keepdims=True)
    y_scr[...] += mm_nt(u, dn)
    dc_scr[...] += mm_nt(dfb, up)
    ddn_ref[0] = mm(gyt_scr[...], u).astype(BF)
    dup_ref[0] = mm(ct_scr[...], dfb).astype(BF)

    @pl.when(j == pl.num_programs(0) - 1)
    def _():
        sum_gain = jnp.zeros_like(gain)
        sum_dc = jnp.zeros_like(gain)
        sum_dh = jnp.zeros_like(gain)
        dwo0 = jnp.zeros(wo_ref.shape[1:], F32)
        dwo1 = jnp.zeros(wo_ref.shape[1:], F32)
        for i in range(clips):
            rows = pl.ds(i * half, half)
            proj = proj_scr[rows, :]
            normed, inv = normed_rows(x_ref[rows, :].astype(F32) + proj)
            y_ref[rows, :] = (proj + y_scr[rows, :] + bias_2).astype(BF)
            dc = dc_scr[rows, :]
            t = dc * gain
            d1 = inv * (t - row_mean(t) - normed * row_mean(t * normed))
            d1_ref[rows, :] = d1
            dh = gy_ref[rows, :].astype(F32) + d1
            dy = dh.astype(BF)
            sum_gain = sum_gain + jnp.sum(dc * normed, axis=0, keepdims=True)
            sum_dc = sum_dc + jnp.sum(dc, axis=0, keepdims=True)
            sum_dh = sum_dh + jnp.sum(dh, axis=0, keepdims=True)
            do_own[i][...] = mm(dy, wo_ref[0]).astype(BF)
            do_send[i][...] = mm(dy, wo_ref[1]).astype(BF)
            dy_t = dy.T
            dwo0 = dwo0 + mm(dy_t, o_own[i][...])
            dwo1 = dwo1 + mm(dy_t, o_got[i][...])
        dwo_ref[0] = dwo0.astype(BF)
        dwo_ref[1] = dwo1.astype(BF)
        sums_ref[0:1, :] = sum_gain
        sums_ref[1:2, :] = sum_dc
        sums_ref[2:3, :] = sum_dh
        sums_ref[3:8, :] = jnp.zeros((5, sums_ref.shape[1]), F32)


def ffn_call(o_own, o_got, x, gy, wide, b1, rows):
    clips = len(o_own)
    tokens, dim = x.shape
    half, width = o_own[0].shape
    hidden = b1.shape[1]
    block = 512
    per = hidden // block
    resident = lambda shape: pl.BlockSpec(
        shape, lambda j: (0,) * len(shape), pipeline_mode=pl.Buffered(1)
    )
    up_spec = pl.BlockSpec((1, dim, block), lambda j: (j // per, 0, j % per))
    out = pl.pallas_call(
        functools.partial(ffn_kernel, clips),
        grid=(2 * per,),
        in_specs=[resident((half, width))] * (2 * clips)
        + [
            resident((tokens, dim)),
            resident((tokens, dim)),
            pl.BlockSpec(
                (2, dim, width), lambda j: (0, 0, 2 * hidden // width), pipeline_mode=pl.Buffered(1)
            ),
            up_spec,
            pl.BlockSpec((1, dim, block), lambda j: (j // per, 0, j % per + per)),
            pl.BlockSpec((1, 1, block), lambda j: (j, 0, 0)),
            resident((8, dim)),
        ],
        out_specs=[resident((tokens, dim))] * 2
        + [resident((half, width))] * (2 * clips)
        + [
            up_spec,
            up_spec,
            resident((2, dim, width)),
            resident((8, dim)),
            pl.BlockSpec((1, 1, block), lambda j: (j, 0, 0)),
        ],
        out_shape=(
            jax.ShapeDtypeStruct((tokens, dim), BF),
            jax.ShapeDtypeStruct((tokens, dim), F32),
        )
        + (jax.ShapeDtypeStruct((half, width), BF),) * (2 * clips)
        + (
            jax.ShapeDtypeStruct((2, dim, hidden), BF),
            jax.ShapeDtypeStruct((2, dim, hidden), BF),
            jax.ShapeDtypeStruct((2, dim, width), BF),
            jax.ShapeDtypeStruct((8, dim), F32),
            jax.ShapeDtypeStruct((2 * per, 1, block), F32),
        ),
        scratch_shapes=[
            pltpu.VMEM((tokens, dim), F32),
            pltpu.VMEM((tokens, dim), BF),
            pltpu.VMEM((dim, tokens), BF),
            pltpu.VMEM((dim, tokens), BF),
            pltpu.VMEM((tokens, dim), F32),
            pltpu.VMEM((tokens, dim), F32),
        ],
        compiler_params=params(56),
        cost_estimate=pl.CostEstimate(
            flops=24 * tokens * dim * hidden, bytes_accessed=30 * MIB, transcendentals=0
        ),
        name="feed_forward",
    )(*o_own, *o_got, x, gy, wide, wide, wide, b1.reshape(2 * per, 1, block), rows)
    y, d1 = out[:2]
    do_own, do_send = out[2 : 2 + clips], out[2 + clips : 2 + 2 * clips]
    dup, ddn, dwo, sums, db1 = out[2 + 2 * clips :]
    return y, d1, do_own, do_send, dup, ddn, dwo, sums, db1.reshape(2, hidden)


def back_kernel(clips, *refs):
    own_refs, got_refs = refs[0:clips], refs[clips : 2 * clips]
    dq_refs = refs[2 * clips : 3 * clips]
    dk_refs = refs[3 * clips : 4 * clips]
    dv_refs = refs[4 * clips : 5 * clips]
    w_ref, rows_ref = refs[5 * clips : 5 * clips + 2]
    outs = refs[5 * clips + 2 :]
    da_own, da_send = outs[0:clips], outs[clips : 2 * clips]
    dw_ref, sums_ref, bias_ref = outs[2 * clips : 2 * clips + 3]
    acc_scr = outs[2 * clips + 3]
    half = own_refs[0].shape[0]
    width = dq_refs[0].shape[1]
    gain, shift = rows_ref[0:1, :], rows_ref[1:2, :]
    sum_gain = jnp.zeros_like(gain)
    sum_da = jnp.zeros_like(gain)
    sum_q = jnp.zeros((1, width), F32)
    sum_v = jnp.zeros((1, width), F32)
    for i in range(clips):
        for s, (x_ref, da_ref) in enumerate(((own_refs[i], da_own[i]), (got_refs[i], da_send[i]))):
            rows = pl.ds(s * half, half)
            normed, _ = normed_rows(x_ref[...].astype(F32))
            act = normed * gain + shift
            act_t = act.astype(BF).T
            da = jnp.zeros(act.shape, F32)
            for j, ref in enumerate((dq_refs[i], dk_refs[i], dv_refs[i])):
                g = ref[rows, :]
                cols = slice(j * width, (j + 1) * width)
                da = da + mm_nt(g, w_ref[:, cols])
                part = mm(act_t, g)
                if i == 0 and s == 0:
                    acc_scr[:, cols] = part
                else:
                    acc_scr[:, cols] += part
                if j == 0:
                    sum_q = sum_q + jnp.sum(g.astype(F32), axis=0, keepdims=True)
                if j == 2:
                    sum_v = sum_v + jnp.sum(g.astype(F32), axis=0, keepdims=True)
            da_ref[...] = da.astype(BF)
            sum_gain = sum_gain + jnp.sum(da * normed, axis=0, keepdims=True)
            sum_da = sum_da + jnp.sum(da, axis=0, keepdims=True)
    dw_ref[...] = acc_scr[...].astype(BF)
    sums_ref[0:1, :] = sum_gain
    sums_ref[1:2, :] = sum_da
    sums_ref[2:8, :] = jnp.zeros((6, sums_ref.shape[1]), F32)
    bias_ref[0:1, :] = sum_q
    bias_ref[1:2, :] = sum_v
    bias_ref[2:8, :] = jnp.zeros((6, width), F32)


def back_call(x_own, x_got, dq, dk, dv, weight, rows):
    clips = len(x_own)
    half, dim = x_own[0].shape
    width = dq[0].shape[1]
    out = pl.pallas_call(
        functools.partial(back_kernel, clips),
        out_shape=(jax.ShapeDtypeStruct((half, dim), BF),) * (2 * clips)
        + (
            jax.ShapeDtypeStruct(weight.shape, BF),
            jax.ShapeDtypeStruct((8, dim), F32),
            jax.ShapeDtypeStruct((8, width), F32),
        ),
        scratch_shapes=[pltpu.VMEM(weight.shape, F32)],
        compiler_params=params(48),
        cost_estimate=pl.CostEstimate(
            flops=8 * clips * half * weight.size, bytes_accessed=16 * MIB, transcendentals=0
        ),
        name="project_back",
    )(*x_own, *x_got, *dq, *dk, *dv, weight, rows)
    return out[:clips], out[clips : 2 * clips], out[2 * clips], out[2 * clips + 1], out[2 * clips + 2]


class Links:
    def __init__(self, mesh):
        self.dp = mesh.shape["dp"]
        self.ctx = mesh.shape["ctx"]
        self.tensor = mesh.shape["tensor"]
        self.dp_bits = self.dp.bit_length() - 1
        self.ctx_bits = self.ctx.bit_length() - 1

    def flat(self, d, c, t):
        return (d * self.ctx + c) * self.tensor + t

    def move(self, value, partner):
        pairs = []
        for d in range(self.dp):
            for c in range(self.ctx):
                for t in range(self.tensor):
                    other = partner(d, c, t)
                    if other != (d, c, t):
                        pairs.append((self.flat(d, c, t), self.flat(*other)))
        return lax.ppermute(value, ("dp", "ctx", "tensor"), pairs)

    def across_x(self, value):
        return self.move(value, lambda d, c, t: (d, c, t ^ 1))

    def across_core(self, value):
        return self.move(value, lambda d, c, t: (d ^ 1, c, t))

    def across_z(self, value):
        return self.move(value, lambda d, c, t: (d, c ^ 1, t))

    def stays(self):
        d, c = lax.axis_index("dp"), lax.axis_index("ctx")
        return (d % 2) == (c // (self.ctx // 2))

    def swap(self, value):
        half = self.ctx // 2
        moved = self.move(
            value,
            lambda d, c, t: (d, c, t) if d % 2 == c // half else (d ^ 1, c ^ half, t),
        )
        return jnp.where(self.stays(), value, moved)

    def stages(self):
        out = []
        for bit in reversed(range(self.ctx_bits)):
            out.append(("ctx", bit, self.ctx_bits - 1 - bit))
        for bit in reversed(range(self.dp_bits)):
            out.append(("dp", bit, self.dp_bits - 1 - bit))
        return out

    def step(self, value, axis, bit):
        if axis == "ctx":
            return self.move(value, lambda d, c, t: (d, c ^ (1 << bit), t))
        return self.move(value, lambda d, c, t: (d ^ (1 << bit), c, t))

    def side(self, axis, bit):
        return (lax.axis_index(axis) // (1 << bit)) % 2

    def gather(self, value, both):
        shape = value.shape
        lead = 0
        for axis, bit, place in self.stages():
            if axis == "dp" and both and not lead:
                value = jnp.stack([value, self.across_x(value)])
                lead = 1
            got = self.step(value, axis, bit)
            low = self.side(axis, bit) == 0
            value = jnp.stack(
                [jnp.where(low, value, got), jnp.where(low, got, value)], axis=lead + place
            )
        shards = self.dp * self.ctx
        return value.reshape((2,) * lead + (shards * shape[0],) + shape[1:])

    def scatter(self, value, both):
        lead = 1 if both else 0
        rest = value.shape[lead + 1 :]
        value = value.reshape(
            value.shape[:lead] + (2,) * (self.dp_bits + self.ctx_bits) + rest
        )
        for axis, bit, place in reversed(self.stages()):
            if axis == "ctx" and lead:
                value = value[0] + self.across_x(value[1])
                lead = 0
            side = self.side(axis, bit)
            keep = lax.dynamic_index_in_dim(value, side, lead + place, keepdims=False)
            give = lax.dynamic_index_in_dim(value, 1 - side, lead + place, keepdims=False)
            value = keep + self.step(give, axis, bit)
        return value


def body(links, *args):
    (
        block_input,
        out_cotangent,
        qkv_weight,
        proj_weight,
        up_weight,
        down_weight,
        norm_gains,
        shift_terms,
        qv_bias,
        up_bias,
        qkv_first,
        qkv_second,
        proj_first,
        proj_second,
        up_first,
        up_second,
        down_first,
        down_second,
        gains_first,
        gains_second,
        shifts_first,
        shifts_second,
        qv_bias_first,
        qv_bias_second,
        up_bias_first,
        up_bias_second,
    ) = args
    half, clips, dim = block_input.shape
    shard = qkv_weight.shape[0]
    shards = dim // shard
    width = qkv_weight.shape[2]
    hidden = up_weight.shape[1]
    heads = width // HD

    x_home = jnp.transpose(block_input, (1, 0, 2)).astype(BF)
    gy_home = jnp.transpose(out_cotangent, (1, 0, 2)).astype(BF)
    x = links.swap(x_home)
    x_own = [x[i] for i in range(clips)]
    x_got = [links.across_x(v) for v in x_own]

    def lanes(parts):
        flat = jnp.concatenate([p.astype(BF).reshape(-1) for p in parts])
        return jnp.pad(flat, (0, shard * 128 - flat.size)).reshape(shard, 128)

    first = jnp.concatenate(
        [qkv_weight.reshape(shard, 3 * width).astype(BF), lanes([norm_gains, shift_terms, qv_bias])],
        axis=1,
    )
    second = jnp.concatenate(
        [up_weight.astype(BF), down_weight.astype(BF), proj_weight.astype(BF), lanes([up_bias])],
        axis=1,
    )
    first = links.gather(first, False)
    second = links.gather(second, True)
    w_qkv = first[:, : 3 * width]
    small = first[:, 3 * width :].reshape(shards, shard * 128)
    n_g, n_s = 2 * shard, 4 * shard
    gains = jnp.transpose(small[:, :n_g].reshape(shards, 2, shard), (1, 0, 2)).reshape(2, dim)
    shifts = jnp.transpose(
        small[:, n_g : n_g + n_s].reshape(shards, 4, shard), (1, 0, 2)
    ).reshape(4, dim)
    qv_cols = qv_bias.shape[2]
    biases = jnp.transpose(
        small[:, n_g + n_s : n_g + n_s + qv_bias.size].reshape(shards, 2, heads, qv_cols),
        (1, 2, 0, 3),
    ).reshape(2, width)
    ub_rows, ub_cols = up_bias.shape
    b1 = jnp.transpose(
        second[:, :, 2 * hidden + width :]
        .reshape(2, shards, shard * 128)[:, :, : up_bias.size]
        .reshape(2, shards, ub_rows, ub_cols),
        (0, 2, 1, 3),
    ).reshape(2, hidden)
    gains, shifts, biases, b1 = (v.astype(F32) for v in (gains, shifts, biases, b1))
    zero4 = jnp.zeros((4, dim), F32)
    rows_one = jnp.concatenate([gains[0:1], shifts[0:1], zero4, zero4[:2]])
    rows_two = jnp.concatenate([gains[1:2], shifts[1:4], zero4])
    biases = jnp.concatenate([biases, jnp.zeros((6, width), F32)])

    q, pieces, o_own, o_send, o_got, lse = [], [], [], [], [], []
    for i in range(clips):
        q_i, kv = qkv_call(x_own[i], x_got[i], w_qkv, rows_one, biases)
        kv_z = links.across_z(kv)
        kv_c = links.across_core(kv)
        kv_d = links.across_core(kv_z)
        q.append(q_i)
        pieces.append((kv, kv_c, kv_z, kv_d))
    gy = links.swap(gy_home)
    for i in range(clips):
        own, send, lse_i = attend_call(q[i], pieces[i])
        o_own.append(own)
        o_send.append(send)
        o_got.append(links.across_x(send))
        lse.append(lse_i)

    tokens = clips * half
    y, d1, do_own, do_send, d_up, d_down, d_proj, sums_two, d_b1 = ffn_call(
        o_own, o_got, x.reshape(tokens, dim), gy.reshape(tokens, dim), second, b1, rows_two
    )
    y_home = links.swap(y.reshape(clips, half, dim))
    block_output = block_input + jnp.transpose(y_home, (1, 0, 2)).astype(F32)

    grads_two = jnp.concatenate([d_up, d_down, d_proj], axis=2)
    grads_two = links.scatter(grads_two.reshape(2, shards, shard, -1), True)

    dq, dk, dv = [], [], []
    do_got = [links.across_x(v) for v in do_send]
    for i in range(clips):
        dq_i, dks, dvs = attend_back_call(
            q[i], do_own[i], do_got[i], o_own[i], o_send[i], lse[i], pieces[i]
        )
        dq.append(dq_i)
        for parts, out in ((dks, dk), (dvs, dv)):
            mine, core, z, diag = parts
            mine = mine + links.across_core(core)
            z = z + links.across_core(diag)
            out.append(mine + links.across_z(z))
    da_own, da_send, d_qkv, sums_one, sums_bias = back_call(
        x_own, x_got, dq, dk, dv, w_qkv, rows_one
    )
    grads_one = links.scatter(d_qkv.reshape(shards, shard, 3 * width), False)
    d1 = d1.reshape(clips, half, dim)
    deltas = []
    for i in range(clips):
        da = da_own[i].astype(F32) + links.across_x(da_send[i]).astype(F32)
        normed, inv = normed_rows(x_own[i].astype(F32))
        w = da * gains[0]
        deltas.append(
            (d1[i] + inv * (w - row_mean(w) - normed * row_mean(w * normed))).astype(BF)
        )
    delta_home = links.swap(jnp.stack(deltas))
    input_grad = out_cotangent + jnp.transpose(delta_home, (1, 0, 2)).astype(F32)

    cot_sum = jnp.sum(out_cotangent, axis=(0, 1))[None]
    both = jnp.concatenate(
        [sums_one[0:1], sums_two[0:1], sums_one[1:2], sums_two[1:2], sums_two[2:3], cot_sum]
    )
    both = jnp.transpose(both.reshape(6, shards, shard), (1, 0, 2)).reshape(shards, 6 * shard)
    ub = jnp.transpose(d_b1.reshape(2, ub_rows, shards, ub_cols), (0, 2, 1, 3)).reshape(
        2, shards, up_bias.size
    )
    crossed = links.across_x(jnp.concatenate([both, ub[1]], axis=1))
    qv = jnp.transpose(
        sums_bias[0:2].reshape(2, heads, shards, qv_cols), (2, 0, 1, 3)
    ).reshape(shards, qv_bias.size)
    vec = jnp.concatenate([jnp.concatenate([both, ub[0]], axis=1) + crossed, qv], axis=1)
    vec = links.scatter(vec, False)
    gains_grad = vec[:n_g].reshape(2, shard)
    shifts_grad = vec[n_g : n_g + n_s].reshape(4, shard)
    up_bias_grad = vec[6 * shard : 6 * shard + up_bias.size].reshape(up_bias.shape)
    qv_bias_grad = vec[6 * shard + up_bias.size :].reshape(qv_bias.shape)

    qkv_grad = grads_one.astype(F32).reshape(qkv_weight.shape)
    grads_two = grads_two.astype(F32)
    up_grad = grads_two[:, :hidden]
    down_grad = grads_two[:, hidden : 2 * hidden]
    proj_grad = grads_two[:, 2 * hidden :]

    qkv_next = adam_step(qkv_weight, qkv_first, qkv_second, qkv_grad, rate_qkv, decay_rate)
    proj_next = adam_step(proj_weight, proj_first, proj_second, proj_grad, rate_proj, decay_rate)
    up_next = adam_step(up_weight, up_first, up_second, up_grad, rate_up, decay_rate)
    down_next = adam_step(down_weight, down_first, down_second, down_grad, rate_down, decay_rate)
    gains_next = adam_step(norm_gains, gains_first, gains_second, gains_grad, rate_gains, 0.0)
    shifts_next = adam_step(shift_terms, shifts_first, shifts_second, shifts_grad, rate_shifts, 0.0)
    qv_next = adam_step(qv_bias, qv_bias_first, qv_bias_second, qv_bias_grad, rate_query_bias, 0.0)
    ub_next = adam_step(up_bias, up_bias_first, up_bias_second, up_bias_grad, rate_up_bias, 0.0)
    nexts = (qkv_next, proj_next, up_next, down_next, gains_next, shifts_next, qv_next, ub_next)
    return (
        block_output,
        input_grad,
        qkv_grad,
        proj_grad,
        up_grad,
        down_grad,
        gains_grad,
        shifts_grad,
        qv_bias_grad,
        up_bias_grad,
        *(n[0] for n in nexts),
        *(m for n in nexts for m in n[1:]),
    )


def solution(mesh):
    rows = P(("ctx", "tensor"), "dp", None)
    qkv = P(("dp", "ctx"), None, "tensor")
    mat = P(("dp", "ctx"), "tensor")
    norm = P(None, ("dp", "ctx"))
    qv = P(None, "tensor", ("dp", "ctx"))
    ub = P("tensor", ("dp", "ctx"))
    each = (qkv, mat, mat, mat, norm, norm, qv, ub)
    moments = tuple(s for s in each for _ in range(2))
    return jax.shard_map(
        functools.partial(body, Links(mesh)),
        mesh=mesh,
        in_specs=(rows, rows) + each + moments,
        out_specs=(rows, rows) + each + each + moments,
        check_vma=False,
    )
```

```python
import functools
import math

import jax
import jax.numpy as jnp
from jax import lax
from jax.experimental import pallas as pl
from jax.experimental.pallas import tpu as pltpu
from jax.sharding import PartitionSpec as P

HD = 64
STEP = 4
F32 = jnp.float32
BF = jnp.bfloat16

eps_norm = 1e-05
beta_one = 0.9
beta_two = 0.98
eps_adam = 1e-06
rate_qkv = 0.6
rate_proj = 1.2
rate_up = 0.1
rate_down = 0.15
rate_gains = 4.0
rate_shifts = 8.0
rate_query_bias = 20.0
rate_up_bias = 0.4
decay_rate = 0.01
root_half = 0.7071067811865476
density_scale = 0.3989422804014327
score_scale = HD ** (-0.5)
MIB = 2**20


def params(limit_mib):
    return pltpu.CompilerParams(vmem_limit_bytes=limit_mib * MIB)


def mm(a, b):
    return lax.dot_general(a, b, (((1,), (0,)), ((), ())), preferred_element_type=F32)


def mm_nt(a, b):
    return lax.dot_general(a, b, (((1,), (1,)), ((), ())), preferred_element_type=F32)


def row_mean(v):
    return jnp.mean(v, axis=-1, keepdims=True)


def normed_rows(v):
    center = v - row_mean(v)
    inv = lax.rsqrt(row_mean(center * center) + eps_norm)
    return center * inv, inv


def adam_step(current, moment_one, moment_two, gradient, rate_value, decay_value):
    one_next = beta_one * moment_one + (1.0 - beta_one) * gradient
    two_next = beta_two * moment_two + (1.0 - beta_two) * gradient * gradient
    step_ratio = (
        one_next / (1.0 - beta_one**STEP) / (jnp.sqrt(two_next / (1.0 - beta_two**STEP)) + eps_adam)
    )
    return (current - rate_value * (step_ratio + decay_value * current), one_next, two_next)


def qkv_kernel(own_ref, other_ref, w_ref, rows_ref, bias_ref, q_ref, kv_ref):
    gain, shift = rows_ref[0:1, :], rows_ref[1:2, :]
    bias_q, bias_v = bias_ref[0:1, :], bias_ref[1:2, :]
    half = own_ref.shape[0]
    width = q_ref.shape[1]
    for i, ref in enumerate((own_ref, other_ref)):
        normed, _ = normed_rows(ref[...].astype(F32))
        act = (normed * gain + shift).astype(BF)
        out = mm(act, w_ref[...])
        rows = pl.ds(i * half, half)
        q = (out[:, :width] + bias_q).astype(BF)
        q_ref[rows, :] = (q.astype(F32) * score_scale).astype(BF)
        kv_ref[rows, :width] = out[:, width : 2 * width].astype(BF)
        kv_ref[rows, width:] = (out[:, 2 * width :] + bias_v).astype(BF)


def qkv_call(own, other, weight, rows, bias):
    half, _ = own.shape
    width = weight.shape[1] // 3
    return pl.pallas_call(
        qkv_kernel,
        out_shape=(
            jax.ShapeDtypeStruct((2 * half, width), BF),
            jax.ShapeDtypeStruct((2 * half, 2 * width), BF),
        ),
        compiler_params=params(32),
        cost_estimate=pl.CostEstimate(
            flops=2 * 2 * half * weight.size, bytes_accessed=4 * MIB, transcendentals=0
        ),
        name="project_qkv",
    )(own, other, weight, rows, bias)


def head_mask(shape, h):
    lane = lax.broadcasted_iota(jnp.int32, shape, 1)
    return (lane >= HD) if h else (lane < HD)


def pick(v, h):
    return jnp.where(head_mask(v.shape, h), v, jnp.zeros_like(v))


def attend_kernel(q_ref, *refs):
    k_refs, v_refs = refs[0:4], refs[4:8]
    own_ref, send_ref, lse_ref, s_scr = refs[8:]
    half = own_ref.shape[0]
    q = q_ref[...]
    n = k_refs[0].shape[0]
    v_t = [r[...].T for r in v_refs]
    parts = []
    for h in range(2):
        qh = pick(q, h)
        tops = []
        for i in range(4):
            s = mm_nt(k_refs[i][...], qh)
            s_scr[h, pl.ds(i * n, n), :] = s
            tops.append(jnp.max(s, axis=0, keepdims=True))
        top = functools.reduce(jnp.maximum, tops)
        total = jnp.zeros_like(top)
        mix = jnp.zeros((HD, q.shape[0]), F32)
        for i in range(4):
            e = jnp.exp(s_scr[h, pl.ds(i * n, n), :] - top)
            total = total + jnp.sum(e, axis=0, keepdims=True)
            mix = mix + mm(v_t[i][h * HD : (h + 1) * HD, :], e.astype(BF))
        parts.append(mix / total)
        lse_ref[0, h : h + 1, :] = top + jnp.log(total)
    o = jnp.concatenate(parts, axis=0).T.astype(BF)
    own_ref[...] = o[:half]
    send_ref[...] = o[half:]


def attend_call(q, pieces):
    rows, width = q.shape
    pairs = width // 128
    n = pieces[0].shape[0]
    half = rows // 2
    k_spec = pl.BlockSpec((n, 128), lambda p: (0, p))
    v_spec = pl.BlockSpec((n, 128), lambda p: (0, p + pairs))
    return pl.pallas_call(
        attend_kernel,
        grid=(pairs,),
        in_specs=[pl.BlockSpec((rows, 128), lambda p: (0, p))] + [k_spec] * 4 + [v_spec] * 4,
        out_specs=[
            pl.BlockSpec((half, 128), lambda p: (0, p)),
            pl.BlockSpec((half, 128), lambda p: (0, p)),
            pl.BlockSpec((1, 2, rows), lambda p: (p, 0, 0)),
        ],
        out_shape=(
            jax.ShapeDtypeStruct((half, width), BF),
            jax.ShapeDtypeStruct((half, width), BF),
            jax.ShapeDtypeStruct((pairs, 2, rows), F32),
        ),
        scratch_shapes=[pltpu.VMEM((2, 4 * n, rows), F32)],
        compiler_params=params(40),
        cost_estimate=pl.CostEstimate(
            flops=16 * rows * 4 * n * width,
            bytes_accessed=4 * MIB,
            transcendentals=pairs * 2 * rows * 4 * n,
        ),
        name="attend",
    )(q, *pieces, *pieces)


def attend_back_kernel(*refs):
    q_ref, do_own_ref, do_got_ref, o_own_ref, o_send_ref, lse_ref = refs[:6]
    k_refs, v_refs = refs[6:10], refs[10:14]
    dq_ref = refs[14]
    dk_refs, dv_refs = refs[15:19], refs[19:23]
    q = q_ref[...]
    do = jnp.concatenate([do_own_ref[...], do_got_ref[...]], axis=0)
    o = jnp.concatenate([o_own_ref[...], o_send_ref[...]], axis=0)
    prod_t = (do.astype(F32) * o.astype(F32)).T
    q_heads = [pick(q, h) for h in range(2)]
    do_heads = [pick(do, h) for h in range(2)]
    deltas = [
        jnp.sum(prod_t[h * HD : (h + 1) * HD, :], axis=0, keepdims=True) for h in range(2)
    ]
    lses = [lse_ref[0, h : h + 1, :] for h in range(2)]
    dq_t = [jnp.zeros((HD, q.shape[0]), F32) for _ in range(2)]
    for i in range(4):
        k = k_refs[i][...]
        v = v_refs[i][...]
        k_t = k.T
        dk = jnp.zeros(k.shape, F32)
        dv = jnp.zeros(k.shape, F32)
        for h in range(2):
            p = jnp.exp(mm_nt(k, q_heads[h]) - lses[h])
            dv = dv + mm(p.astype(BF), do_heads[h])
            ds = (p * (mm_nt(v, do_heads[h]) - deltas[h])).astype(BF)
            dk = dk + mm(ds, q_heads[h])
            dq_t[h] = dq_t[h] + mm(k_t[h * HD : (h + 1) * HD, :], ds)
        dk_refs[i][...] = dk.astype(BF)
        dv_refs[i][...] = dv.astype(BF)
    dq_ref[...] = (jnp.concatenate(dq_t, axis=0).T * score_scale).astype(BF)


def attend_back_call(q, do_own, do_got, o_own, o_send, lse, pieces):
    rows, width = q.shape
    pairs = width // 128
    n = pieces[0].shape[0]
    half = rows // 2
    full = pl.BlockSpec((rows, 128), lambda p: (0, p))
    part = pl.BlockSpec((half, 128), lambda p: (0, p))
    k_spec = pl.BlockSpec((n, 128), lambda p: (0, p))
    v_spec = pl.BlockSpec((n, 128), lambda p: (0, p + pairs))
    out = pl.pallas_call(
        attend_back_kernel,
        grid=(pairs,),
        in_specs=[full, part, part, part, part, pl.BlockSpec((1, 2, rows), lambda p: (p, 0, 0))]
        + [k_spec] * 4
        + [v_spec] * 4,
        out_specs=[full] + [k_spec] * 8,
        out_shape=(jax.ShapeDtypeStruct((rows, width), BF),)
        + (jax.ShapeDtypeStruct((n, width), BF),) * 8,
        compiler_params=params(40),
        cost_estimate=pl.CostEstimate(
            flops=40 * rows * 4 * n * width,
            bytes_accessed=8 * MIB,
            transcendentals=pairs * 2 * rows * 4 * n,
        ),
        name="attend_back",
    )(q, do_own, do_got, o_own, o_send, lse, *pieces, *pieces)
    return out[0], out[1:5], out[5:9]


def ffn_kernel(clips, *refs):
    o_own, o_got = refs[0:clips], refs[clips : 2 * clips]
    x_ref, gy_ref, wo_ref, up_ref, dn_ref, b1_ref, rows_ref = refs[2 * clips : 2 * clips + 7]
    outs = refs[2 * clips + 7 :]
    y_ref, d1_ref = outs[0:2]
    do_own, do_send = outs[2 : 2 + clips], outs[2 + clips : 2 + 2 * clips]
    dup_ref, ddn_ref, dwo_ref, sums_ref, db1_ref = outs[2 + 2 * clips : 7 + 2 * clips]
    proj_scr, c_scr, ct_scr, gyt_scr, y_scr, dc_scr = outs[7 + 2 * clips :]
    half = o_own[0].shape[0]
    j = pl.program_id(0)
    gain, shift = rows_ref[0:1, :], rows_ref[1:2, :]
    bias_o, bias_2 = rows_ref[2:3, :], rows_ref[3:4, :]

    @pl.when(j == 0)
    def _():
        for i in range(clips):
            rows = pl.ds(i * half, half)
            proj = mm_nt(o_own[i][...], wo_ref[0]) + mm_nt(o_got[i][...], wo_ref[1]) + bias_o
            proj_scr[rows, :] = proj
            normed, _ = normed_rows(x_ref[rows, :].astype(F32) + proj)
            c_scr[rows, :] = (normed * gain + shift).astype(BF)
        ct_scr[...] = c_scr[...].T
        gyt_scr[...] = gy_ref[...].T
        y_scr[...] = jnp.zeros_like(y_scr)
        dc_scr[...] = jnp.zeros_like(dc_scr)

    up = up_ref[0]
    dn = dn_ref[0]
    f = mm(c_scr[...], up) + b1_ref[0]
    cdf = 0.5 * (1.0 + lax.erf(f * root_half))
    u = (f * cdf).astype(BF)
    slope = cdf + f * (density_scale * jnp.exp(-0.5 * f * f))
    df = mm(gy_ref[...], dn) * slope
    dfb = df.astype(BF)
    db1_ref[0] = jnp.sum(df, axis=0, keepdims=True)
    y_scr[...] += mm_nt(u, dn)
    dc_scr[...] += mm_nt(dfb, up)
    ddn_ref[0] = mm(gyt_scr[...], u).astype(BF)
    dup_ref[0] = mm(ct_scr[...], dfb).astype(BF)

    @pl.when(j == pl.num_programs(0) - 1)
    def _():
        sum_gain = jnp.zeros_like(gain)
        sum_dc = jnp.zeros_like(gain)
        sum_dh = jnp.zeros_like(gain)
        dwo0 = jnp.zeros(wo_ref.shape[1:], F32)
        dwo1 = jnp.zeros(wo_ref.shape[1:], F32)
        for i in range(clips):
            rows = pl.ds(i * half, half)
            proj = proj_scr[rows, :]
            normed, inv = normed_rows(x_ref[rows, :].astype(F32) + proj)
            y_ref[rows, :] = (proj + y_scr[rows, :] + bias_2).astype(BF)
            dc = dc_scr[rows, :]
            t = dc * gain
            d1 = inv * (t - row_mean(t) - normed * row_mean(t * normed))
            d1_ref[rows, :] = d1
            dh = gy_ref[rows, :].astype(F32) + d1
            dy = dh.astype(BF)
            sum_gain = sum_gain + jnp.sum(dc * normed, axis=0, keepdims=True)
            sum_dc = sum_dc + jnp.sum(dc, axis=0, keepdims=True)
            sum_dh = sum_dh + jnp.sum(dh, axis=0, keepdims=True)
            do_own[i][...] = mm(dy, wo_ref[0]).astype(BF)
            do_send[i][...] = mm(dy, wo_ref[1]).astype(BF)
            dy_t = dy.T
            dwo0 = dwo0 + mm(dy_t, o_own[i][...])
            dwo1 = dwo1 + mm(dy_t, o_got[i][...])
        dwo_ref[0] = dwo0.astype(BF)
        dwo_ref[1] = dwo1.astype(BF)
        sums_ref[0:1, :] = sum_gain
        sums_ref[1:2, :] = sum_dc
        sums_ref[2:3, :] = sum_dh
        sums_ref[3:8, :] = jnp.zeros((5, sums_ref.shape[1]), F32)


def ffn_call(o_own, o_got, x, gy, wide, b1, rows):
    clips = len(o_own)
    tokens, dim = x.shape
    half, width = o_own[0].shape
    hidden = b1.shape[1]
    block = 512
    per = hidden // block
    resident = lambda shape: pl.BlockSpec(
        shape, lambda j: (0,) * len(shape), pipeline_mode=pl.Buffered(1)
    )
    up_spec = pl.BlockSpec((1, dim, block), lambda j: (j // per, 0, j % per))
    out = pl.pallas_call(
        functools.partial(ffn_kernel, clips),
        grid=(2 * per,),
        in_specs=[resident((half, width))] * (2 * clips)
        + [
            resident((tokens, dim)),
            resident((tokens, dim)),
            pl.BlockSpec(
                (2, dim, width), lambda j: (0, 0, 2 * hidden // width), pipeline_mode=pl.Buffered(1)
            ),
            up_spec,
            pl.BlockSpec((1, dim, block), lambda j: (j // per, 0, j % per + per)),
            pl.BlockSpec((1, 1, block), lambda j: (j, 0, 0)),
            resident((8, dim)),
        ],
        out_specs=[resident((tokens, dim))] * 2
        + [resident((half, width))] * (2 * clips)
        + [
            up_spec,
            up_spec,
            resident((2, dim, width)),
            resident((8, dim)),
            pl.BlockSpec((1, 1, block), lambda j: (j, 0, 0)),
        ],
        out_shape=(
            jax.ShapeDtypeStruct((tokens, dim), BF),
            jax.ShapeDtypeStruct((tokens, dim), F32),
        )
        + (jax.ShapeDtypeStruct((half, width), BF),) * (2 * clips)
        + (
            jax.ShapeDtypeStruct((2, dim, hidden), BF),
            jax.ShapeDtypeStruct((2, dim, hidden), BF),
            jax.ShapeDtypeStruct((2, dim, width), BF),
            jax.ShapeDtypeStruct((8, dim), F32),
            jax.ShapeDtypeStruct((2 * per, 1, block), F32),
        ),
        scratch_shapes=[
            pltpu.VMEM((tokens, dim), F32),
            pltpu.VMEM((tokens, dim), BF),
            pltpu.VMEM((dim, tokens), BF),
            pltpu.VMEM((dim, tokens), BF),
            pltpu.VMEM((tokens, dim), F32),
            pltpu.VMEM((tokens, dim), F32),
        ],
        compiler_params=params(56),
        cost_estimate=pl.CostEstimate(
            flops=24 * tokens * dim * hidden, bytes_accessed=30 * MIB, transcendentals=0
        ),
        name="feed_forward",
    )(*o_own, *o_got, x, gy, wide, wide, wide, b1.reshape(2 * per, 1, block), rows)
    y, d1 = out[:2]
    do_own, do_send = out[2 : 2 + clips], out[2 + clips : 2 + 2 * clips]
    dup, ddn, dwo, sums, db1 = out[2 + 2 * clips :]
    return y, d1, do_own, do_send, dup, ddn, dwo, sums, db1.reshape(2, hidden)


def back_kernel(clips, *refs):
    own_refs, got_refs = refs[0:clips], refs[clips : 2 * clips]
    dq_refs = refs[2 * clips : 3 * clips]
    dk_refs = refs[3 * clips : 4 * clips]
    dv_refs = refs[4 * clips : 5 * clips]
    w_ref, rows_ref = refs[5 * clips : 5 * clips + 2]
    outs = refs[5 * clips + 2 :]
    da_own, da_send = outs[0:clips], outs[clips : 2 * clips]
    dw_ref, sums_ref, bias_ref = outs[2 * clips : 2 * clips + 3]
    acc_scr = outs[2 * clips + 3]
    half = own_refs[0].shape[0]
    width = dq_refs[0].shape[1]
    gain, shift = rows_ref[0:1, :], rows_ref[1:2, :]
    sum_gain = jnp.zeros_like(gain)
    sum_da = jnp.zeros_like(gain)
    sum_q = jnp.zeros((1, width), F32)
    sum_v = jnp.zeros((1, width), F32)
    for i in range(clips):
        for s, (x_ref, da_ref) in enumerate(((own_refs[i], da_own[i]), (got_refs[i], da_send[i]))):
            rows = pl.ds(s * half, half)
            normed, _ = normed_rows(x_ref[...].astype(F32))
            act = normed * gain + shift
            act_t = act.astype(BF).T
            da = jnp.zeros(act.shape, F32)
            for j, ref in enumerate((dq_refs[i], dk_refs[i], dv_refs[i])):
                g = ref[rows, :]
                cols = slice(j * width, (j + 1) * width)
                da = da + mm_nt(g, w_ref[:, cols])
                part = mm(act_t, g)
                if i == 0 and s == 0:
                    acc_scr[:, cols] = part
                else:
                    acc_scr[:, cols] += part
                if j == 0:
                    sum_q = sum_q + jnp.sum(g.astype(F32), axis=0, keepdims=True)
                if j == 2:
                    sum_v = sum_v + jnp.sum(g.astype(F32), axis=0, keepdims=True)
            da_ref[...] = da.astype(BF)
            sum_gain = sum_gain + jnp.sum(da * normed, axis=0, keepdims=True)
            sum_da = sum_da + jnp.sum(da, axis=0, keepdims=True)
    dw_ref[...] = acc_scr[...].astype(BF)
    sums_ref[0:1, :] = sum_gain
    sums_ref[1:2, :] = sum_da
    sums_ref[2:8, :] = jnp.zeros((6, sums_ref.shape[1]), F32)
    bias_ref[0:1, :] = sum_q
    bias_ref[1:2, :] = sum_v
    bias_ref[2:8, :] = jnp.zeros((6, width), F32)


def back_call(x_own, x_got, dq, dk, dv, weight, rows):
    clips = len(x_own)
    half, dim = x_own[0].shape
    width = dq[0].shape[1]
    out = pl.pallas_call(
        functools.partial(back_kernel, clips),
        out_shape=(jax.ShapeDtypeStruct((half, dim), BF),) * (2 * clips)
        + (
            jax.ShapeDtypeStruct(weight.shape, BF),
            jax.ShapeDtypeStruct((8, dim), F32),
            jax.ShapeDtypeStruct((8, width), F32),
        ),
        scratch_shapes=[pltpu.VMEM(weight.shape, F32)],
        compiler_params=params(48),
        cost_estimate=pl.CostEstimate(
            flops=8 * clips * half * weight.size, bytes_accessed=16 * MIB, transcendentals=0
        ),
        name="project_back",
    )(*x_own, *x_got, *dq, *dk, *dv, weight, rows)
    return out[:clips], out[clips : 2 * clips], out[2 * clips], out[2 * clips + 1], out[2 * clips + 2]


MESH_ID = pl.DeviceIdType.MESH


def flip(v, bit):
    step = 1 << bit
    return v + step - 2 * step * ((v // step) % 2)


def remote(src, dst, send, recv, device):
    return pltpu.make_async_remote_copy(
        src_ref=src, dst_ref=dst, send_sem=send, recv_sem=recv, device_id=device, device_id_type=MESH_ID
    )


def partners():
    d, c, t = lax.axis_index("dp"), lax.axis_index("ctx"), lax.axis_index("tensor")
    return d, c, t, {
        "x": (d, c, 1 - t),
        "z1": (d, flip(c, 0), t),
        "z2": (d, flip(c, 1), t),
        "core": (flip(d, 0), c, t),
        "y": (flip(d, 1), c, t),
        "swap": (flip(d, 0), flip(c, 1), t),
    }


def greet(devices):
    barrier = pltpu.get_barrier_semaphore()
    for device in devices:
        pl.semaphore_signal(barrier, inc=1, device_id=device, device_id_type=MESH_ID)
    pl.semaphore_wait(barrier, len(devices))


class Plan:
    def __init__(self, steps):
        self.steps = sorted(steps, key=lambda s: s[0])

    def pump(self, now):
        while self.steps and self.steps[0][0] <= now:
            self.steps.pop(0)[1]()


def pick_matrix(out_rows, per, shard):
    rows = shard * (out_rows // per)
    r = lax.broadcasted_iota(jnp.int32, (out_rows, rows), 0)
    k = lax.broadcasted_iota(jnp.int32, (out_rows, rows), 1)
    return jnp.where(k == (r // per) * shard + r % per, 1.0, 0.0).astype(BF)


def attend_pair(q, kvs, s_scr, between):
    n = kvs[0].shape[0]
    ks = [r.at[:, 0:128] for r in kvs]
    v_t = [r[:, 128:256].T for r in kvs]
    parts, lses = [], []
    for h in range(2):
        if h:
            between()
        qh = pick(q, h)
        tops = []
        for i in range(4):
            s = mm_nt(ks[i][...], qh)
            s_scr[h, pl.ds(i * n, n), :] = s
            tops.append(jnp.max(s, axis=0, keepdims=True))
        top = functools.reduce(jnp.maximum, tops)
        total = jnp.zeros_like(top)
        mix = jnp.zeros((HD, q.shape[0]), F32)
        for i in range(4):
            e = jnp.exp(s_scr[h, pl.ds(i * n, n), :] - top)
            total = total + jnp.sum(e, axis=0, keepdims=True)
            mix = mix + mm(v_t[i][h * HD : (h + 1) * HD, :], e.astype(BF))
        parts.append(mix / total)
        lses.append(top + jnp.log(total))
    return jnp.concatenate(parts, axis=0).T.astype(BF), jnp.concatenate(lses, axis=0)


def start_kernel(
    x_home,
    gy_home,
    first,
    second,
    x_ref,
    gy_ref,
    wf_ref,
    ws_ref,
    rows_ref,
    q_ref,
    kv_ref,
    own_ref,
    send_ref,
    got_ref,
    lse_ref,
    s_scr,
    local_sem,
    swap_s,
    swap_r,
    gy_s,
    gy_r,
    xe_s,
    xe_r,
    kv_s,
    kv_r,
    oe_s,
    oe_r,
    f_s,
    f_r,
    s_s,
    s_r,
):
    clips, half, dim = x_home.shape
    shard = first.shape[0]
    chunks = second.shape[0]
    width = q_ref.shape[2]
    pairs = width // 128
    d, c, t, dev = partners()
    me = pl.multiple_of((d * 4 + c) * shard, shard)
    me_z2 = pl.multiple_of((d * 4 + flip(c, 1)) * shard, shard)
    quad = pl.multiple_of(d * 4 * shard, 4 * shard)
    quad_y = pl.multiple_of(flip(d, 1) * 4 * shard, 4 * shard)
    moves = (d % 2) != (c // 2)
    greet([dev[k] for k in ("x", "z1", "z2", "core", "y", "swap")])

    place_f = pltpu.make_async_copy(first, wf_ref.at[pl.ds(me, shard)], local_sem.at[0])
    place_s = pltpu.make_async_copy(second, ws_ref.at[:, 0, pl.ds(me, shard)], local_sem.at[1])
    place_f.start()
    place_s.start()
    keep_x = pltpu.make_async_copy(x_home, x_ref.at[0], local_sem.at[2])
    keep_gy = pltpu.make_async_copy(gy_home, gy_ref, local_sem.at[3])

    swaps = [
        remote(x_home.at[i], x_ref.at[0, i], swap_s.at[i], swap_r.at[i], dev["swap"])
        for i in range(clips)
    ]
    swap_gy = remote(gy_home, gy_ref, gy_s.at[0], gy_r.at[0], dev["swap"])

    @pl.when(moves)
    def _():
        for cp in swaps:
            cp.start()

    @pl.when(jnp.logical_not(moves))
    def _():
        keep_x.start()
        keep_gy.start()

    def first_stage(i, src, rows, count, device):
        block = wf_ref.at[pl.ds(rows, count)]
        return remote(src if src is not None else block, block, f_s.at[i], f_r.at[i], device)

    f_stages = [
        [first_stage(0, first, me, shard, dev["z2"])],
        [first_stage(1, None, me, shard, dev["z1"]), first_stage(2, None, me_z2, shard, dev["z1"])],
        [first_stage(3, None, quad, 4 * shard, dev["y"])],
        [
            first_stage(4, None, quad, 4 * shard, dev["core"]),
            first_stage(5, None, quad_y, 4 * shard, dev["core"]),
        ],
    ]

    def second_stages(ch):
        def own(i, src, rows, count, device):
            block = ws_ref.at[ch, 0, pl.ds(rows, count)]
            return remote(src if src is not None else block, block, s_s.at[ch, i], s_r.at[ch, i], device)

        def both(i, rows, device):
            block = ws_ref.at[ch, :, pl.ds(rows, 4 * shard)]
            return remote(block, block, s_s.at[ch, i], s_r.at[ch, i], device)

        return [
            [own(0, second.at[ch], me, shard, dev["z2"])],
            [own(1, None, me, shard, dev["z1"]), own(2, None, me_z2, shard, dev["z1"])],
            [
                remote(
                    ws_ref.at[ch, 0, pl.ds(quad, 4 * shard)],
                    ws_ref.at[ch, 1, pl.ds(quad, 4 * shard)],
                    s_s.at[ch, 3],
                    s_r.at[ch, 3],
                    dev["x"],
                )
            ],
            [both(4, quad, dev["y"])],
            [both(5, quad, dev["core"]), both(6, quad_y, dev["core"])],
        ]

    def start(copies):
        for cp in copies:
            cp.start()

    def wait(copies):
        for cp in copies:
            cp.wait()

    start(f_stages[0])
    place_f.wait()
    place_s.wait()

    s_stages = [second_stages(ch) for ch in range(chunks)]
    steps = []
    t_z2, t_z1, t_x, t_y, t_c = 17.0, 20.0, 26.0, 32.0, 36.0
    for ch in range(chunks):
        t_z2 += 1.7
        t_z1 = max(t_z1, t_z2) + 3.0
        t_x = max(t_x, t_z1) + 5.0
        t_y = max(t_y, t_x) + 7.0
        t_c = max(t_c, t_y) + 1.6
        for k, when in enumerate((t_z2, t_z1, t_x, t_y, t_c)):

            def step(ch=ch, k=k):
                wait(s_stages[ch][k])
                if k + 1 < len(s_stages[ch]):
                    start(s_stages[ch][k + 1])

            steps.append((when, step))

    def gy_start():
        @pl.when(moves)
        def _():
            swap_gy.start()

    steps.append((40.0, gy_start))
    plan = Plan(steps)

    wait(f_stages[0])
    start(f_stages[1])
    wait(f_stages[1])
    start(f_stages[2])
    exchange = [
        remote(x_ref.at[0, i], x_ref.at[1, i], xe_s.at[i], xe_r.at[i], dev["x"]) for i in range(clips)
    ]

    @pl.when(jnp.logical_not(moves))
    def _():
        keep_x.wait()
        keep_gy.wait()

    for i in range(clips):

        @pl.when(moves)
        def _():
            swaps[i].wait()

        exchange[i].start()
    for ch in range(chunks):
        start(s_stages[ch][0])
    wait(f_stages[2])
    start(f_stages[3])
    wait(f_stages[3])

    extra = wf_ref[:, 3 * width : 3 * width + 128]
    rows_t = extra.astype(F32).T
    rows_ref[0:8, :] = rows_t[0:8, :]
    shards = dim // shard
    qv = mm(pick_matrix(HD, HD // shards, shard), extra).T
    biases = []
    for r in range(2):
        biases.append(
            jnp.concatenate(
                [qv[8 + r * 2 * pairs + h : 9 + r * 2 * pairs + h, :] for h in range(2 * pairs)], axis=1
            )
        )
    gain, shift = rows_t[0:1, :], rows_t[2:3, :]

    def project(i, s):
        normed, _ = normed_rows(x_ref[s, i].astype(F32))
        act = (normed * gain + shift).astype(BF)
        out = mm(act, wf_ref[:, : 3 * width])
        rows = pl.ds(s * half, half)
        q = (out[:, :width] + biases[0]).astype(BF)
        q_ref[i, rows, :] = (q.astype(F32) * score_scale).astype(BF)
        v = out[:, 2 * width :] + biases[1]
        for p in range(pairs):
            kv_ref[0, i, p, rows, 0:128] = out[:, width + p * 128 : width + (p + 1) * 128].astype(BF)
            kv_ref[0, i, p, rows, 128:256] = v[:, p * 128 : (p + 1) * 128].astype(BF)

    def kv_copy(j, u, src, dst, device):
        i, p = u
        return remote(
            kv_ref.at[src, i, p], kv_ref.at[dst, i, p], kv_s.at[j, i, p], kv_r.at[j, i, p], device
        )

    units = [(i, p) for i in range(clips) for p in range(pairs)]
    to_core = [kv_copy(0, u, 0, 1, dev["core"]) for u in units]
    to_z = [kv_copy(1, u, 0, 2, dev["z1"]) for u in units]
    to_diag = [kv_copy(2, u, 2, 3, dev["core"]) for u in units]
    for i in range(clips):
        project(i, 0)
        exchange[i].wait()
        project(i, 1)
        for n in range(i * pairs, (i + 1) * pairs):
            to_z[n].start()
            to_core[n].start()
        plan.pump(22 + 6 * i)

    o_copies = [
        remote(send_ref.at[i], got_ref.at[i], oe_s.at[i], oe_r.at[i], dev["x"]) for i in range(clips)
    ]

    def relay(n):
        if n < len(units):
            to_z[n].wait()
            to_diag[n].start()

    relay(0)
    for n, (i, p) in enumerate(units):
        to_core[n].wait()
        to_diag[n].wait()
        cols = pl.ds(p * 128, 128)
        o, lse = attend_pair(
            q_ref[i, :, cols],
            [kv_ref.at[s, i, p] for s in range(4)],
            s_scr,
            functools.partial(relay, n + 1),
        )
        own_ref[i, :, cols] = o[:half]
        send_ref[i, :, cols] = o[half:]
        lse_ref[i, p] = lse
        plan.pump(35 + 3.4 * n)
        if p == pairs - 1:
            o_copies[i].start()
    plan.pump(1e9)

    @pl.when(moves)
    def _():
        swap_gy.wait()

    wait(o_copies)


def start_call(x_home, gy_home, first, second):
    clips, half, dim = x_home.shape
    shard = first.shape[0]
    width = (first.shape[1] - 128) // 3
    chunks = second.shape[0]
    pairs = width // 128
    any_spec = pl.BlockSpec(memory_space=pl.ANY)
    vmem = pl.BlockSpec(memory_space=pltpu.VMEM)
    dma = pltpu.SemaphoreType.DMA
    return pl.pallas_call(
        start_kernel,
        in_specs=[vmem, any_spec, vmem, any_spec],
        out_specs=[vmem, any_spec, vmem, any_spec] + [vmem] * 7,
        out_shape=(
            jax.ShapeDtypeStruct((2, clips, half, dim), BF),
            jax.ShapeDtypeStruct((clips, half, dim), BF),
            jax.ShapeDtypeStruct((dim, first.shape[1]), BF),
            jax.ShapeDtypeStruct((chunks, 2, dim, second.shape[2]), BF),
            jax.ShapeDtypeStruct((8, dim), F32),
            jax.ShapeDtypeStruct((clips, 2 * half, width), BF),
            jax.ShapeDtypeStruct((4, clips, pairs, 2 * half, 256), BF),
            jax.ShapeDtypeStruct((clips, half, width), BF),
            jax.ShapeDtypeStruct((clips, half, width), BF),
            jax.ShapeDtypeStruct((clips, half, width), BF),
            jax.ShapeDtypeStruct((clips, pairs, 2, 2 * half), F32),
        ),
        scratch_shapes=[
            pltpu.VMEM((2, 8 * half, 2 * half), F32),
            dma((4,)),
            dma((clips,)),
            dma((clips,)),
            dma((1,)),
            dma((1,)),
            dma((clips,)),
            dma((clips,)),
            dma((3, clips, pairs)),
            dma((3, clips, pairs)),
            dma((clips,)),
            dma((clips,)),
            dma((6,)),
            dma((6,)),
            dma((chunks, 7)),
            dma((chunks, 7)),
        ],
        compiler_params=pltpu.CompilerParams(
            collective_id=1, has_side_effects=True, vmem_limit_bytes=56 * MIB
        ),
        cost_estimate=pl.CostEstimate(
            flops=8 * 10**9, bytes_accessed=40 * MIB, transcendentals=11 * 10**6
        ),
        name="start_attend",
    )(x_home, gy_home, first, second)


def ffn_all_kernel(
    blocks,
    shards,
    o_own,
    o_got,
    x_ref,
    gy_ref,
    wo_ref,
    up_ref,
    dn_ref,
    rows_ref,
    y_ref,
    d1_ref,
    do_own,
    do_send,
    dup_ref,
    ddn_ref,
    dwo_ref,
    sums_ref,
    db1_ref,
    proj_scr,
    c_scr,
    ct_scr,
    gyt_scr,
    y_scr,
    dc_scr,
    b1_scr,
):
    clips, half, width = o_own.shape
    dim = x_ref.shape[1]
    block = up_ref.shape[3]
    j = pl.program_id(0)
    gain, shift = rows_ref[1:2, :], rows_ref[3:4, :]
    bias_o, bias_2 = rows_ref[4:5, :], rows_ref[5:6, :]

    @pl.when(j == 0)
    def _():
        for i in range(clips):
            rows = pl.ds(i * half, half)
            proj = mm_nt(o_own[i], wo_ref[0, 0, :, :width]) + mm_nt(o_got[i], wo_ref[0, 1, :, :width]) + bias_o
            proj_scr[rows, :] = proj
            normed, _ = normed_rows(x_ref[rows, :].astype(F32) + proj)
            c_scr[rows, :] = (normed * gain + shift).astype(BF)
        taken = pick_matrix(128, 128 // shards, dim // shards)
        for s in range(2):
            cols = mm(taken, wo_ref[0, s, :, width : width + 128]).T
            for b in range(blocks):
                b1_scr[s * blocks + b] = jnp.concatenate(
                    [cols[b * 4 + r : b * 4 + r + 1, :] for r in range(4)], axis=1
                )
        ct_scr[...] = c_scr[...].T
        gyt_scr[...] = gy_ref[...].T
        y_scr[...] = jnp.zeros_like(y_scr)
        dc_scr[...] = jnp.zeros_like(dc_scr)

    up = up_ref[0, 0]
    dn = dn_ref[0, 0]
    f = mm(c_scr[...], up) + b1_scr[j]
    cdf = 0.5 * (1.0 + lax.erf(f * root_half))
    u = (f * cdf).astype(BF)
    slope = cdf + f * (density_scale * jnp.exp(-0.5 * f * f))
    df = mm(gy_ref[...], dn) * slope
    dfb = df.astype(BF)
    db1_ref[0] = jnp.sum(df, axis=0, keepdims=True)
    y_scr[...] += mm_nt(u, dn)
    dc_scr[...] += mm_nt(dfb, up)
    ddn_ref[0, 0] = mm(gyt_scr[...], u).astype(BF)
    dup_ref[0, 0] = mm(ct_scr[...], dfb).astype(BF)

    @pl.when(j == pl.num_programs(0) - 1)
    def _():
        sum_gain = jnp.zeros_like(gain)
        sum_dc = jnp.zeros_like(gain)
        sum_dh = jnp.zeros_like(gain)
        sum_gy = jnp.zeros_like(gain)
        dwo0 = jnp.zeros((dim, width), F32)
        dwo1 = jnp.zeros((dim, width), F32)
        for i in range(clips):
            rows = pl.ds(i * half, half)
            proj = proj_scr[rows, :]
            normed, inv = normed_rows(x_ref[rows, :].astype(F32) + proj)
            y_ref[rows, :] = (proj + y_scr[rows, :] + bias_2).astype(BF)
            dc = dc_scr[rows, :]
            t = dc * gain
            d1 = inv * (t - row_mean(t) - normed * row_mean(t * normed))
            d1_ref[rows, :] = d1
            dh = gy_ref[rows, :].astype(F32) + d1
            dy = dh.astype(BF)
            sum_gain = sum_gain + jnp.sum(dc * normed, axis=0, keepdims=True)
            sum_dc = sum_dc + jnp.sum(dc, axis=0, keepdims=True)
            sum_dh = sum_dh + jnp.sum(dh, axis=0, keepdims=True)
            sum_gy = sum_gy + jnp.sum(gy_ref[rows, :].astype(F32), axis=0, keepdims=True)
            do_own[i] = mm(dy, wo_ref[0, 0, :, :width]).astype(BF)
            do_send[i] = mm(dy, wo_ref[0, 1, :, :width]).astype(BF)
            dy_t = dy.T
            dwo0 = dwo0 + mm(dy_t, o_own[i])
            dwo1 = dwo1 + mm(dy_t, o_got[i])
        dwo_ref[0, :, :width] = dwo0.astype(BF)
        dwo_ref[1, :, :width] = dwo1.astype(BF)
        dwo_ref[:, :, width:] = jnp.zeros((2, dim, block - width), BF)
        sums_ref[0:1, :] = sum_gain
        sums_ref[1:2, :] = sum_dc
        sums_ref[2:3, :] = sum_dh
        sums_ref[3:4, :] = sum_gy
        sums_ref[4:8, :] = jnp.zeros((4, dim), F32)


def ffn_all_call(o_own, o_got, x, gy, wide, rows, shards):
    clips, half, width = o_own.shape
    tokens, dim = gy.shape
    chunks, _, _, block = wide.shape
    per = (chunks - 1) // 2
    hidden = per * block
    resident = lambda shape: pl.BlockSpec(
        shape, lambda j: (0,) * len(shape), pipeline_mode=pl.Buffered(1)
    )
    up_spec = pl.BlockSpec((1, 1, dim, block), lambda j: (j % per, j // per, 0, 0))
    head = resident((clips, half, width))
    return pl.pallas_call(
        functools.partial(ffn_all_kernel, per, shards),
        grid=(2 * per,),
        in_specs=[
            head,
            head,
            resident((tokens, dim)),
            resident((tokens, dim)),
            pl.BlockSpec(
                (1, 2, dim, block), lambda j: (2 * per, 0, 0, 0), pipeline_mode=pl.Buffered(1)
            ),
            up_spec,
            pl.BlockSpec((1, 1, dim, block), lambda j: (j % per + per, j // per, 0, 0)),
            resident((8, dim)),
        ],
        out_specs=[
            resident((tokens, dim)),
            resident((tokens, dim)),
            head,
            head,
            up_spec,
            up_spec,
            resident((2, dim, block)),
            resident((8, dim)),
            pl.BlockSpec((1, 1, block), lambda j: (j, 0, 0)),
        ],
        out_shape=(
            jax.ShapeDtypeStruct((tokens, dim), BF),
            jax.ShapeDtypeStruct((tokens, dim), F32),
            jax.ShapeDtypeStruct((clips, half, width), BF),
            jax.ShapeDtypeStruct((clips, half, width), BF),
            jax.ShapeDtypeStruct((per, 2, dim, block), BF),
            jax.ShapeDtypeStruct((per, 2, dim, block), BF),
            jax.ShapeDtypeStruct((2, dim, block), BF),
            jax.ShapeDtypeStruct((8, dim), F32),
            jax.ShapeDtypeStruct((2 * per, 1, block), F32),
        ),
        scratch_shapes=[
            pltpu.VMEM((tokens, dim), F32),
            pltpu.VMEM((tokens, dim), BF),
            pltpu.VMEM((dim, tokens), BF),
            pltpu.VMEM((dim, tokens), BF),
            pltpu.VMEM((tokens, dim), F32),
            pltpu.VMEM((tokens, dim), F32),
            pltpu.VMEM((2 * per, 1, block), F32),
        ],
        compiler_params=params(56),
        cost_estimate=pl.CostEstimate(
            flops=24 * tokens * dim * hidden, bytes_accessed=30 * MIB, transcendentals=0
        ),
        name="feed_forward_all",
    )(o_own, o_got, x, gy, wide, wide, wide, rows)


def end_kernel(
    q_ref,
    kv_hbm,
    own_ref,
    send_ref,
    lse_ref,
    do_own_ref,
    do_send_ref,
    x_hbm,
    wf_hbm,
    rows_ref,
    d1_hbm,
    y_hbm,
    up_hbm,
    dn_hbm,
    wo_hbm,
    sums_ref,
    db1_ref,
    yh_ref,
    dh_ref,
    g2_ref,
    g1_ref,
    vec_ref,
    kv_scr,
    x_scr,
    wf_scr,
    d1_scr,
    do_got,
    core_got,
    z_got,
    dq_scr,
    acc_scr,
    dw_scr,
    da_own,
    da_send,
    da_got,
    delta_scr,
    loc_scr,
    rc_scr,
    ry_scr,
    rx_scr,
    rz1_scr,
    rz2_scr,
    c1_scr,
    y1_scr,
    p1_scr,
    q1_scr,
    vs_scr,
    vr_scr,
    kv_sem,
    in_sem,
    loc_sem,
    keep_sem,
    do_s,
    do_r,
    y_s,
    y_r,
    dc_s,
    dc_r,
    dz_s,
    dz_r,
    da_s,
    da_r,
    sw_s,
    sw_r,
    h_s,
    h_r,
    g_s,
    g_r,
    v_s,
    v_r,
):
    clips, half, width = own_ref.shape
    pairs = width // 128
    dim = rows_ref.shape[1]
    shard = g1_ref.shape[0]
    chunks = g2_ref.shape[0]
    per = (chunks - 1) // 2
    rows4 = 4 * shard
    d, c, t, dev = partners()
    moves = (d % 2) != (c // 2)
    greet([dev[k] for k in ("x", "z1", "z2", "core", "y", "swap")])

    def start(copies):
        for cp in copies:
            cp.start()

    def wait(copies):
        for cp in copies:
            cp.wait()

    units = [(i, p) for i in range(clips) for p in range(pairs)]
    do_copies = [
        remote(do_send_ref.at[i], do_got.at[i], do_s.at[i], do_r.at[i], dev["x"]) for i in range(clips)
    ]
    start(do_copies)
    loads = [
        pltpu.make_async_copy(
            kv_hbm.at[:, i, p], kv_scr.at[:, i, p], kv_sem.at[i, p]
        )
        for i, p in units
    ]
    start(loads)
    late = [
        pltpu.make_async_copy(x_hbm, x_scr, in_sem.at[0]),
        pltpu.make_async_copy(wf_hbm, wf_scr, in_sem.at[1]),
        pltpu.make_async_copy(d1_hbm, d1_scr, in_sem.at[2]),
    ]
    start(late)
    y_swap = remote(y_hbm, yh_ref, y_s.at[0], y_r.at[0], dev["swap"])
    y_keep = pltpu.make_async_copy(y_hbm, yh_ref, keep_sem.at[0])

    @pl.when(moves)
    def _():
        y_swap.start()

    @pl.when(jnp.logical_not(moves))
    def _():
        y_keep.start()

    def grad(ch):
        if ch < per:
            return up_hbm.at[ch]
        if ch < 2 * per:
            return dn_hbm.at[ch - per]
        return wo_hbm

    def band(block):
        return pl.ds(pl.multiple_of(block * rows4, rows4), rows4)

    def strip(block):
        return pl.ds(pl.multiple_of(block * shard, shard), shard)

    mine = [d, flip(d, 1)]
    theirs = [flip(d, 0), flip(flip(d, 0), 1)]

    def g_copy(ch, k, src, dst, device):
        return remote(src, dst, g_s.at[ch, k], g_r.at[ch, k], device)

    def g_stages(ch):
        return [
            [
                g_copy(ch, k, grad(ch).at[:, band(theirs[k])], rc_scr.at[ch, k], dev["core"])
                for k in range(2)
            ],
            [g_copy(ch, 2, rc_scr.at[ch, 1], ry_scr.at[ch], dev["y"])],
            [g_copy(ch, 3, ry_scr.at[ch, 1], rx_scr.at[ch], dev["x"])],
            [
                g_copy(ch, 4, rx_scr.at[ch, strip(flip(c, 0))], rz1_scr.at[ch, 0], dev["z1"]),
                g_copy(
                    ch, 5, rx_scr.at[ch, strip(flip(flip(c, 0), 1))], rz1_scr.at[ch, 1], dev["z1"]
                ),
            ],
            [g_copy(ch, 6, rz1_scr.at[ch, 1], rz2_scr.at[ch], dev["z2"])],
        ]

    stages = [g_stages(ch) for ch in range(chunks)]
    own_loads = [
        [
            pltpu.make_async_copy(
                grad(ch).at[:, band(mine[k])], loc_scr.at[ch % 2, k], loc_sem.at[ch % 2, k]
            )
            for k in range(2)
        ]
        for ch in range(chunks)
    ]

    def g_step(ch, k):
        wait(stages[ch][k])
        if k == 0:
            wait(own_loads[ch])
            for m in range(2):
                rc_scr[ch, m] = rc_scr[ch, m] + loc_scr[ch % 2, m]
            if ch + 2 < chunks:
                start(own_loads[ch + 2])
        elif k == 1:
            ry_scr[ch] = ry_scr[ch] + rc_scr[ch, 0]
        elif k == 2:
            rx_scr[ch] = rx_scr[ch] + ry_scr[ch, 0]
        elif k == 3:
            rz1_scr[ch, 0] = rz1_scr[ch, 0] + rx_scr[ch, strip(c)]
            rz1_scr[ch, 1] = rz1_scr[ch, 1] + rx_scr[ch, strip(flip(c, 1))]
        else:
            g2_ref[ch] = rz1_scr[ch, 0].astype(F32) + rz2_scr[ch].astype(F32)
        if k + 1 < len(stages[ch]):
            start(stages[ch][k + 1])

    steps = []
    t0, t1, t2, t3, t4 = 4.0, 8.0, 14.0, 20.0, 24.0
    for ch in range(chunks):
        t0 += 2.0
        t1 = max(t1, t0) + 7.0
        t2 = max(t2, t1) + 5.0
        t3 = max(t3, t2) + 3.0
        t4 = max(t4, t3) + 3.0
        for k, when in enumerate((t0, t1, t2, t3, t4)):
            steps.append((when, functools.partial(g_step, ch, k)))
    plan = Plan(steps)
    start(own_loads[0])
    start(own_loads[1])

    def dkv_copies(u):
        i, p = u
        return [
            remote(
                kv_scr.at[2 * m + 1, i, p],
                core_got.at[m, i, p],
                dc_s.at[m, i, p],
                dc_r.at[m, i, p],
                dev["core"],
            )
            for m in range(2)
        ]

    def dkv_z(u):
        i, p = u
        return remote(kv_scr.at[2, i, p], z_got.at[i, p], dz_s.at[i, p], dz_r.at[i, p], dev["z1"])

    to_core = [dkv_copies(u) for u in units]
    to_z = [dkv_z(u) for u in units]

    def relay(n):
        if n < 0:
            return
        i, p = units[n]
        wait(to_core[n])
        kv_scr[2, i, p] = kv_scr[2, i, p] + core_got[1, i, p]
        to_z[n].start()

    def attention(n):
        i, p = units[n]
        cols = pl.ds(p * 128, 128)
        loads[n].wait()
        q = q_ref[i, :, cols]
        do = jnp.concatenate([do_own_ref[i, :, cols], do_got[i, :, cols]], axis=0)
        o = jnp.concatenate([own_ref[i, :, cols], send_ref[i, :, cols]], axis=0)
        prod_t = (do.astype(F32) * o.astype(F32)).T
        q_heads = [pick(q, h) for h in range(2)]
        do_heads = [pick(do, h) for h in range(2)]
        deltas = [
            jnp.sum(prod_t[h * HD : (h + 1) * HD, :], axis=0, keepdims=True) for h in range(2)
        ]
        lses = [lse_ref[i, p, h : h + 1, :] for h in range(2)]
        dq_t = [jnp.zeros((HD, q.shape[0]), F32) for _ in range(2)]
        for s in range(4):
            k = kv_scr[s, i, p, :, 0:128]
            v = kv_scr[s, i, p, :, 128:256]
            k_t = k.T
            dk = jnp.zeros(k.shape, F32)
            dv = jnp.zeros(k.shape, F32)
            for h in range(2):
                prob = jnp.exp(mm_nt(k, q_heads[h]) - lses[h])
                dv = dv + mm(prob.astype(BF), do_heads[h])
                ds = (prob * (mm_nt(v, do_heads[h]) - deltas[h])).astype(BF)
                dk = dk + mm(ds, q_heads[h])
                dq_t[h] = dq_t[h] + mm(k_t[h * HD : (h + 1) * HD, :], ds)
            kv_scr[s, i, p, :, 0:128] = dk.astype(BF)
            kv_scr[s, i, p, :, 128:256] = dv.astype(BF)
            if s == 1:
                relay(n - 1)
        dq_scr[i, :, cols] = (jnp.concatenate(dq_t, axis=0).T * score_scale).astype(BF)
        start(to_core[n])

    gain, shift = rows_ref[0:1, :], rows_ref[2:3, :]
    sums = {
        "gain": jnp.zeros((1, dim), F32),
        "da": jnp.zeros((1, dim), F32),
        "q": jnp.zeros((1, width), F32),
        "v": jnp.zeros((1, width), F32),
    }
    da_copies = [
        remote(da_send.at[i], da_got.at[i], da_s.at[i], da_r.at[i], dev["x"]) for i in range(clips)
    ]

    def project_back(i):
        for n, u in enumerate(units):
            if u[0] == i:
                to_z[n].wait()
        for s in (1, 0):
            rows = pl.ds(s * half, half)
            normed, _ = normed_rows(x_scr[s, i].astype(F32))
            act_t = (normed * gain + shift).astype(BF).T
            halves = [
                kv_scr[0, i, p, rows, :] + (core_got[0, i, p, rows, :] + z_got[i, p, rows, :])
                for p in range(pairs)
            ]
            g = jnp.concatenate(
                [dq_scr[i, rows, :]] + [v[:, :128] for v in halves] + [v[:, 128:] for v in halves],
                axis=1,
            )
            da = mm_nt(g, wf_scr[:, : 3 * width])
            part = mm(act_t, g)
            if i == 0 and s == 1:
                acc_scr[...] = part
            else:
                acc_scr[...] += part
            total = jnp.sum(g.astype(F32), axis=0, keepdims=True)
            sums["q"] = sums["q"] + total[:, :width]
            sums["v"] = sums["v"] + total[:, 2 * width :]
            sums["gain"] = sums["gain"] + jnp.sum(da * normed, axis=0, keepdims=True)
            sums["da"] = sums["da"] + jnp.sum(da, axis=0, keepdims=True)
            if s:
                da_send[i] = da.astype(BF)
                da_copies[i].start()
            else:
                da_own[i] = da

    swaps = [
        remote(delta_scr.at[i], dh_ref.at[i], sw_s.at[i], sw_r.at[i], dev["swap"]) for i in range(clips)
    ]
    keeps = [
        pltpu.make_async_copy(delta_scr.at[i], dh_ref.at[i], keep_sem.at[1 + i]) for i in range(clips)
    ]

    def finish(i):
        da_copies[i].wait()
        w = (da_own[i] + da_got[i].astype(F32)) * gain
        normed, inv = normed_rows(x_scr[0, i].astype(F32))
        rows = pl.ds(i * half, half)
        delta_scr[i] = (
            d1_scr[rows, :] + inv * (w - row_mean(w) - normed * row_mean(w * normed))
        ).astype(BF)

        @pl.when(moves)
        def _():
            swaps[i].start()

        @pl.when(jnp.logical_not(moves))
        def _():
            keeps[i].start()

    for ch in range(chunks):
        start(stages[ch][0])
    for n, (i, p) in enumerate(units):
        if p == 0:
            do_copies[i].wait()
        attention(n)
        plan.pump(4 + 4.8 * (n + 1) + 3.4 * max(i - (p < 1), 0))
        if i > 0 and p == 1:
            if i == 1:
                wait(late)
            project_back(i - 1)
        if i > 1 and p == 0:
            finish(i - 2)
    relay(len(units) - 1)
    if clips == 1:
        wait(late)
    plan.pump(60.0)
    if clips > 1:
        finish(clips - 2)
    project_back(clips - 1)

    def h_copy(k, src, dst, device):
        return remote(src, dst, h_s.at[k], h_r.at[k], device)

    dw_scr[...] = acc_scr[...].astype(BF)
    h_stages = [
        [h_copy(k, dw_scr.at[band(theirs[k])], c1_scr.at[k], dev["core"]) for k in range(2)],
        [h_copy(2, c1_scr.at[1], y1_scr, dev["y"])],
        [
            h_copy(3, y1_scr.at[strip(flip(c, 0))], p1_scr.at[0], dev["z1"]),
            h_copy(4, y1_scr.at[strip(flip(flip(c, 0), 1))], p1_scr.at[1], dev["z1"]),
        ],
        [h_copy(5, p1_scr.at[1], q1_scr, dev["z2"])],
    ]
    start(h_stages[0])

    zero = jnp.zeros((1, dim), F32)
    shared = [
        sums["gain"],
        sums_ref[0:1, :],
        sums["da"],
        sums_ref[1:2, :],
        sums_ref[2:3, :],
        sums_ref[3:4, :],
    ]
    ub = [
        jnp.concatenate([db1_ref[s * per + b] for b in range(per)], axis=1) for s in range(2)
    ]
    for r, row in enumerate(shared):
        vs_scr[0, r : r + 1, :] = row
        vs_scr[1, r : r + 1, :] = row
    vs_scr[0, 6:7, :] = jnp.concatenate([sums["q"], sums["v"]], axis=1)
    vs_scr[1, 6:7, :] = zero
    vs_scr[0, 7:8, :] = zero
    vs_scr[1, 7:8, :] = zero
    vs_scr[0, 10:16, :] = jnp.zeros((6, dim), F32)
    vs_scr[1, 10:16, :] = jnp.zeros((6, dim), F32)
    for s in range(2):
        vs_scr[s, 8:9, :] = ub[s][:, :dim]
        vs_scr[s, 9:10, :] = ub[s][:, dim:]
    v_devices = ("x", "core", "y", "z1", "z2")

    def v_copy(k):
        src = vs_scr.at[1] if k == 0 else vs_scr.at[0] if k == 1 else vr_scr.at[k - 1]
        return remote(src, vr_scr.at[k], v_s.at[k], v_r.at[k], dev[v_devices[k]])

    v_copies = [v_copy(k) for k in range(len(v_devices))]

    def v_step(k):
        v_copies[k].wait()
        if k == 0:
            vs_scr[0] = vs_scr[0] + vr_scr[0]
        elif k == 1:
            vr_scr[1] = vr_scr[1] + vs_scr[0]
        else:
            vr_scr[k] = vr_scr[k] + vr_scr[k - 1]
        if k + 1 < len(v_devices):
            v_copies[k + 1].start()
        else:
            vec_ref[...] = vr_scr[k]

    v_copies[0].start()
    wait(h_stages[0])
    for m in range(2):
        c1_scr[m] = c1_scr[m] + dw_scr[band(mine[m]), :]
    start(h_stages[1])
    v_step(0)
    plan.pump(1e9)
    v_step(1)
    finish(clips - 1)
    v_step(2)
    wait(h_stages[1])
    y1_scr[...] = y1_scr[...] + c1_scr[0]
    start(h_stages[2])
    v_step(3)
    wait(h_stages[2])
    p1_scr[0] = p1_scr[0] + y1_scr[strip(c), :]
    p1_scr[1] = p1_scr[1] + y1_scr[strip(flip(c, 1)), :]
    start(h_stages[3])
    v_step(4)
    wait(h_stages[3])
    g1_ref[...] = p1_scr[0].astype(F32) + q1_scr[...].astype(F32)

    @pl.when(moves)
    def _():
        y_swap.wait()
        wait(swaps)

    @pl.when(jnp.logical_not(moves))
    def _():
        y_keep.wait()
        wait(keeps)


def end_call(q, kv, own, send, lse, do_own, do_send, x, wf, rows, d1, y, up, dn, wo, sums, db1):
    clips, half, width = own.shape
    pairs = width // 128
    dim = rows.shape[1]
    shard = dim // 16
    per, _, _, block = up.shape
    chunks = 2 * per + 1
    any_spec = pl.BlockSpec(memory_space=pl.ANY)
    vmem = pl.BlockSpec(memory_space=pltpu.VMEM)
    dma = pltpu.SemaphoreType.DMA
    rows4 = 4 * shard
    both = lambda *shape: [dma(shape), dma(shape)]
    return pl.pallas_call(
        end_kernel,
        in_specs=[vmem, any_spec, vmem, vmem, vmem, vmem, vmem, any_spec, any_spec, vmem]
        + [any_spec] * 5
        + [vmem, vmem],
        out_specs=[any_spec, any_spec, vmem, vmem, vmem],
        out_shape=(
            jax.ShapeDtypeStruct((clips, half, dim), BF),
            jax.ShapeDtypeStruct((clips, half, dim), BF),
            jax.ShapeDtypeStruct((chunks, shard, block), F32),
            jax.ShapeDtypeStruct((shard, 3 * width), F32),
            jax.ShapeDtypeStruct((16, dim), F32),
        ),
        scratch_shapes=[
            pltpu.VMEM(kv.shape, BF),
            pltpu.VMEM(x.shape, BF),
            pltpu.VMEM(wf.shape, BF),
            pltpu.VMEM(d1.shape, F32),
            pltpu.VMEM(do_send.shape, BF),
            pltpu.VMEM((2, clips, pairs, 2 * half, 256), BF),
            pltpu.VMEM((clips, pairs, 2 * half, 256), BF),
            pltpu.VMEM(q.shape, BF),
            pltpu.VMEM((dim, 3 * width), F32),
            pltpu.VMEM((dim, 3 * width), BF),
            pltpu.VMEM((clips, half, dim), F32),
            pltpu.VMEM((clips, half, dim), BF),
            pltpu.VMEM((clips, half, dim), BF),
            pltpu.VMEM((clips, half, dim), BF),
            pltpu.VMEM((2, 2, 2, rows4, block), BF),
            pltpu.VMEM((chunks, 2, 2, rows4, block), BF),
            pltpu.VMEM((chunks, 2, rows4, block), BF),
            pltpu.VMEM((chunks, rows4, block), BF),
            pltpu.VMEM((chunks, 2, shard, block), BF),
            pltpu.VMEM((chunks, shard, block), BF),
            pltpu.VMEM((2, rows4, 3 * width), BF),
            pltpu.VMEM((rows4, 3 * width), BF),
            pltpu.VMEM((2, shard, 3 * width), BF),
            pltpu.VMEM((shard, 3 * width), BF),
            pltpu.VMEM((2, 16, dim), F32),
            pltpu.VMEM((5, 16, dim), F32),
            dma((clips, pairs)),
            dma((3,)),
            dma((2, 2)),
            dma((1 + clips,)),
            *both(clips),
            *both(1),
            *both(2, clips, pairs),
            *both(clips, pairs),
            *both(clips),
            *both(clips),
            *both(6),
            *both(chunks, 7),
            *both(5),
        ],
        compiler_params=pltpu.CompilerParams(
            collective_id=2, has_side_effects=True, vmem_limit_bytes=62 * MIB
        ),
        cost_estimate=pl.CostEstimate(
            flops=20 * 10**9, bytes_accessed=40 * MIB, transcendentals=11 * 10**6
        ),
        name="attend_back_end",
    )(q, kv, own, send, lse, do_own, do_send, x, wf, rows, d1, y, up, dn, wo, sums, db1)


class Links:
    def __init__(self, mesh):
        self.dp = mesh.shape["dp"]
        self.ctx = mesh.shape["ctx"]
        self.tensor = mesh.shape["tensor"]
        self.dp_bits = self.dp.bit_length() - 1
        self.ctx_bits = self.ctx.bit_length() - 1

    def flat(self, d, c, t):
        return (d * self.ctx + c) * self.tensor + t

    def move(self, value, partner):
        pairs = []
        for d in range(self.dp):
            for c in range(self.ctx):
                for t in range(self.tensor):
                    other = partner(d, c, t)
                    if other != (d, c, t):
                        pairs.append((self.flat(d, c, t), self.flat(*other)))
        return lax.ppermute(value, ("dp", "ctx", "tensor"), pairs)

    def across_x(self, value):
        return self.move(value, lambda d, c, t: (d, c, t ^ 1))

    def across_core(self, value):
        return self.move(value, lambda d, c, t: (d ^ 1, c, t))

    def across_z(self, value):
        return self.move(value, lambda d, c, t: (d, c ^ 1, t))

    def stays(self):
        d, c = lax.axis_index("dp"), lax.axis_index("ctx")
        return (d % 2) == (c // (self.ctx // 2))

    def swap(self, value):
        half = self.ctx // 2
        moved = self.move(
            value,
            lambda d, c, t: (d, c, t) if d % 2 == c // half else (d ^ 1, c ^ half, t),
        )
        return jnp.where(self.stays(), value, moved)

    def stages(self):
        out = []
        for bit in reversed(range(self.ctx_bits)):
            out.append(("ctx", bit, self.ctx_bits - 1 - bit))
        for bit in reversed(range(self.dp_bits)):
            out.append(("dp", bit, self.dp_bits - 1 - bit))
        return out

    def step(self, value, axis, bit):
        if axis == "ctx":
            return self.move(value, lambda d, c, t: (d, c ^ (1 << bit), t))
        return self.move(value, lambda d, c, t: (d ^ (1 << bit), c, t))

    def side(self, axis, bit):
        return (lax.axis_index(axis) // (1 << bit)) % 2

    def gather(self, value, both):
        shape = value.shape
        lead = 0
        for axis, bit, place in self.stages():
            if axis == "dp" and both and not lead:
                value = jnp.stack([value, self.across_x(value)])
                lead = 1
            got = self.step(value, axis, bit)
            low = self.side(axis, bit) == 0
            value = jnp.stack(
                [jnp.where(low, value, got), jnp.where(low, got, value)], axis=lead + place
            )
        shards = self.dp * self.ctx
        return value.reshape((2,) * lead + (shards * shape[0],) + shape[1:])

    def scatter(self, value, both):
        lead = 1 if both else 0
        rest = value.shape[lead + 1 :]
        value = value.reshape(
            value.shape[:lead] + (2,) * (self.dp_bits + self.ctx_bits) + rest
        )
        for axis, bit, place in reversed(self.stages()):
            if axis == "ctx" and lead:
                value = value[0] + self.across_x(value[1])
                lead = 0
            side = self.side(axis, bit)
            keep = lax.dynamic_index_in_dim(value, side, lead + place, keepdims=False)
            give = lax.dynamic_index_in_dim(value, 1 - side, lead + place, keepdims=False)
            value = keep + self.step(give, axis, bit)
        return value


def body(links, *args):
    (
        block_input,
        out_cotangent,
        qkv_weight,
        proj_weight,
        up_weight,
        down_weight,
        norm_gains,
        shift_terms,
        qv_bias,
        up_bias,
        qkv_first,
        qkv_second,
        proj_first,
        proj_second,
        up_first,
        up_second,
        down_first,
        down_second,
        gains_first,
        gains_second,
        shifts_first,
        shifts_second,
        qv_bias_first,
        qv_bias_second,
        up_bias_first,
        up_bias_second,
    ) = args
    half, clips, dim = block_input.shape
    shard = qkv_weight.shape[0]
    shards = dim // shard
    width = qkv_weight.shape[2]
    hidden = up_weight.shape[1]
    heads = width // HD

    x_home = jnp.transpose(block_input, (1, 0, 2)).astype(BF)
    gy_home = jnp.transpose(out_cotangent, (1, 0, 2)).astype(BF)
    x = links.swap(x_home)
    x_own = [x[i] for i in range(clips)]
    x_got = [links.across_x(v) for v in x_own]

    def lanes(parts):
        flat = jnp.concatenate([p.astype(BF).reshape(-1) for p in parts])
        return jnp.pad(flat, (0, shard * 128 - flat.size)).reshape(shard, 128)

    first = jnp.concatenate(
        [qkv_weight.reshape(shard, 3 * width).astype(BF), lanes([norm_gains, shift_terms, qv_bias])],
        axis=1,
    )
    second = jnp.concatenate(
        [up_weight.astype(BF), down_weight.astype(BF), proj_weight.astype(BF), lanes([up_bias])],
        axis=1,
    )
    first = links.gather(first, False)
    second = links.gather(second, True)
    w_qkv = first[:, : 3 * width]
    small = first[:, 3 * width :].reshape(shards, shard * 128)
    n_g, n_s = 2 * shard, 4 * shard
    gains = jnp.transpose(small[:, :n_g].reshape(shards, 2, shard), (1, 0, 2)).reshape(2, dim)
    shifts = jnp.transpose(
        small[:, n_g : n_g + n_s].reshape(shards, 4, shard), (1, 0, 2)
    ).reshape(4, dim)
    qv_cols = qv_bias.shape[2]
    biases = jnp.transpose(
        small[:, n_g + n_s : n_g + n_s + qv_bias.size].reshape(shards, 2, heads, qv_cols),
        (1, 2, 0, 3),
    ).reshape(2, width)
    ub_rows, ub_cols = up_bias.shape
    b1 = jnp.transpose(
        second[:, :, 2 * hidden + width :]
        .reshape(2, shards, shard * 128)[:, :, : up_bias.size]
        .reshape(2, shards, ub_rows, ub_cols),
        (0, 2, 1, 3),
    ).reshape(2, hidden)
    gains, shifts, biases, b1 = (v.astype(F32) for v in (gains, shifts, biases, b1))
    zero4 = jnp.zeros((4, dim), F32)
    rows_one = jnp.concatenate([gains[0:1], shifts[0:1], zero4, zero4[:2]])
    rows_two = jnp.concatenate([gains[1:2], shifts[1:4], zero4])
    biases = jnp.concatenate([biases, jnp.zeros((6, width), F32)])

    q, pieces, o_own, o_send, o_got, lse = [], [], [], [], [], []
    for i in range(clips):
        q_i, kv = qkv_call(x_own[i], x_got[i], w_qkv, rows_one, biases)
        kv_z = links.across_z(kv)
        kv_c = links.across_core(kv)
        kv_d = links.across_core(kv_z)
        q.append(q_i)
        pieces.append((kv, kv_c, kv_z, kv_d))
    gy = links.swap(gy_home)
    for i in range(clips):
        own, send, lse_i = attend_call(q[i], pieces[i])
        o_own.append(own)
        o_send.append(send)
        o_got.append(links.across_x(send))
        lse.append(lse_i)

    tokens = clips * half
    y, d1, do_own, do_send, d_up, d_down, d_proj, sums_two, d_b1 = ffn_call(
        o_own, o_got, x.reshape(tokens, dim), gy.reshape(tokens, dim), second, b1, rows_two
    )
    y_home = links.swap(y.reshape(clips, half, dim))
    block_output = block_input + jnp.transpose(y_home, (1, 0, 2)).astype(F32)

    grads_two = jnp.concatenate([d_up, d_down, d_proj], axis=2)
    grads_two = links.scatter(grads_two.reshape(2, shards, shard, -1), True)

    dq, dk, dv = [], [], []
    do_got = [links.across_x(v) for v in do_send]
    for i in range(clips):
        dq_i, dks, dvs = attend_back_call(
            q[i], do_own[i], do_got[i], o_own[i], o_send[i], lse[i], pieces[i]
        )
        dq.append(dq_i)
        for parts, out in ((dks, dk), (dvs, dv)):
            mine, core, z, diag = parts
            mine = mine + links.across_core(core)
            z = z + links.across_core(diag)
            out.append(mine + links.across_z(z))
    da_own, da_send, d_qkv, sums_one, sums_bias = back_call(
        x_own, x_got, dq, dk, dv, w_qkv, rows_one
    )
    grads_one = links.scatter(d_qkv.reshape(shards, shard, 3 * width), False)
    d1 = d1.reshape(clips, half, dim)
    deltas = []
    for i in range(clips):
        da = da_own[i].astype(F32) + links.across_x(da_send[i]).astype(F32)
        normed, inv = normed_rows(x_own[i].astype(F32))
        w = da * gains[0]
        deltas.append(
            (d1[i] + inv * (w - row_mean(w) - normed * row_mean(w * normed))).astype(BF)
        )
    delta_home = links.swap(jnp.stack(deltas))
    input_grad = out_cotangent + jnp.transpose(delta_home, (1, 0, 2)).astype(F32)

    cot_sum = jnp.sum(out_cotangent, axis=(0, 1))[None]
    both = jnp.concatenate(
        [sums_one[0:1], sums_two[0:1], sums_one[1:2], sums_two[1:2], sums_two[2:3], cot_sum]
    )
    both = jnp.transpose(both.reshape(6, shards, shard), (1, 0, 2)).reshape(shards, 6 * shard)
    ub = jnp.transpose(d_b1.reshape(2, ub_rows, shards, ub_cols), (0, 2, 1, 3)).reshape(
        2, shards, up_bias.size
    )
    crossed = links.across_x(jnp.concatenate([both, ub[1]], axis=1))
    qv = jnp.transpose(
        sums_bias[0:2].reshape(2, heads, shards, qv_cols), (2, 0, 1, 3)
    ).reshape(shards, qv_bias.size)
    vec = jnp.concatenate([jnp.concatenate([both, ub[0]], axis=1) + crossed, qv], axis=1)
    vec = links.scatter(vec, False)
    gains_grad = vec[:n_g].reshape(2, shard)
    shifts_grad = vec[n_g : n_g + n_s].reshape(4, shard)
    up_bias_grad = vec[6 * shard : 6 * shard + up_bias.size].reshape(up_bias.shape)
    qv_bias_grad = vec[6 * shard + up_bias.size :].reshape(qv_bias.shape)

    qkv_grad = grads_one.astype(F32).reshape(qkv_weight.shape)
    grads_two = grads_two.astype(F32)
    up_grad = grads_two[:, :hidden]
    down_grad = grads_two[:, hidden : 2 * hidden]
    proj_grad = grads_two[:, 2 * hidden :]

    qkv_next = adam_step(qkv_weight, qkv_first, qkv_second, qkv_grad, rate_qkv, decay_rate)
    proj_next = adam_step(proj_weight, proj_first, proj_second, proj_grad, rate_proj, decay_rate)
    up_next = adam_step(up_weight, up_first, up_second, up_grad, rate_up, decay_rate)
    down_next = adam_step(down_weight, down_first, down_second, down_grad, rate_down, decay_rate)
    gains_next = adam_step(norm_gains, gains_first, gains_second, gains_grad, rate_gains, 0.0)
    shifts_next = adam_step(shift_terms, shifts_first, shifts_second, shifts_grad, rate_shifts, 0.0)
    qv_next = adam_step(qv_bias, qv_bias_first, qv_bias_second, qv_bias_grad, rate_query_bias, 0.0)
    ub_next = adam_step(up_bias, up_bias_first, up_bias_second, up_bias_grad, rate_up_bias, 0.0)
    nexts = (qkv_next, proj_next, up_next, down_next, gains_next, shifts_next, qv_next, ub_next)
    return (
        block_output,
        input_grad,
        qkv_grad,
        proj_grad,
        up_grad,
        down_grad,
        gains_grad,
        shifts_grad,
        qv_bias_grad,
        up_bias_grad,
        *(n[0] for n in nexts),
        *(m for n in nexts for m in n[1:]),
    )


def body_fused(links, *args):
    (
        block_input,
        out_cotangent,
        qkv_weight,
        proj_weight,
        up_weight,
        down_weight,
        norm_gains,
        shift_terms,
        qv_bias,
        up_bias,
        *moments,
    ) = args
    half, clips, dim = block_input.shape
    shard = qkv_weight.shape[0]
    shards = dim // shard
    width = qkv_weight.shape[2]
    hidden = up_weight.shape[1]
    heads = width // HD
    block = 512
    per = hidden // block
    me = lax.axis_index("dp") * lax.axis_size("ctx") + lax.axis_index("ctx")

    x_home = jnp.transpose(block_input, (1, 0, 2)).astype(BF)
    gy_home = jnp.transpose(out_cotangent, (1, 0, 2)).astype(BF)

    def columns(v):
        return jnp.pad(v.T, ((0, shard - v.shape[1]), (0, 0)))

    first = jnp.concatenate(
        [
            qkv_weight.reshape(shard, 3 * width),
            columns(norm_gains),
            columns(shift_terms),
            jnp.zeros((shard, 2), F32),
            columns(qv_bias.reshape(2 * heads, -1)),
            jnp.zeros((shard, 120 - 2 * heads), F32),
        ],
        axis=1,
    ).astype(BF)
    last = jnp.concatenate(
        [
            proj_weight,
            columns(up_bias),
            jnp.zeros((shard, block - width - up_bias.shape[0]), F32),
        ],
        axis=1,
    )
    second = jnp.stack(
        [w[:, b * block : (b + 1) * block] for w in (up_weight, down_weight) for b in range(per)] + [last]
    ).astype(BF)
    x, gy, wf, ws, rows, q, kv, own, send, got, lse = start_call(x_home, gy_home, first, second)
    tokens = clips * half
    y, d1, do_own, do_send, up, dn, wo, sums, db1 = ffn_all_call(
        own, got, x[0].reshape(tokens, dim), gy.reshape(tokens, dim), ws, rows, shards
    )
    y_home, delta_home, g2, g1, vec = end_call(
        q,
        kv,
        own,
        send,
        lse,
        do_own,
        do_send,
        x,
        wf,
        rows,
        d1,
        y.reshape(clips, half, dim),
        up,
        dn,
        wo,
        sums,
        db1,
    )
    block_output = block_input + jnp.transpose(y_home, (1, 0, 2)).astype(F32)
    input_grad = out_cotangent + jnp.transpose(delta_home, (1, 0, 2)).astype(F32)

    qkv_grad = g1.reshape(qkv_weight.shape)
    up_grad = jnp.concatenate([g2[b] for b in range(per)], axis=1)
    down_grad = jnp.concatenate([g2[per + b] for b in range(per)], axis=1)
    proj_grad = g2[2 * per, :, :width]
    cols = lax.dynamic_slice_in_dim(vec[0:6], me * shard, shard, 1)
    gains_grad, shifts_grad = cols[0:2], cols[2:6]
    qv_cols = qv_bias.shape[2]
    qv_bias_grad = lax.dynamic_slice_in_dim(
        vec[6].reshape(2, heads, HD), me * qv_cols, qv_cols, 2
    )
    ub_cols = up_bias.shape[1]
    up_bias_grad = lax.dynamic_slice_in_dim(
        vec[8:10].reshape(up_bias.shape[0], 128), me * ub_cols, ub_cols, 1
    )
    grads = (
        qkv_grad,
        proj_grad,
        up_grad,
        down_grad,
        gains_grad,
        shifts_grad,
        qv_bias_grad,
        up_bias_grad,
    )
    rates = (
        (rate_qkv, decay_rate),
        (rate_proj, decay_rate),
        (rate_up, decay_rate),
        (rate_down, decay_rate),
        (rate_gains, 0.0),
        (rate_shifts, 0.0),
        (rate_query_bias, 0.0),
        (rate_up_bias, 0.0),
    )
    nexts = [
        adam_step(args[2 + n], moments[2 * n], moments[2 * n + 1], grads[n], *rates[n])
        for n in range(8)
    ]
    return (
        block_output,
        input_grad,
        *grads,
        *(n[0] for n in nexts),
        *(m for n in nexts for m in n[1:]),
    )


def solution(mesh):
    rows = P(("ctx", "tensor"), "dp", None)
    qkv = P(("dp", "ctx"), None, "tensor")
    mat = P(("dp", "ctx"), "tensor")
    norm = P(None, ("dp", "ctx"))
    qv = P(None, "tensor", ("dp", "ctx"))
    ub = P("tensor", ("dp", "ctx"))
    each = (qkv, mat, mat, mat, norm, norm, qv, ub)
    moments = tuple(s for s in each for _ in range(2))
    fused = (mesh.shape["dp"], mesh.shape["ctx"], mesh.shape["tensor"]) == (4, 4, 2)
    return jax.shard_map(
        functools.partial(body_fused if fused else body, Links(mesh)),
        mesh=mesh,
        in_specs=(rows, rows) + each + moments,
        out_specs=(rows, rows) + each + each + moments,
        check_vma=False,
    )
```

```python
import functools
import math

import jax
import jax.numpy as jnp
from jax import lax
from jax.experimental import pallas as pl
from jax.experimental.pallas import tpu as pltpu
from jax.sharding import PartitionSpec as P

HD = 64
STEP = 4
F32 = jnp.float32
BF = jnp.bfloat16

eps_norm = 1e-05
beta_one = 0.9
beta_two = 0.98
eps_adam = 1e-06
rate_qkv = 0.6
rate_proj = 1.2
rate_up = 0.1
rate_down = 0.15
rate_gains = 4.0
rate_shifts = 8.0
rate_query_bias = 20.0
rate_up_bias = 0.4
decay_rate = 0.01
root_half = 0.7071067811865476
density_scale = 0.3989422804014327
score_scale = HD ** (-0.5)
MIB = 2**20


def params(limit_mib):
    return pltpu.CompilerParams(vmem_limit_bytes=limit_mib * MIB)


def mm(a, b):
    return lax.dot_general(a, b, (((1,), (0,)), ((), ())), preferred_element_type=F32)


def mm_nt(a, b):
    return lax.dot_general(a, b, (((1,), (1,)), ((), ())), preferred_element_type=F32)


def row_mean(v):
    return jnp.mean(v, axis=-1, keepdims=True)


def normed_rows(v):
    center = v - row_mean(v)
    inv = lax.rsqrt(row_mean(center * center) + eps_norm)
    return center * inv, inv


def adam_step(current, moment_one, moment_two, gradient, rate_value, decay_value):
    one_next = beta_one * moment_one + (1.0 - beta_one) * gradient
    two_next = beta_two * moment_two + (1.0 - beta_two) * gradient * gradient
    step_ratio = (
        one_next / (1.0 - beta_one**STEP) / (jnp.sqrt(two_next / (1.0 - beta_two**STEP)) + eps_adam)
    )
    return (current - rate_value * (step_ratio + decay_value * current), one_next, two_next)


def qkv_kernel(own_ref, other_ref, w_ref, rows_ref, bias_ref, q_ref, kv_ref):
    gain, shift = rows_ref[0:1, :], rows_ref[1:2, :]
    bias_q, bias_v = bias_ref[0:1, :], bias_ref[1:2, :]
    half = own_ref.shape[0]
    width = q_ref.shape[1]
    for i, ref in enumerate((own_ref, other_ref)):
        normed, _ = normed_rows(ref[...].astype(F32))
        act = (normed * gain + shift).astype(BF)
        out = mm(act, w_ref[...])
        rows = pl.ds(i * half, half)
        q = (out[:, :width] + bias_q).astype(BF)
        q_ref[rows, :] = (q.astype(F32) * score_scale).astype(BF)
        kv_ref[rows, :width] = out[:, width : 2 * width].astype(BF)
        kv_ref[rows, width:] = (out[:, 2 * width :] + bias_v).astype(BF)


def qkv_call(own, other, weight, rows, bias):
    half, _ = own.shape
    width = weight.shape[1] // 3
    return pl.pallas_call(
        qkv_kernel,
        out_shape=(
            jax.ShapeDtypeStruct((2 * half, width), BF),
            jax.ShapeDtypeStruct((2 * half, 2 * width), BF),
        ),
        compiler_params=params(32),
        cost_estimate=pl.CostEstimate(
            flops=2 * 2 * half * weight.size, bytes_accessed=4 * MIB, transcendentals=0
        ),
        name="project_qkv",
    )(own, other, weight, rows, bias)


def head_mask(shape, h):
    lane = lax.broadcasted_iota(jnp.int32, shape, 1)
    return (lane >= HD) if h else (lane < HD)


def pick(v, h):
    return jnp.where(head_mask(v.shape, h), v, jnp.zeros_like(v))


def attend_kernel(q_ref, *refs):
    k_refs, v_refs = refs[0:4], refs[4:8]
    own_ref, send_ref, lse_ref, s_scr = refs[8:]
    half = own_ref.shape[0]
    q = q_ref[...]
    n = k_refs[0].shape[0]
    v_t = [r[...].T for r in v_refs]
    parts = []
    for h in range(2):
        qh = pick(q, h)
        tops = []
        for i in range(4):
            s = mm_nt(k_refs[i][...], qh)
            s_scr[h, pl.ds(i * n, n), :] = s
            tops.append(jnp.max(s, axis=0, keepdims=True))
        top = functools.reduce(jnp.maximum, tops)
        total = jnp.zeros_like(top)
        mix = jnp.zeros((HD, q.shape[0]), F32)
        for i in range(4):
            e = jnp.exp(s_scr[h, pl.ds(i * n, n), :] - top)
            total = total + jnp.sum(e, axis=0, keepdims=True)
            mix = mix + mm(v_t[i][h * HD : (h + 1) * HD, :], e.astype(BF))
        parts.append(mix / total)
        lse_ref[0, h : h + 1, :] = top + jnp.log(total)
    o = jnp.concatenate(parts, axis=0).T.astype(BF)
    own_ref[...] = o[:half]
    send_ref[...] = o[half:]


def attend_call(q, pieces):
    rows, width = q.shape
    pairs = width // 128
    n = pieces[0].shape[0]
    half = rows // 2
    k_spec = pl.BlockSpec((n, 128), lambda p: (0, p))
    v_spec = pl.BlockSpec((n, 128), lambda p: (0, p + pairs))
    return pl.pallas_call(
        attend_kernel,
        grid=(pairs,),
        in_specs=[pl.BlockSpec((rows, 128), lambda p: (0, p))] + [k_spec] * 4 + [v_spec] * 4,
        out_specs=[
            pl.BlockSpec((half, 128), lambda p: (0, p)),
            pl.BlockSpec((half, 128), lambda p: (0, p)),
            pl.BlockSpec((1, 2, rows), lambda p: (p, 0, 0)),
        ],
        out_shape=(
            jax.ShapeDtypeStruct((half, width), BF),
            jax.ShapeDtypeStruct((half, width), BF),
            jax.ShapeDtypeStruct((pairs, 2, rows), F32),
        ),
        scratch_shapes=[pltpu.VMEM((2, 4 * n, rows), F32)],
        compiler_params=params(40),
        cost_estimate=pl.CostEstimate(
            flops=16 * rows * 4 * n * width,
            bytes_accessed=4 * MIB,
            transcendentals=pairs * 2 * rows * 4 * n,
        ),
        name="attend",
    )(q, *pieces, *pieces)


def attend_back_kernel(*refs):
    q_ref, do_own_ref, do_got_ref, o_own_ref, o_send_ref, lse_ref = refs[:6]
    k_refs, v_refs = refs[6:10], refs[10:14]
    dq_ref = refs[14]
    dk_refs, dv_refs = refs[15:19], refs[19:23]
    q = q_ref[...]
    do = jnp.concatenate([do_own_ref[...], do_got_ref[...]], axis=0)
    o = jnp.concatenate([o_own_ref[...], o_send_ref[...]], axis=0)
    prod_t = (do.astype(F32) * o.astype(F32)).T
    q_heads = [pick(q, h) for h in range(2)]
    do_heads = [pick(do, h) for h in range(2)]
    deltas = [
        jnp.sum(prod_t[h * HD : (h + 1) * HD, :], axis=0, keepdims=True) for h in range(2)
    ]
    lses = [lse_ref[0, h : h + 1, :] for h in range(2)]
    dq_t = [jnp.zeros((HD, q.shape[0]), F32) for _ in range(2)]
    for i in range(4):
        k = k_refs[i][...]
        v = v_refs[i][...]
        k_t = k.T
        dk = jnp.zeros(k.shape, F32)
        dv = jnp.zeros(k.shape, F32)
        for h in range(2):
            p = jnp.exp(mm_nt(k, q_heads[h]) - lses[h])
            dv = dv + mm(p.astype(BF), do_heads[h])
            ds = (p * (mm_nt(v, do_heads[h]) - deltas[h])).astype(BF)
            dk = dk + mm(ds, q_heads[h])
            dq_t[h] = dq_t[h] + mm(k_t[h * HD : (h + 1) * HD, :], ds)
        dk_refs[i][...] = dk.astype(BF)
        dv_refs[i][...] = dv.astype(BF)
    dq_ref[...] = (jnp.concatenate(dq_t, axis=0).T * score_scale).astype(BF)


def attend_back_call(q, do_own, do_got, o_own, o_send, lse, pieces):
    rows, width = q.shape
    pairs = width // 128
    n = pieces[0].shape[0]
    half = rows // 2
    full = pl.BlockSpec((rows, 128), lambda p: (0, p))
    part = pl.BlockSpec((half, 128), lambda p: (0, p))
    k_spec = pl.BlockSpec((n, 128), lambda p: (0, p))
    v_spec = pl.BlockSpec((n, 128), lambda p: (0, p + pairs))
    out = pl.pallas_call(
        attend_back_kernel,
        grid=(pairs,),
        in_specs=[full, part, part, part, part, pl.BlockSpec((1, 2, rows), lambda p: (p, 0, 0))]
        + [k_spec] * 4
        + [v_spec] * 4,
        out_specs=[full] + [k_spec] * 8,
        out_shape=(jax.ShapeDtypeStruct((rows, width), BF),)
        + (jax.ShapeDtypeStruct((n, width), BF),) * 8,
        compiler_params=params(40),
        cost_estimate=pl.CostEstimate(
            flops=40 * rows * 4 * n * width,
            bytes_accessed=8 * MIB,
            transcendentals=pairs * 2 * rows * 4 * n,
        ),
        name="attend_back",
    )(q, do_own, do_got, o_own, o_send, lse, *pieces, *pieces)
    return out[0], out[1:5], out[5:9]


def ffn_kernel(clips, *refs):
    o_own, o_got = refs[0:clips], refs[clips : 2 * clips]
    x_ref, gy_ref, wo_ref, up_ref, dn_ref, b1_ref, rows_ref = refs[2 * clips : 2 * clips + 7]
    outs = refs[2 * clips + 7 :]
    y_ref, d1_ref = outs[0:2]
    do_own, do_send = outs[2 : 2 + clips], outs[2 + clips : 2 + 2 * clips]
    dup_ref, ddn_ref, dwo_ref, sums_ref, db1_ref = outs[2 + 2 * clips : 7 + 2 * clips]
    proj_scr, c_scr, ct_scr, gyt_scr, y_scr, dc_scr = outs[7 + 2 * clips :]
    half = o_own[0].shape[0]
    j = pl.program_id(0)
    gain, shift = rows_ref[0:1, :], rows_ref[1:2, :]
    bias_o, bias_2 = rows_ref[2:3, :], rows_ref[3:4, :]

    @pl.when(j == 0)
    def _():
        for i in range(clips):
            rows = pl.ds(i * half, half)
            proj = mm_nt(o_own[i][...], wo_ref[0]) + mm_nt(o_got[i][...], wo_ref[1]) + bias_o
            proj_scr[rows, :] = proj
            normed, _ = normed_rows(x_ref[rows, :].astype(F32) + proj)
            c_scr[rows, :] = (normed * gain + shift).astype(BF)
        ct_scr[...] = c_scr[...].T
        gyt_scr[...] = gy_ref[...].T
        y_scr[...] = jnp.zeros_like(y_scr)
        dc_scr[...] = jnp.zeros_like(dc_scr)

    up = up_ref[0]
    dn = dn_ref[0]
    f = mm(c_scr[...], up) + b1_ref[0]
    cdf = 0.5 * (1.0 + lax.erf(f * root_half))
    u = (f * cdf).astype(BF)
    slope = cdf + f * (density_scale * jnp.exp(-0.5 * f * f))
    df = mm(gy_ref[...], dn) * slope
    dfb = df.astype(BF)
    db1_ref[0] = jnp.sum(df, axis=0, keepdims=True)
    y_scr[...] += mm_nt(u, dn)
    dc_scr[...] += mm_nt(dfb, up)
    ddn_ref[0] = mm(gyt_scr[...], u).astype(BF)
    dup_ref[0] = mm(ct_scr[...], dfb).astype(BF)

    @pl.when(j == pl.num_programs(0) - 1)
    def _():
        sum_gain = jnp.zeros_like(gain)
        sum_dc = jnp.zeros_like(gain)
        sum_dh = jnp.zeros_like(gain)
        dwo0 = jnp.zeros(wo_ref.shape[1:], F32)
        dwo1 = jnp.zeros(wo_ref.shape[1:], F32)
        for i in range(clips):
            rows = pl.ds(i * half, half)
            proj = proj_scr[rows, :]
            normed, inv = normed_rows(x_ref[rows, :].astype(F32) + proj)
            y_ref[rows, :] = (proj + y_scr[rows, :] + bias_2).astype(BF)
            dc = dc_scr[rows, :]
            t = dc * gain
            d1 = inv * (t - row_mean(t) - normed * row_mean(t * normed))
            d1_ref[rows, :] = d1
            dh = gy_ref[rows, :].astype(F32) + d1
            dy = dh.astype(BF)
            sum_gain = sum_gain + jnp.sum(dc * normed, axis=0, keepdims=True)
            sum_dc = sum_dc + jnp.sum(dc, axis=0, keepdims=True)
            sum_dh = sum_dh + jnp.sum(dh, axis=0, keepdims=True)
            do_own[i][...] = mm(dy, wo_ref[0]).astype(BF)
            do_send[i][...] = mm(dy, wo_ref[1]).astype(BF)
            dy_t = dy.T
            dwo0 = dwo0 + mm(dy_t, o_own[i][...])
            dwo1 = dwo1 + mm(dy_t, o_got[i][...])
        dwo_ref[0] = dwo0.astype(BF)
        dwo_ref[1] = dwo1.astype(BF)
        sums_ref[0:1, :] = sum_gain
        sums_ref[1:2, :] = sum_dc
        sums_ref[2:3, :] = sum_dh
        sums_ref[3:8, :] = jnp.zeros((5, sums_ref.shape[1]), F32)


def ffn_call(o_own, o_got, x, gy, wide, b1, rows):
    clips = len(o_own)
    tokens, dim = x.shape
    half, width = o_own[0].shape
    hidden = b1.shape[1]
    block = 512
    per = hidden // block
    resident = lambda shape: pl.BlockSpec(
        shape, lambda j: (0,) * len(shape), pipeline_mode=pl.Buffered(1)
    )
    up_spec = pl.BlockSpec((1, dim, block), lambda j: (j // per, 0, j % per))
    out = pl.pallas_call(
        functools.partial(ffn_kernel, clips),
        grid=(2 * per,),
        in_specs=[resident((half, width))] * (2 * clips)
        + [
            resident((tokens, dim)),
            resident((tokens, dim)),
            pl.BlockSpec(
                (2, dim, width), lambda j: (0, 0, 2 * hidden // width), pipeline_mode=pl.Buffered(1)
            ),
            up_spec,
            pl.BlockSpec((1, dim, block), lambda j: (j // per, 0, j % per + per)),
            pl.BlockSpec((1, 1, block), lambda j: (j, 0, 0)),
            resident((8, dim)),
        ],
        out_specs=[resident((tokens, dim))] * 2
        + [resident((half, width))] * (2 * clips)
        + [
            up_spec,
            up_spec,
            resident((2, dim, width)),
            resident((8, dim)),
            pl.BlockSpec((1, 1, block), lambda j: (j, 0, 0)),
        ],
        out_shape=(
            jax.ShapeDtypeStruct((tokens, dim), BF),
            jax.ShapeDtypeStruct((tokens, dim), F32),
        )
        + (jax.ShapeDtypeStruct((half, width), BF),) * (2 * clips)
        + (
            jax.ShapeDtypeStruct((2, dim, hidden), BF),
            jax.ShapeDtypeStruct((2, dim, hidden), BF),
            jax.ShapeDtypeStruct((2, dim, width), BF),
            jax.ShapeDtypeStruct((8, dim), F32),
            jax.ShapeDtypeStruct((2 * per, 1, block), F32),
        ),
        scratch_shapes=[
            pltpu.VMEM((tokens, dim), F32),
            pltpu.VMEM((tokens, dim), BF),
            pltpu.VMEM((dim, tokens), BF),
            pltpu.VMEM((dim, tokens), BF),
            pltpu.VMEM((tokens, dim), F32),
            pltpu.VMEM((tokens, dim), F32),
        ],
        compiler_params=params(56),
        cost_estimate=pl.CostEstimate(
            flops=24 * tokens * dim * hidden, bytes_accessed=30 * MIB, transcendentals=0
        ),
        name="feed_forward",
    )(*o_own, *o_got, x, gy, wide, wide, wide, b1.reshape(2 * per, 1, block), rows)
    y, d1 = out[:2]
    do_own, do_send = out[2 : 2 + clips], out[2 + clips : 2 + 2 * clips]
    dup, ddn, dwo, sums, db1 = out[2 + 2 * clips :]
    return y, d1, do_own, do_send, dup, ddn, dwo, sums, db1.reshape(2, hidden)


def back_kernel(clips, *refs):
    own_refs, got_refs = refs[0:clips], refs[clips : 2 * clips]
    dq_refs = refs[2 * clips : 3 * clips]
    dk_refs = refs[3 * clips : 4 * clips]
    dv_refs = refs[4 * clips : 5 * clips]
    w_ref, rows_ref = refs[5 * clips : 5 * clips + 2]
    outs = refs[5 * clips + 2 :]
    da_own, da_send = outs[0:clips], outs[clips : 2 * clips]
    dw_ref, sums_ref, bias_ref = outs[2 * clips : 2 * clips + 3]
    acc_scr = outs[2 * clips + 3]
    half = own_refs[0].shape[0]
    width = dq_refs[0].shape[1]
    gain, shift = rows_ref[0:1, :], rows_ref[1:2, :]
    sum_gain = jnp.zeros_like(gain)
    sum_da = jnp.zeros_like(gain)
    sum_q = jnp.zeros((1, width), F32)
    sum_v = jnp.zeros((1, width), F32)
    for i in range(clips):
        for s, (x_ref, da_ref) in enumerate(((own_refs[i], da_own[i]), (got_refs[i], da_send[i]))):
            rows = pl.ds(s * half, half)
            normed, _ = normed_rows(x_ref[...].astype(F32))
            act = normed * gain + shift
            act_t = act.astype(BF).T
            da = jnp.zeros(act.shape, F32)
            for j, ref in enumerate((dq_refs[i], dk_refs[i], dv_refs[i])):
                g = ref[rows, :]
                cols = slice(j * width, (j + 1) * width)
                da = da + mm_nt(g, w_ref[:, cols])
                part = mm(act_t, g)
                if i == 0 and s == 0:
                    acc_scr[:, cols] = part
                else:
                    acc_scr[:, cols] += part
                if j == 0:
                    sum_q = sum_q + jnp.sum(g.astype(F32), axis=0, keepdims=True)
                if j == 2:
                    sum_v = sum_v + jnp.sum(g.astype(F32), axis=0, keepdims=True)
            da_ref[...] = da.astype(BF)
            sum_gain = sum_gain + jnp.sum(da * normed, axis=0, keepdims=True)
            sum_da = sum_da + jnp.sum(da, axis=0, keepdims=True)
    dw_ref[...] = acc_scr[...].astype(BF)
    sums_ref[0:1, :] = sum_gain
    sums_ref[1:2, :] = sum_da
    sums_ref[2:8, :] = jnp.zeros((6, sums_ref.shape[1]), F32)
    bias_ref[0:1, :] = sum_q
    bias_ref[1:2, :] = sum_v
    bias_ref[2:8, :] = jnp.zeros((6, width), F32)


def back_call(x_own, x_got, dq, dk, dv, weight, rows):
    clips = len(x_own)
    half, dim = x_own[0].shape
    width = dq[0].shape[1]
    out = pl.pallas_call(
        functools.partial(back_kernel, clips),
        out_shape=(jax.ShapeDtypeStruct((half, dim), BF),) * (2 * clips)
        + (
            jax.ShapeDtypeStruct(weight.shape, BF),
            jax.ShapeDtypeStruct((8, dim), F32),
            jax.ShapeDtypeStruct((8, width), F32),
        ),
        scratch_shapes=[pltpu.VMEM(weight.shape, F32)],
        compiler_params=params(48),
        cost_estimate=pl.CostEstimate(
            flops=8 * clips * half * weight.size, bytes_accessed=16 * MIB, transcendentals=0
        ),
        name="project_back",
    )(*x_own, *x_got, *dq, *dk, *dv, weight, rows)
    return out[:clips], out[clips : 2 * clips], out[2 * clips], out[2 * clips + 1], out[2 * clips + 2]


MESH_ID = pl.DeviceIdType.MESH


def flip(v, bit):
    step = 1 << bit
    return v + step - 2 * step * ((v // step) % 2)


def remote(src, dst, send, recv, device):
    return pltpu.make_async_remote_copy(
        src_ref=src, dst_ref=dst, send_sem=send, recv_sem=recv, device_id=device, device_id_type=MESH_ID
    )


def partners():
    d, c, t = lax.axis_index("dp"), lax.axis_index("ctx"), lax.axis_index("tensor")
    return d, c, t, {
        "x": (d, c, 1 - t),
        "z1": (d, flip(c, 0), t),
        "z2": (d, flip(c, 1), t),
        "core": (flip(d, 0), c, t),
        "y": (flip(d, 1), c, t),
        "swap": (flip(d, 0), flip(c, 1), t),
    }


def greet(devices):
    barrier = pltpu.get_barrier_semaphore()
    for device in devices:
        pl.semaphore_signal(barrier, inc=1, device_id=device, device_id_type=MESH_ID)
    pl.semaphore_wait(barrier, len(devices))


class Plan:
    def __init__(self, steps):
        self.steps = sorted(steps, key=lambda s: s[0])

    def pump(self, now):
        while self.steps and self.steps[0][0] <= now:
            self.steps.pop(0)[1]()


def pick_matrix(out_rows, per, shard):
    rows = shard * (out_rows // per)
    r = lax.broadcasted_iota(jnp.int32, (out_rows, rows), 0)
    k = lax.broadcasted_iota(jnp.int32, (out_rows, rows), 1)
    return jnp.where(k == (r // per) * shard + r % per, 1.0, 0.0).astype(BF)


def attend_pair(q, kvs, s_scr, between):
    n = kvs[0].shape[0]
    ks = [r.at[:, 0:128] for r in kvs]
    v_t = [r[:, 128:256].T for r in kvs]
    parts, lses = [], []
    for h in range(2):
        if h:
            between()
        qh = pick(q, h)
        tops = []
        for i in range(4):
            s = mm_nt(ks[i][...], qh)
            s_scr[h, pl.ds(i * n, n), :] = s
            tops.append(jnp.max(s, axis=0, keepdims=True))
        top = functools.reduce(jnp.maximum, tops)
        total = jnp.zeros_like(top)
        mix = jnp.zeros((HD, q.shape[0]), F32)
        for i in range(4):
            e = jnp.exp(s_scr[h, pl.ds(i * n, n), :] - top)
            total = total + jnp.sum(e, axis=0, keepdims=True)
            mix = mix + mm(v_t[i][h * HD : (h + 1) * HD, :], e.astype(BF))
        parts.append(mix / total)
        lses.append(top + jnp.log(total))
    return jnp.concatenate(parts, axis=0).T.astype(BF), jnp.concatenate(lses, axis=0)


Y_FIRST = (4, 5)
SWAPS_FIRST = (0,)
PROJECT_AT = {0: (0,), 2: (1,), 4: (2,)}
POINTS = {
    "s0": (3,),
    "f1": (3,),
    "f2": (3,),
    "z0": (6, 0, 6, 4),
    "w1": (0,),
    "c0": (4,),
    "p0": (6, 5, 2),
    "u0": (-1, 1),
    "u1": (-3, 3, 6, 5, 2),
    "c1": (1,),
    "p1": (0, -2, 3),
    "u2": (-4,),
    "c2": (1, 0, 6, 5),
    "u4": (4,),
    "u5": (2,),
    "u6": (0,),
    "u8": (1,),
    "g": (4,),
    "g0": (4, 5, 1, 2),
    "g2": (5, 0, 2),
}


def start_kernel(
    x_home,
    gy_home,
    first,
    second,
    x_ref,
    wf_ref,
    ws_ref,
    rows_ref,
    q_ref,
    kv_ref,
    own_ref,
    send_ref,
    lse_ref,
    y_ref,
    d1_ref,
    do_own,
    do_send,
    up_hbm,
    dn_hbm,
    dwo_ref,
    sums_ref,
    db1_ref,
    gy_ref,
    got_ref,
    s_scr,
    w_scr,
    wo_scr,
    g_scr,
    proj_scr,
    c_scr,
    ct_scr,
    gyt_scr,
    y_scr,
    dc_scr,
    b1_scr,
    local_sem,
    w_sem,
    g_sem,
    swap_s,
    swap_r,
    gy_s,
    gy_r,
    xe_s,
    xe_r,
    kv_s,
    kv_r,
    oe_s,
    oe_r,
    f_s,
    f_r,
    s_s,
    s_r,
):
    clips, half, dim = x_home.shape
    shard = first.shape[0]
    chunks = second.shape[0]
    width = q_ref.shape[2]
    pairs = width // 128
    d, c, t, dev = partners()
    me = pl.multiple_of((d * 4 + c) * shard, shard)
    me_z2 = pl.multiple_of((d * 4 + flip(c, 1)) * shard, shard)
    quad = pl.multiple_of(d * 4 * shard, 4 * shard)
    quad_y = pl.multiple_of(flip(d, 1) * 4 * shard, 4 * shard)
    moves = (d % 2) != (c // 2)
    greet([dev[k] for k in ("x", "z1", "z2", "core", "y", "swap")])

    place_f = pltpu.make_async_copy(first, wf_ref.at[pl.ds(me, shard)], local_sem.at[0])
    place_s = pltpu.make_async_copy(second, ws_ref.at[:, 0, pl.ds(me, shard)], local_sem.at[1])
    place_f.start()
    place_s.start()
    keep_x = pltpu.make_async_copy(x_home, x_ref.at[0], local_sem.at[2])
    keep_gy = pltpu.make_async_copy(gy_home, gy_ref, local_sem.at[3])

    swaps = [
        remote(x_home.at[i], x_ref.at[0, i], swap_s.at[i], swap_r.at[i], dev["swap"])
        for i in range(clips)
    ]
    swap_gy = remote(gy_home, gy_ref, gy_s.at[0], gy_r.at[0], dev["swap"])

    def first_stage(i, src, rows, count, device):
        block = wf_ref.at[pl.ds(rows, count)]
        return remote(src if src is not None else block, block, f_s.at[i], f_r.at[i], device)

    f_stages = [
        [first_stage(0, first, me, shard, dev["z2"])],
        [first_stage(1, None, me, shard, dev["z1"]), first_stage(2, None, me_z2, shard, dev["z1"])],
        [first_stage(3, None, quad, 4 * shard, dev["y"])],
        [
            first_stage(4, None, quad, 4 * shard, dev["core"]),
            first_stage(5, None, quad_y, 4 * shard, dev["core"]),
        ],
    ]

    def second_stages(ch):
        def own(i, src, rows, count, device):
            block = ws_ref.at[ch, 0, pl.ds(rows, count)]
            return remote(src if src is not None else block, block, s_s.at[ch, i], s_r.at[ch, i], device)

        def both(i, rows, device):
            block = ws_ref.at[ch, :, pl.ds(rows, 4 * shard)]
            return remote(block, block, s_s.at[ch, i], s_r.at[ch, i], device)

        def over_x(i, rows):
            rows = pl.ds(rows, 4 * shard)
            return remote(
                ws_ref.at[ch, 0, rows], ws_ref.at[ch, 1, rows], s_s.at[ch, i], s_r.at[ch, i], dev["x"]
            )

        along_z = [
            [own(0, second.at[ch], me, shard, dev["z2"])],
            [own(1, None, me, shard, dev["z1"]), own(2, None, me_z2, shard, dev["z1"])],
        ]
        if ch in Y_FIRST:
            plane = [[own(4, None, quad, 4 * shard, dev["y"])], [over_x(3, quad), over_x(7, quad_y)]]
        else:
            plane = [[over_x(3, quad)], [both(4, quad, dev["y"])]]
        return along_z + plane + [[both(5, quad, dev["core"]), both(6, quad_y, dev["core"])]]

    def start(copies):
        for cp in copies:
            cp.start()

    def wait(copies):
        for cp in copies:
            cp.wait()

    s_stages = [second_stages(ch) for ch in range(chunks)]
    reached = [-1] * chunks

    def advance(point):
        for ch in POINTS.get(point, ()):
            if ch < 0:
                special[ch]()
                continue
            if reached[ch] >= len(s_stages[ch]):
                continue
            if reached[ch] >= 0:
                wait(s_stages[ch][reached[ch]])
            reached[ch] += 1
            if reached[ch] < len(s_stages[ch]):
                start(s_stages[ch][reached[ch]])
    def row_copy(j, i, src, dst, device):
        return remote(x_ref.at[src, i], x_ref.at[dst, i], xe_s.at[j, i], xe_r.at[j, i], device)

    own_x = [row_copy(0, i, 0, 1, dev["x"]) for i in range(clips)]
    own_z = [row_copy(1, i, 0, 2, dev["z1"]) for i in range(clips)]
    far_x = [row_copy(2, i, 2, 3, dev["x"]) for i in range(clips)]

    def swap_start(clip_list):
        @pl.when(moves)
        def _():
            for i in clip_list:
                swaps[i].start()

    def swap_done(i):
        @pl.when(moves)
        def _():
            swaps[i].wait()

        own_z[i].start()
        own_x[i].start()

    def far_start(i):
        own_z[i].wait()
        far_x[i].start()

    def gy_start():
        @pl.when(moves)
        def _():
            swap_gy.start()

    special = {
        -1: functools.partial(far_start, 1),
        -2: functools.partial(far_start, 2),
        -3: functools.partial(swap_done, 2),
        -4: gy_start,
    }

    start(f_stages[0])
    swap_start(SWAPS_FIRST)

    @pl.when(jnp.logical_not(moves))
    def _():
        keep_x.start()
        keep_gy.start()
        keep_x.wait()
        keep_gy.wait()

    place_f.wait()
    place_s.wait()
    advance("s0")
    wait(f_stages[0])
    start(f_stages[1])
    advance("f1")
    wait(f_stages[1])
    start(f_stages[2])
    swap_start([i for i in range(clips) if i not in SWAPS_FIRST])
    advance("f2")
    swap_done(0)
    advance("w0")
    wait(f_stages[2])
    start(f_stages[3])
    advance("f3")
    far_start(0)
    advance("z0")
    swap_done(1)
    advance("w1")
    wait(f_stages[3])
    advance("f4")

    extra = wf_ref[:, 3 * width : 3 * width + 128]
    rows_t = extra.astype(F32).T
    rows_ref[0:8, :] = rows_t[0:8, :]
    shards = dim // shard
    qv = mm(pick_matrix(HD, HD // shards, shard), extra).T
    biases = []
    for r in range(2):
        biases.append(
            jnp.concatenate(
                [qv[8 + r * 2 * pairs + h : 9 + r * 2 * pairs + h, :] for h in range(2 * pairs)], axis=1
            )
        )
    gain, shift = rows_t[0:1, :], rows_t[2:3, :]

    def project(i, s):
        normed, _ = normed_rows(x_ref[s, i].astype(F32))
        act = (normed * gain + shift).astype(BF)
        rows = pl.ds((s % 2) * half, half)
        if s < 2:
            out = mm(act, wf_ref[:, : 3 * width])
            q = (out[:, :width] + biases[0]).astype(BF)
            q_ref[i, rows, :] = (q.astype(F32) * score_scale).astype(BF)
            out = out[:, width:]
        else:
            out = mm(act, wf_ref[:, width : 3 * width])
        v = out[:, width:] + biases[1]
        for p in range(pairs):
            cols = slice(p * 128, (p + 1) * 128)
            kv_ref[s // 2 * 2, i, p, rows, 0:128] = out[:, cols].astype(BF)
            kv_ref[s // 2 * 2, i, p, rows, 128:256] = v[:, cols].astype(BF)

    def kv_copy(j, i):
        return remote(
            kv_ref.at[2 * j, i], kv_ref.at[2 * j + 1, i], kv_s.at[j, i], kv_r.at[j, i], dev["core"]
        )

    units = [(i, p) for i in range(clips) for p in range(pairs)]
    to_core = [[kv_copy(j, i) for j in range(2)] for i in range(clips)]

    o_copies = [
        remote(send_ref.at[i], got_ref.at[i], oe_s.at[i], oe_r.at[i], dev["x"]) for i in range(clips)
    ]

    def project_clip(i):
        project(i, 0)
        own_x[i].wait()
        project(i, 1)
        to_core[i][0].start()
        advance(f"c{i}")
        project(i, 2)
        far_x[i].wait()
        project(i, 3)
        to_core[i][1].start()
        advance(f"p{i}")

    for n, (i, p) in enumerate(units):
        for clip in PROJECT_AT.get(n, ()):
            project_clip(clip)
        if p == 0:
            wait(to_core[i])
        cols = pl.ds(p * 128, 128)
        o, lse = attend_pair(
            q_ref[i, :, cols],
            [kv_ref.at[s, i, p] for s in range(4)],
            s_scr,
            lambda: None,
        )
        own_ref[i, :, cols] = o[:half]
        send_ref[i, :, cols] = o[half:]
        lse_ref[i, p] = lse
        advance(f"u{n}")
        if p == pairs - 1:
            o_copies[i].start()

    per = (chunks - 1) // 2
    block = ws_ref.shape[3]
    tokens = clips * half
    gain, shift = rows_ref[1:2, :], rows_ref[3:4, :]
    bias_o, bias_2 = rows_ref[4:5, :], rows_ref[5:6, :]

    def finish_chunk(ch):
        while reached[ch] < len(s_stages[ch]):
            if reached[ch] >= 0:
                wait(s_stages[ch][reached[ch]])
            reached[ch] += 1
            if reached[ch] < len(s_stages[ch]):
                start(s_stages[ch][reached[ch]])

    @pl.when(moves)
    def _():
        swap_gy.wait()

    gyt_scr[...] = gy_ref[...].reshape(tokens, dim).T
    finish_chunk(2 * per)
    load_wo = pltpu.make_async_copy(ws_ref.at[2 * per], wo_scr, local_sem.at[1])
    load_wo.start()
    load_wo.wait()
    taken = pick_matrix(128, 128 // shards, shard)
    for s in range(2):
        cols = mm(taken, wo_scr[s, :, width : width + 128]).T
        for b in range(per):
            b1_scr[s * per + b] = jnp.concatenate(
                [cols[b * 4 + r : b * 4 + r + 1, :] for r in range(4)], axis=1
            )
    for i in range(clips):
        rows = pl.ds(i * half, half)
        wait([o_copies[i]])
        proj = (
            mm_nt(own_ref[i], wo_scr[0, :, :width])
            + mm_nt(got_ref[i], wo_scr[1, :, :width])
            + bias_o
        )
        proj_scr[rows, :] = proj
        normed, _ = normed_rows(x_ref[0, i].astype(F32) + proj)
        c_scr[rows, :] = (normed * gain + shift).astype(BF)
    ct_scr[...] = c_scr[...].T
    advance("g")

    def load_block(b, s, r):
        return pltpu.make_async_copy(ws_ref.at[r * per + b, s], w_scr.at[s, r], w_sem.at[s, r])

    def store_block(b, s, r):
        out = dn_hbm if r else up_hbm
        return pltpu.make_async_copy(g_scr.at[s, r], out.at[b, s], g_sem.at[s, r])

    for b in range(per):
        finish_chunk(b)
        finish_chunk(per + b)
        for s in range(2):
            start([load_block(b, s, r) for r in range(2)])
        for s in range(2):
            wait([load_block(b, s, r) for r in range(2)])
            up, dn = w_scr[s, 0], w_scr[s, 1]
            f = mm(c_scr[...], up) + b1_scr[s * per + b]
            cdf = 0.5 * (1.0 + lax.erf(f * root_half))
            u = (f * cdf).astype(BF)
            slope = cdf + f * (density_scale * jnp.exp(-0.5 * f * f))
            df = mm(gy_ref[...].reshape(tokens, dim), dn) * slope
            dfb = df.astype(BF)
            db1_ref[s * per + b] = jnp.sum(df, axis=0, keepdims=True)
            if b + s:
                y_scr[...] += mm_nt(u, dn)
                dc_scr[...] += mm_nt(dfb, up)
            else:
                y_scr[...] = mm_nt(u, dn)
                dc_scr[...] = mm_nt(dfb, up)
            if b:
                wait([store_block(b - 1, s, r) for r in range(2)])
            g_scr[s, 0] = mm(ct_scr[...], dfb).astype(BF)
            g_scr[s, 1] = mm(gyt_scr[...], u).astype(BF)
            start([store_block(b, s, r) for r in range(2)])
            advance(f"g{2 * b + s}")

    sum_gain = jnp.zeros((1, dim), F32)
    sum_dc = jnp.zeros((1, dim), F32)
    sum_dh = jnp.zeros((1, dim), F32)
    sum_gy = jnp.zeros((1, dim), F32)
    dwo = [jnp.zeros((dim, width), F32) for _ in range(2)]
    for i in range(clips):
        rows = pl.ds(i * half, half)
        proj = proj_scr[rows, :]
        normed, inv = normed_rows(x_ref[0, i].astype(F32) + proj)
        y_ref[i] = (proj + y_scr[rows, :] + bias_2).astype(BF)
        dc = dc_scr[rows, :]
        t_rows = dc * gain
        d1 = inv * (t_rows - row_mean(t_rows) - normed * row_mean(t_rows * normed))
        d1_ref[rows, :] = d1
        gy_rows = gy_ref[i].astype(F32)
        dh = gy_rows + d1
        dy = dh.astype(BF)
        sum_gain = sum_gain + jnp.sum(dc * normed, axis=0, keepdims=True)
        sum_dc = sum_dc + jnp.sum(dc, axis=0, keepdims=True)
        sum_dh = sum_dh + jnp.sum(dh, axis=0, keepdims=True)
        sum_gy = sum_gy + jnp.sum(gy_rows, axis=0, keepdims=True)
        do_own[i] = mm(dy, wo_scr[0, :, :width]).astype(BF)
        do_send[i] = mm(dy, wo_scr[1, :, :width]).astype(BF)
        dy_t = dy.T
        dwo = [dwo[0] + mm(dy_t, own_ref[i]), dwo[1] + mm(dy_t, got_ref[i])]
    for s in range(2):
        dwo_ref[s, :, :width] = dwo[s].astype(BF)
    dwo_ref[:, :, width:] = jnp.zeros((2, dim, block - width), BF)
    for r, row in enumerate((sum_gain, sum_dc, sum_dh, sum_gy)):
        sums_ref[r : r + 1, :] = row
    sums_ref[4:8, :] = jnp.zeros((4, dim), F32)
    for s in range(2):
        wait([store_block(per - 1, s, r) for r in range(2)])


def start_call(x_home, gy_home, first, second):
    clips, half, dim = x_home.shape
    shard = first.shape[0]
    width = (first.shape[1] - 128) // 3
    chunks, _, block = second.shape
    per = (chunks - 1) // 2
    pairs = width // 128
    tokens = clips * half
    any_spec = pl.BlockSpec(memory_space=pl.ANY)
    vmem = pl.BlockSpec(memory_space=pltpu.VMEM)
    dma = pltpu.SemaphoreType.DMA
    both = lambda *shape: [dma(shape), dma(shape)]
    shaped = jax.ShapeDtypeStruct
    head = shaped((clips, half, width), BF)
    return pl.pallas_call(
        start_kernel,
        in_specs=[vmem] * 4,
        out_specs=[vmem, vmem, any_spec] + [vmem] * 10 + [any_spec] * 2 + [vmem] * 3,
        out_shape=(
            shaped((4, clips, half, dim), BF),
            shaped((dim, first.shape[1]), BF),
            shaped((chunks, 2, dim, block), BF),
            shaped((8, dim), F32),
            shaped((clips, 2 * half, width), BF),
            shaped((4, clips, pairs, 2 * half, 256), BF),
            head,
            head,
            shaped((clips, pairs, 2, 2 * half), F32),
            shaped((clips, half, dim), BF),
            shaped((tokens, dim), F32),
            head,
            head,
            shaped((per, 2, dim, block), BF),
            shaped((per, 2, dim, block), BF),
            shaped((2, dim, block), BF),
            shaped((8, dim), F32),
            shaped((2 * per, 1, block), F32),
        ),
        scratch_shapes=[
            pltpu.VMEM((clips, half, dim), BF),
            pltpu.VMEM((clips, half, width), BF),
            pltpu.VMEM((2, 8 * half, 2 * half), F32),
            pltpu.VMEM((2, 2, dim, block), BF),
            pltpu.VMEM((2, dim, block), BF),
            pltpu.VMEM((2, 2, dim, block), BF),
            pltpu.VMEM((tokens, dim), F32),
            pltpu.VMEM((tokens, dim), BF),
            pltpu.VMEM((dim, tokens), BF),
            pltpu.VMEM((dim, tokens), BF),
            pltpu.VMEM((tokens, dim), F32),
            pltpu.VMEM((tokens, dim), F32),
            pltpu.VMEM((2 * per, 1, block), F32),
            dma((4,)),
            dma((2, 2)),
            dma((2, 2)),
            *both(clips),
            *both(1),
            *both(3, clips),
            *both(2, clips),
            *both(clips),
            *both(6),
            *both(chunks, 8),
        ],
        compiler_params=pltpu.CompilerParams(
            collective_id=1, has_side_effects=True, vmem_limit_bytes=60 * MIB
        ),
        cost_estimate=pl.CostEstimate(
            flops=30 * 10**9, bytes_accessed=80 * MIB, transcendentals=11 * 10**6
        ),
        name="start_attend",
    )(x_home, gy_home, first, second)


X_FIRST = (4, 6)
ORDER = (
    ("g", 4), ("g", 3), ("g", 1), ("g", 5), ("g", 4), ("g", 2), ("g", 3), ("g", 0),
    ("g", 6), ("u", 0), ("g", 2), ("u", 2), ("g", 6), ("y", 0), ("g", 5), ("u", 1),
    ("g", 3), ("u", 3), ("b", 0), ("g", 5), ("g", 4), ("u", 5), ("f", 0), ("u", 4),
    ("g", 3), ("g", 6), ("g", 0), ("g", 4), ("b", 1), ("g", 5), ("e", 0), ("g", 1),
    ("g", 2), ("f", 1), ("u", 6), ("g", 0), ("u", 8), ("g", 4), ("e", 1), ("g", 6),
    ("u", 7), ("g", 0), ("g", 1), ("g", 3), ("g", 5), ("g", 2), ("b", 2), ("g", 1),
    ("h", 0), ("g", 6), ("g", 0), ("g", 4), ("f", 2), ("g", 2), ("g", 1), ("h", 0),
    ("g", 3), ("v", 0), ("g", 5), ("v", 0), ("e", 2), ("h", 0), ("v", 0), ("v", 0),
    ("g", 6), ("g", 2), ("h", 0), ("v", 0), ("g", 0), ("g", 1), ("h", 0), ("v", 0),
)


def end_kernel(
    q_ref,
    kv_hbm,
    own_ref,
    send_ref,
    lse_ref,
    do_own_ref,
    do_send_ref,
    x_hbm,
    wf_hbm,
    rows_ref,
    d1_hbm,
    y_ref,
    up_hbm,
    dn_hbm,
    wo_hbm,
    sums_ref,
    db1_ref,
    yh_ref,
    dh_ref,
    g2_ref,
    g1_ref,
    vec_ref,
    kv_scr,
    x_scr,
    wf_scr,
    d1_scr,
    do_got,
    core_got,
    dq_scr,
    acc_scr,
    dw_scr,
    da_own,
    da_send,
    da_got,
    far_scr,
    far_got,
    delta_scr,
    loc_scr,
    rc_scr,
    ry_scr,
    rx_scr,
    rz1_scr,
    rz2_scr,
    c1_scr,
    y1_scr,
    p1_scr,
    q1_scr,
    vs_scr,
    vr_scr,
    kv_sem,
    in_sem,
    loc_sem,
    keep_sem,
    do_s,
    do_r,
    y_s,
    y_r,
    dc_s,
    dc_r,
    da_s,
    da_r,
    fz_s,
    fz_r,
    sw_s,
    sw_r,
    h_s,
    h_r,
    g_s,
    g_r,
    v_s,
    v_r,
):
    clips, half, width = own_ref.shape
    pairs = width // 128
    dim = rows_ref.shape[1]
    shard = g1_ref.shape[0]
    chunks = g2_ref.shape[0]
    per = (chunks - 1) // 2
    rows4 = 4 * shard
    d, c, t, dev = partners()
    moves = (d % 2) != (c // 2)
    greet([dev[k] for k in ("x", "z1", "z2", "core", "y", "swap")])

    def start(copies):
        for cp in copies:
            cp.start()

    def wait(copies):
        for cp in copies:
            cp.wait()

    units = [(i, p) for i in range(clips) for p in range(pairs)]
    do_copies = [
        remote(do_send_ref.at[i], do_got.at[i], do_s.at[i], do_r.at[i], dev["x"]) for i in range(clips)
    ]
    start(do_copies)
    loads = [
        pltpu.make_async_copy(
            kv_hbm.at[:, i, p], kv_scr.at[:, i, p], kv_sem.at[i, p]
        )
        for i, p in units
    ]
    start(loads)
    late = [
        pltpu.make_async_copy(x_hbm, x_scr, in_sem.at[0]),
        pltpu.make_async_copy(wf_hbm, wf_scr, in_sem.at[1]),
        pltpu.make_async_copy(d1_hbm, d1_scr, in_sem.at[2]),
    ]
    start(late)
    y_swap = remote(y_ref, yh_ref, y_s.at[0], y_r.at[0], dev["swap"])
    y_keep = pltpu.make_async_copy(y_ref, yh_ref, keep_sem.at[0])

    def y_start():
        @pl.when(moves)
        def _():
            y_swap.start()

        @pl.when(jnp.logical_not(moves))
        def _():
            y_keep.start()

    def grad(ch):
        if ch < per:
            return up_hbm.at[ch]
        if ch < 2 * per:
            return dn_hbm.at[ch - per]
        return wo_hbm

    def band(block):
        return pl.ds(pl.multiple_of(block * rows4, rows4), rows4)

    def strip(block):
        return pl.ds(pl.multiple_of(block * shard, shard), shard)

    mine = [d, flip(d, 1)]
    theirs = [flip(d, 0), flip(flip(d, 0), 1)]

    def g_copy(ch, k, src, dst, device):
        return remote(src, dst, g_s.at[ch, k], g_r.at[ch, k], device)

    def g_stages(ch):
        return [
            [
                g_copy(ch, k, grad(ch).at[:, band(theirs[k])], rc_scr.at[ch, k], dev["core"])
                for k in range(2)
            ],
            [
                g_copy(ch, 2, rc_scr.at[ch, 0, 1], ry_scr.at[ch, 0], dev["x"]),
                g_copy(ch, 7, rc_scr.at[ch, 1, 1], ry_scr.at[ch, 1], dev["x"]),
            ]
            if ch in X_FIRST
            else [g_copy(ch, 2, rc_scr.at[ch, 1], ry_scr.at[ch], dev["y"])],
            [g_copy(ch, 3, ry_scr.at[ch, 1], rx_scr.at[ch], dev["y" if ch in X_FIRST else "x"])],
            [
                g_copy(ch, 4, rx_scr.at[ch, strip(flip(c, 0))], rz1_scr.at[ch, 0], dev["z1"]),
                g_copy(
                    ch, 5, rx_scr.at[ch, strip(flip(flip(c, 0), 1))], rz1_scr.at[ch, 1], dev["z1"]
                ),
            ],
            [g_copy(ch, 6, rz1_scr.at[ch, 1], rz2_scr.at[ch], dev["z2"])],
        ]

    stages = [g_stages(ch) for ch in range(chunks)]
    seen = [ch for kind, ch in ORDER if kind == "g"]
    firsts = [n for n, ch in enumerate(seen) if seen[:n].count(ch) == 1]
    turns = [seen[n] for n in firsts]

    def own_loads(ch):
        slot = turns.index(ch) % 2
        return [
            pltpu.make_async_copy(
                grad(ch).at[:, band(mine[k])], loc_scr.at[slot, k], loc_sem.at[slot, k]
            )
            for k in range(2)
        ]

    reached = [-1] * chunks

    def g_step(ch):
        k = reached[ch]
        if k >= 0:
            wait(stages[ch][k])
        if k == 0:
            turn = turns.index(ch)
            wait(own_loads(ch))
            for m in range(2):
                rc_scr[ch, m] = rc_scr[ch, m] + loc_scr[turn % 2, m]
            if turn + 2 < chunks:
                start(own_loads(turns[turn + 2]))
        elif k == 1:
            if ch in X_FIRST:
                for m in range(2):
                    ry_scr[ch, m] = ry_scr[ch, m] + rc_scr[ch, m, 0]
            else:
                ry_scr[ch] = ry_scr[ch] + rc_scr[ch, 0]
        elif k == 2:
            rx_scr[ch] = rx_scr[ch] + ry_scr[ch, 0]
        elif k == 3:
            rz1_scr[ch, 0] = rz1_scr[ch, 0] + rx_scr[ch, strip(c)]
            rz1_scr[ch, 1] = rz1_scr[ch, 1] + rx_scr[ch, strip(flip(c, 1))]
        elif k == 4:
            g2_ref[ch] = rz1_scr[ch, 0].astype(F32) + rz2_scr[ch].astype(F32)
        if k + 1 < len(stages[ch]):
            start(stages[ch][k + 1])
        reached[ch] = k + 1

    start(own_loads(turns[0]))
    start(own_loads(turns[1]))

    def dkv_copies(u):
        i, p = u
        return [
            remote(
                kv_scr.at[2 * m + 1, i, p],
                core_got.at[m, i, p],
                dc_s.at[m, i, p],
                dc_r.at[m, i, p],
                dev["core"],
            )
            for m in range(2)
        ]

    to_core = [dkv_copies(u) for u in units]

    do_here = []

    def attention(n):
        i, p = units[n]
        cols = pl.ds(p * 128, 128)
        if i not in do_here:
            do_here.append(i)
            do_copies[i].wait()
        loads[n].wait()
        q = q_ref[i, :, cols]
        do = jnp.concatenate([do_own_ref[i, :, cols], do_got[i, :, cols]], axis=0)
        o = jnp.concatenate([own_ref[i, :, cols], send_ref[i, :, cols]], axis=0)
        prod_t = (do.astype(F32) * o.astype(F32)).T
        q_heads = [pick(q, h) for h in range(2)]
        do_heads = [pick(do, h) for h in range(2)]
        deltas = [
            jnp.sum(prod_t[h * HD : (h + 1) * HD, :], axis=0, keepdims=True) for h in range(2)
        ]
        lses = [lse_ref[i, p, h : h + 1, :] for h in range(2)]
        dq_t = [jnp.zeros((HD, q.shape[0]), F32) for _ in range(2)]
        for s in range(4):
            k = kv_scr[s, i, p, :, 0:128]
            v = kv_scr[s, i, p, :, 128:256]
            k_t = k.T
            dk = jnp.zeros(k.shape, F32)
            dv = jnp.zeros(k.shape, F32)
            for h in range(2):
                prob = jnp.exp(mm_nt(k, q_heads[h]) - lses[h])
                dv = dv + mm(prob.astype(BF), do_heads[h])
                ds = (prob * (mm_nt(v, do_heads[h]) - deltas[h])).astype(BF)
                dk = dk + mm(ds, q_heads[h])
                dq_t[h] = dq_t[h] + mm(k_t[h * HD : (h + 1) * HD, :], ds)
            kv_scr[s, i, p, :, 0:128] = dk.astype(BF)
            kv_scr[s, i, p, :, 128:256] = dv.astype(BF)
        dq_scr[i, :, cols] = (jnp.concatenate(dq_t, axis=0).T * score_scale).astype(BF)
        start(to_core[n])

    gain, shift = rows_ref[0:1, :], rows_ref[2:3, :]
    sums = {
        "gain": jnp.zeros((1, dim), F32),
        "da": jnp.zeros((1, dim), F32),
        "q": jnp.zeros((1, width), F32),
        "v": jnp.zeros((1, width), F32),
    }
    def da_x(i, j):
        return remote(da_send.at[i, j], da_got.at[i, j], da_s.at[i, j], da_r.at[i, j], dev["x"])

    da_xs = [[da_x(i, j) for j in range(2)] for i in range(clips)]
    da_zs = [remote(far_scr.at[i], far_got.at[i], fz_s.at[i], fz_r.at[i], dev["z1"]) for i in range(clips)]

    def project_back(i):
        if i == 0:
            wait(late)
        for n, u in enumerate(units):
            if u[0] == i:
                wait(to_core[n])
        for s in (3, 1, 2, 0):
            m = s // 2
            rows = pl.ds((s % 2) * half, half)
            normed, _ = normed_rows(x_scr[s, i].astype(F32))
            act_t = (normed * gain + shift).astype(BF).T
            halves = [
                kv_scr[2 * m, i, p, rows, :] + core_got[m, i, p, rows, :] for p in range(pairs)
            ]
            g = jnp.concatenate(
                ([] if m else [dq_scr[i, rows, :]])
                + [v[:, :128] for v in halves]
                + [v[:, 128:] for v in halves],
                axis=1,
            )
            cols = slice(width, 3 * width) if m else slice(0, 3 * width)
            da = mm_nt(g, wf_scr[:, cols])
            part = mm(act_t, g)
            if i == 0 and s == 3:
                acc_scr[:, :width] = jnp.zeros((dim, width), F32)
                acc_scr[:, width:] = part
            else:
                acc_scr[:, cols] += part
            total = jnp.sum(g.astype(F32), axis=0, keepdims=True)
            if m == 0:
                sums["q"] = sums["q"] + total[:, :width]
            sums["v"] = sums["v"] + total[:, total.shape[1] - width :]
            sums["gain"] = sums["gain"] + jnp.sum(da * normed, axis=0, keepdims=True)
            sums["da"] = sums["da"] + jnp.sum(da, axis=0, keepdims=True)
            if s % 2:
                da_send[i, m] = da.astype(BF)
                da_xs[i][m].start()
            elif m:
                far_scr[i] = da.astype(BF)
            else:
                da_own[i] = da

    def far_back(i):
        da_xs[i][1].wait()
        far_scr[i] = far_scr[i] + da_got[i, 1]
        da_zs[i].start()

    swaps = [
        remote(delta_scr.at[i], dh_ref.at[i], sw_s.at[i], sw_r.at[i], dev["swap"]) for i in range(clips)
    ]
    keeps = [
        pltpu.make_async_copy(delta_scr.at[i], dh_ref.at[i], keep_sem.at[1 + i]) for i in range(clips)
    ]

    def finish(i):
        da_xs[i][0].wait()
        da_zs[i].wait()
        da = da_own[i] + da_got[i, 0].astype(F32) + far_got[i].astype(F32)
        w = da * gain
        normed, inv = normed_rows(x_scr[0, i].astype(F32))
        rows = pl.ds(i * half, half)
        delta_scr[i] = (
            d1_scr[rows, :] + inv * (w - row_mean(w) - normed * row_mean(w * normed))
        ).astype(BF)

        @pl.when(moves)
        def _():
            swaps[i].start()

        @pl.when(jnp.logical_not(moves))
        def _():
            keeps[i].start()

    def h_copy(k, src, dst, device):
        return remote(src, dst, h_s.at[k], h_r.at[k], device)

    h_stages = [
        [h_copy(k, dw_scr.at[band(theirs[k])], c1_scr.at[k], dev["core"]) for k in range(2)],
        [h_copy(2, c1_scr.at[1], y1_scr, dev["y"])],
        [
            h_copy(3, y1_scr.at[strip(flip(c, 0))], p1_scr.at[0], dev["z1"]),
            h_copy(4, y1_scr.at[strip(flip(flip(c, 0), 1))], p1_scr.at[1], dev["z1"]),
        ],
        [h_copy(5, p1_scr.at[1], q1_scr, dev["z2"])],
    ]
    h_reached = [-1]

    def h_step():
        k = h_reached[0]
        if k < 0:
            dw_scr[...] = acc_scr[...].astype(BF)
        else:
            wait(h_stages[k])
        if k == 0:
            for m in range(2):
                c1_scr[m] = c1_scr[m] + dw_scr[band(mine[m]), :]
        elif k == 1:
            y1_scr[...] = y1_scr[...] + c1_scr[0]
        elif k == 2:
            p1_scr[0] = p1_scr[0] + y1_scr[strip(c), :]
            p1_scr[1] = p1_scr[1] + y1_scr[strip(flip(c, 1)), :]
        elif k == 3:
            g1_ref[...] = p1_scr[0].astype(F32) + q1_scr[...].astype(F32)
        if k + 1 < len(h_stages):
            start(h_stages[k + 1])
        h_reached[0] = k + 1

    def small_sums():
        zero = jnp.zeros((1, dim), F32)
        shared = [
            sums["gain"],
            sums_ref[0:1, :],
            sums["da"],
            sums_ref[1:2, :],
            sums_ref[2:3, :],
            sums_ref[3:4, :],
        ]
        ub = [
            jnp.concatenate([db1_ref[s * per + b] for b in range(per)], axis=1) for s in range(2)
        ]
        for r, row in enumerate(shared):
            vs_scr[0, r : r + 1, :] = row
            vs_scr[1, r : r + 1, :] = row
        vs_scr[0, 6:7, :] = jnp.concatenate([sums["q"], sums["v"]], axis=1)
        vs_scr[1, 6:7, :] = zero
        vs_scr[0, 7:8, :] = zero
        vs_scr[1, 7:8, :] = zero
        vs_scr[0, 10:16, :] = jnp.zeros((6, dim), F32)
        vs_scr[1, 10:16, :] = jnp.zeros((6, dim), F32)
        for s in range(2):
            vs_scr[s, 8:9, :] = ub[s][:, :dim]
            vs_scr[s, 9:10, :] = ub[s][:, dim:]
    v_devices = ("x", "core", "y", "z1", "z2")

    def v_copy(k):
        src = vs_scr.at[1] if k == 0 else vs_scr.at[0] if k == 1 else vr_scr.at[k - 1]
        return remote(src, vr_scr.at[k], v_s.at[k], v_r.at[k], dev[v_devices[k]])

    v_copies = [v_copy(k) for k in range(len(v_devices))]

    v_reached = [-1]

    def v_step():
        k = v_reached[0]
        if k < 0:
            small_sums()
        else:
            v_copies[k].wait()
        if k == 0:
            vs_scr[0] = vs_scr[0] + vr_scr[0]
        elif k == 1:
            vr_scr[1] = vr_scr[1] + vs_scr[0]
        elif k > 1:
            vr_scr[k] = vr_scr[k] + vr_scr[k - 1]
        if k + 1 < len(v_devices):
            v_copies[k + 1].start()
        else:
            vec_ref[...] = vr_scr[k]
        v_reached[0] = k + 1

    steps = {
        "y": lambda n: y_start(),
        "u": attention,
        "b": project_back,
        "f": far_back,
        "e": finish,
        "g": g_step,
        "h": lambda n: h_step(),
        "v": lambda n: v_step(),
    }
    for kind, n in ORDER:
        steps[kind](n)

    @pl.when(moves)
    def _():
        y_swap.wait()
        wait(swaps)

    @pl.when(jnp.logical_not(moves))
    def _():
        y_keep.wait()
        wait(keeps)


def end_call(q, kv, own, send, lse, do_own, do_send, x, wf, rows, d1, y, up, dn, wo, sums, db1):
    clips, half, width = own.shape
    pairs = width // 128
    dim = rows.shape[1]
    shard = dim // 16
    per, _, _, block = up.shape
    chunks = 2 * per + 1
    any_spec = pl.BlockSpec(memory_space=pl.ANY)
    vmem = pl.BlockSpec(memory_space=pltpu.VMEM)
    dma = pltpu.SemaphoreType.DMA
    rows4 = 4 * shard
    both = lambda *shape: [dma(shape), dma(shape)]
    return pl.pallas_call(
        end_kernel,
        in_specs=[vmem, any_spec, vmem, vmem, vmem, vmem, vmem, any_spec, any_spec, vmem]
        + [any_spec, vmem]
        + [any_spec] * 3
        + [vmem, vmem],
        out_specs=[any_spec, any_spec, vmem, vmem, vmem],
        out_shape=(
            jax.ShapeDtypeStruct((clips, half, dim), BF),
            jax.ShapeDtypeStruct((clips, half, dim), BF),
            jax.ShapeDtypeStruct((chunks, shard, block), F32),
            jax.ShapeDtypeStruct((shard, 3 * width), F32),
            jax.ShapeDtypeStruct((16, dim), F32),
        ),
        scratch_shapes=[
            pltpu.VMEM(kv.shape, BF),
            pltpu.VMEM(x.shape, BF),
            pltpu.VMEM(wf.shape, BF),
            pltpu.VMEM(d1.shape, F32),
            pltpu.VMEM(do_send.shape, BF),
            pltpu.VMEM((2, clips, pairs, 2 * half, 256), BF),
            pltpu.VMEM(q.shape, BF),
            pltpu.VMEM((dim, 3 * width), F32),
            pltpu.VMEM((dim, 3 * width), BF),
            pltpu.VMEM((clips, half, dim), F32),
            pltpu.VMEM((clips, 2, half, dim), BF),
            pltpu.VMEM((clips, 2, half, dim), BF),
            pltpu.VMEM((clips, half, dim), BF),
            pltpu.VMEM((clips, half, dim), BF),
            pltpu.VMEM((clips, half, dim), BF),
            pltpu.VMEM((2, 2, 2, rows4, block), BF),
            pltpu.VMEM((chunks, 2, 2, rows4, block), BF),
            pltpu.VMEM((chunks, 2, rows4, block), BF),
            pltpu.VMEM((chunks, rows4, block), BF),
            pltpu.VMEM((chunks, 2, shard, block), BF),
            pltpu.VMEM((chunks, shard, block), BF),
            pltpu.VMEM((2, rows4, 3 * width), BF),
            pltpu.VMEM((rows4, 3 * width), BF),
            pltpu.VMEM((2, shard, 3 * width), BF),
            pltpu.VMEM((shard, 3 * width), BF),
            pltpu.VMEM((2, 16, dim), F32),
            pltpu.VMEM((5, 16, dim), F32),
            dma((clips, pairs)),
            dma((3,)),
            dma((2, 2)),
            dma((1 + clips,)),
            *both(clips),
            *both(1),
            *both(2, clips, pairs),
            *both(clips, 2),
            *both(clips),
            *both(clips),
            *both(6),
            *both(chunks, 8),
            *both(5),
        ],
        compiler_params=pltpu.CompilerParams(
            collective_id=2, has_side_effects=True, vmem_limit_bytes=62 * MIB
        ),
        cost_estimate=pl.CostEstimate(
            flops=20 * 10**9, bytes_accessed=40 * MIB, transcendentals=11 * 10**6
        ),
        name="attend_back_end",
    )(q, kv, own, send, lse, do_own, do_send, x, wf, rows, d1, y, up, dn, wo, sums, db1)


class Links:
    def __init__(self, mesh):
        self.dp = mesh.shape["dp"]
        self.ctx = mesh.shape["ctx"]
        self.tensor = mesh.shape["tensor"]
        self.dp_bits = self.dp.bit_length() - 1
        self.ctx_bits = self.ctx.bit_length() - 1

    def flat(self, d, c, t):
        return (d * self.ctx + c) * self.tensor + t

    def move(self, value, partner):
        pairs = []
        for d in range(self.dp):
            for c in range(self.ctx):
                for t in range(self.tensor):
                    other = partner(d, c, t)
                    if other != (d, c, t):
                        pairs.append((self.flat(d, c, t), self.flat(*other)))
        return lax.ppermute(value, ("dp", "ctx", "tensor"), pairs)

    def across_x(self, value):
        return self.move(value, lambda d, c, t: (d, c, t ^ 1))

    def across_core(self, value):
        return self.move(value, lambda d, c, t: (d ^ 1, c, t))

    def across_z(self, value):
        return self.move(value, lambda d, c, t: (d, c ^ 1, t))

    def stays(self):
        d, c = lax.axis_index("dp"), lax.axis_index("ctx")
        return (d % 2) == (c // (self.ctx // 2))

    def swap(self, value):
        half = self.ctx // 2
        moved = self.move(
            value,
            lambda d, c, t: (d, c, t) if d % 2 == c // half else (d ^ 1, c ^ half, t),
        )
        return jnp.where(self.stays(), value, moved)

    def stages(self):
        out = []
        for bit in reversed(range(self.ctx_bits)):
            out.append(("ctx", bit, self.ctx_bits - 1 - bit))
        for bit in reversed(range(self.dp_bits)):
            out.append(("dp", bit, self.dp_bits - 1 - bit))
        return out

    def step(self, value, axis, bit):
        if axis == "ctx":
            return self.move(value, lambda d, c, t: (d, c ^ (1 << bit), t))
        return self.move(value, lambda d, c, t: (d ^ (1 << bit), c, t))

    def side(self, axis, bit):
        return (lax.axis_index(axis) // (1 << bit)) % 2

    def gather(self, value, both):
        shape = value.shape
        lead = 0
        for axis, bit, place in self.stages():
            if axis == "dp" and both and not lead:
                value = jnp.stack([value, self.across_x(value)])
                lead = 1
            got = self.step(value, axis, bit)
            low = self.side(axis, bit) == 0
            value = jnp.stack(
                [jnp.where(low, value, got), jnp.where(low, got, value)], axis=lead + place
            )
        shards = self.dp * self.ctx
        return value.reshape((2,) * lead + (shards * shape[0],) + shape[1:])

    def scatter(self, value, both):
        lead = 1 if both else 0
        rest = value.shape[lead + 1 :]
        value = value.reshape(
            value.shape[:lead] + (2,) * (self.dp_bits + self.ctx_bits) + rest
        )
        for axis, bit, place in reversed(self.stages()):
            if axis == "ctx" and lead:
                value = value[0] + self.across_x(value[1])
                lead = 0
            side = self.side(axis, bit)
            keep = lax.dynamic_index_in_dim(value, side, lead + place, keepdims=False)
            give = lax.dynamic_index_in_dim(value, 1 - side, lead + place, keepdims=False)
            value = keep + self.step(give, axis, bit)
        return value


def body(links, *args):
    (
        block_input,
        out_cotangent,
        qkv_weight,
        proj_weight,
        up_weight,
        down_weight,
        norm_gains,
        shift_terms,
        qv_bias,
        up_bias,
        qkv_first,
        qkv_second,
        proj_first,
        proj_second,
        up_first,
        up_second,
        down_first,
        down_second,
        gains_first,
        gains_second,
        shifts_first,
        shifts_second,
        qv_bias_first,
        qv_bias_second,
        up_bias_first,
        up_bias_second,
    ) = args
    half, clips, dim = block_input.shape
    shard = qkv_weight.shape[0]
    shards = dim // shard
    width = qkv_weight.shape[2]
    hidden = up_weight.shape[1]
    heads = width // HD

    x_home = jnp.transpose(block_input, (1, 0, 2)).astype(BF)
    gy_home = jnp.transpose(out_cotangent, (1, 0, 2)).astype(BF)
    x = links.swap(x_home)
    x_own = [x[i] for i in range(clips)]
    x_got = [links.across_x(v) for v in x_own]

    def lanes(parts):
        flat = jnp.concatenate([p.astype(BF).reshape(-1) for p in parts])
        return jnp.pad(flat, (0, shard * 128 - flat.size)).reshape(shard, 128)

    first = jnp.concatenate(
        [qkv_weight.reshape(shard, 3 * width).astype(BF), lanes([norm_gains, shift_terms, qv_bias])],
        axis=1,
    )
    second = jnp.concatenate(
        [up_weight.astype(BF), down_weight.astype(BF), proj_weight.astype(BF), lanes([up_bias])],
        axis=1,
    )
    first = links.gather(first, False)
    second = links.gather(second, True)
    w_qkv = first[:, : 3 * width]
    small = first[:, 3 * width :].reshape(shards, shard * 128)
    n_g, n_s = 2 * shard, 4 * shard
    gains = jnp.transpose(small[:, :n_g].reshape(shards, 2, shard), (1, 0, 2)).reshape(2, dim)
    shifts = jnp.transpose(
        small[:, n_g : n_g + n_s].reshape(shards, 4, shard), (1, 0, 2)
    ).reshape(4, dim)
    qv_cols = qv_bias.shape[2]
    biases = jnp.transpose(
        small[:, n_g + n_s : n_g + n_s + qv_bias.size].reshape(shards, 2, heads, qv_cols),
        (1, 2, 0, 3),
    ).reshape(2, width)
    ub_rows, ub_cols = up_bias.shape
    b1 = jnp.transpose(
        second[:, :, 2 * hidden + width :]
        .reshape(2, shards, shard * 128)[:, :, : up_bias.size]
        .reshape(2, shards, ub_rows, ub_cols),
        (0, 2, 1, 3),
    ).reshape(2, hidden)
    gains, shifts, biases, b1 = (v.astype(F32) for v in (gains, shifts, biases, b1))
    zero4 = jnp.zeros((4, dim), F32)
    rows_one = jnp.concatenate([gains[0:1], shifts[0:1], zero4, zero4[:2]])
    rows_two = jnp.concatenate([gains[1:2], shifts[1:4], zero4])
    biases = jnp.concatenate([biases, jnp.zeros((6, width), F32)])

    q, pieces, o_own, o_send, o_got, lse = [], [], [], [], [], []
    for i in range(clips):
        q_i, kv = qkv_call(x_own[i], x_got[i], w_qkv, rows_one, biases)
        kv_z = links.across_z(kv)
        kv_c = links.across_core(kv)
        kv_d = links.across_core(kv_z)
        q.append(q_i)
        pieces.append((kv, kv_c, kv_z, kv_d))
    gy = links.swap(gy_home)
    for i in range(clips):
        own, send, lse_i = attend_call(q[i], pieces[i])
        o_own.append(own)
        o_send.append(send)
        o_got.append(links.across_x(send))
        lse.append(lse_i)

    tokens = clips * half
    y, d1, do_own, do_send, d_up, d_down, d_proj, sums_two, d_b1 = ffn_call(
        o_own, o_got, x.reshape(tokens, dim), gy.reshape(tokens, dim), second, b1, rows_two
    )
    y_home = links.swap(y.reshape(clips, half, dim))
    block_output = block_input + jnp.transpose(y_home, (1, 0, 2)).astype(F32)

    grads_two = jnp.concatenate([d_up, d_down, d_proj], axis=2)
    grads_two = links.scatter(grads_two.reshape(2, shards, shard, -1), True)

    dq, dk, dv = [], [], []
    do_got = [links.across_x(v) for v in do_send]
    for i in range(clips):
        dq_i, dks, dvs = attend_back_call(
            q[i], do_own[i], do_got[i], o_own[i], o_send[i], lse[i], pieces[i]
        )
        dq.append(dq_i)
        for parts, out in ((dks, dk), (dvs, dv)):
            mine, core, z, diag = parts
            mine = mine + links.across_core(core)
            z = z + links.across_core(diag)
            out.append(mine + links.across_z(z))
    da_own, da_send, d_qkv, sums_one, sums_bias = back_call(
        x_own, x_got, dq, dk, dv, w_qkv, rows_one
    )
    grads_one = links.scatter(d_qkv.reshape(shards, shard, 3 * width), False)
    d1 = d1.reshape(clips, half, dim)
    deltas = []
    for i in range(clips):
        da = da_own[i].astype(F32) + links.across_x(da_send[i]).astype(F32)
        normed, inv = normed_rows(x_own[i].astype(F32))
        w = da * gains[0]
        deltas.append(
            (d1[i] + inv * (w - row_mean(w) - normed * row_mean(w * normed))).astype(BF)
        )
    delta_home = links.swap(jnp.stack(deltas))
    input_grad = out_cotangent + jnp.transpose(delta_home, (1, 0, 2)).astype(F32)

    cot_sum = jnp.sum(out_cotangent, axis=(0, 1))[None]
    both = jnp.concatenate(
        [sums_one[0:1], sums_two[0:1], sums_one[1:2], sums_two[1:2], sums_two[2:3], cot_sum]
    )
    both = jnp.transpose(both.reshape(6, shards, shard), (1, 0, 2)).reshape(shards, 6 * shard)
    ub = jnp.transpose(d_b1.reshape(2, ub_rows, shards, ub_cols), (0, 2, 1, 3)).reshape(
        2, shards, up_bias.size
    )
    crossed = links.across_x(jnp.concatenate([both, ub[1]], axis=1))
    qv = jnp.transpose(
        sums_bias[0:2].reshape(2, heads, shards, qv_cols), (2, 0, 1, 3)
    ).reshape(shards, qv_bias.size)
    vec = jnp.concatenate([jnp.concatenate([both, ub[0]], axis=1) + crossed, qv], axis=1)
    vec = links.scatter(vec, False)
    gains_grad = vec[:n_g].reshape(2, shard)
    shifts_grad = vec[n_g : n_g + n_s].reshape(4, shard)
    up_bias_grad = vec[6 * shard : 6 * shard + up_bias.size].reshape(up_bias.shape)
    qv_bias_grad = vec[6 * shard + up_bias.size :].reshape(qv_bias.shape)

    qkv_grad = grads_one.astype(F32).reshape(qkv_weight.shape)
    grads_two = grads_two.astype(F32)
    up_grad = grads_two[:, :hidden]
    down_grad = grads_two[:, hidden : 2 * hidden]
    proj_grad = grads_two[:, 2 * hidden :]

    qkv_next = adam_step(qkv_weight, qkv_first, qkv_second, qkv_grad, rate_qkv, decay_rate)
    proj_next = adam_step(proj_weight, proj_first, proj_second, proj_grad, rate_proj, decay_rate)
    up_next = adam_step(up_weight, up_first, up_second, up_grad, rate_up, decay_rate)
    down_next = adam_step(down_weight, down_first, down_second, down_grad, rate_down, decay_rate)
    gains_next = adam_step(norm_gains, gains_first, gains_second, gains_grad, rate_gains, 0.0)
    shifts_next = adam_step(shift_terms, shifts_first, shifts_second, shifts_grad, rate_shifts, 0.0)
    qv_next = adam_step(qv_bias, qv_bias_first, qv_bias_second, qv_bias_grad, rate_query_bias, 0.0)
    ub_next = adam_step(up_bias, up_bias_first, up_bias_second, up_bias_grad, rate_up_bias, 0.0)
    nexts = (qkv_next, proj_next, up_next, down_next, gains_next, shifts_next, qv_next, ub_next)
    return (
        block_output,
        input_grad,
        qkv_grad,
        proj_grad,
        up_grad,
        down_grad,
        gains_grad,
        shifts_grad,
        qv_bias_grad,
        up_bias_grad,
        *(n[0] for n in nexts),
        *(m for n in nexts for m in n[1:]),
    )


def body_fused(links, *args):
    (
        block_input,
        out_cotangent,
        qkv_weight,
        proj_weight,
        up_weight,
        down_weight,
        norm_gains,
        shift_terms,
        qv_bias,
        up_bias,
        *moments,
    ) = args
    half, clips, dim = block_input.shape
    shard = qkv_weight.shape[0]
    width = qkv_weight.shape[2]
    hidden = up_weight.shape[1]
    heads = width // HD
    block = 512
    per = hidden // block
    me = lax.axis_index("dp") * lax.axis_size("ctx") + lax.axis_index("ctx")

    x_home = jnp.transpose(block_input, (1, 0, 2)).astype(BF)
    gy_home = jnp.transpose(out_cotangent, (1, 0, 2)).astype(BF)

    def columns(v):
        return jnp.pad(v.T, ((0, shard - v.shape[1]), (0, 0)))

    first = jnp.concatenate(
        [
            qkv_weight.reshape(shard, 3 * width),
            columns(norm_gains),
            columns(shift_terms),
            jnp.zeros((shard, 2), F32),
            columns(qv_bias.reshape(2 * heads, -1)),
            jnp.zeros((shard, 120 - 2 * heads), F32),
        ],
        axis=1,
    ).astype(BF)
    last = jnp.concatenate(
        [
            proj_weight,
            columns(up_bias),
            jnp.zeros((shard, block - width - up_bias.shape[0]), F32),
        ],
        axis=1,
    )
    second = jnp.stack(
        [w[:, b * block : (b + 1) * block] for w in (up_weight, down_weight) for b in range(per)] + [last]
    ).astype(BF)
    x, wf, _, rows, q, kv, own, send, lse, y, d1, do_own, do_send, up, dn, wo, sums, db1 = start_call(
        x_home, gy_home, first, second
    )
    y_home, delta_home, g2, g1, vec = end_call(
        q,
        kv,
        own,
        send,
        lse,
        do_own,
        do_send,
        x,
        wf,
        rows,
        d1,
        y,
        up,
        dn,
        wo,
        sums,
        db1,
    )
    block_output = block_input + jnp.transpose(y_home, (1, 0, 2)).astype(F32)
    input_grad = out_cotangent + jnp.transpose(delta_home, (1, 0, 2)).astype(F32)

    qkv_grad = g1.reshape(qkv_weight.shape)
    up_grad = jnp.concatenate([g2[b] for b in range(per)], axis=1)
    down_grad = jnp.concatenate([g2[per + b] for b in range(per)], axis=1)
    proj_grad = g2[2 * per, :, :width]
    cols = lax.dynamic_slice_in_dim(vec[0:6], me * shard, shard, 1)
    gains_grad, shifts_grad = cols[0:2], cols[2:6]
    qv_cols = qv_bias.shape[2]
    qv_bias_grad = lax.dynamic_slice_in_dim(
        vec[6].reshape(2, heads, HD), me * qv_cols, qv_cols, 2
    )
    ub_cols = up_bias.shape[1]
    up_bias_grad = lax.dynamic_slice_in_dim(
        vec[8:10].reshape(up_bias.shape[0], 128), me * ub_cols, ub_cols, 1
    )
    grads = (
        qkv_grad,
        proj_grad,
        up_grad,
        down_grad,
        gains_grad,
        shifts_grad,
        qv_bias_grad,
        up_bias_grad,
    )
    rates = (
        (rate_qkv, decay_rate),
        (rate_proj, decay_rate),
        (rate_up, decay_rate),
        (rate_down, decay_rate),
        (rate_gains, 0.0),
        (rate_shifts, 0.0),
        (rate_query_bias, 0.0),
        (rate_up_bias, 0.0),
    )
    nexts = [
        adam_step(args[2 + n], moments[2 * n], moments[2 * n + 1], grads[n], *rates[n])
        for n in range(8)
    ]
    return (
        block_output,
        input_grad,
        *grads,
        *(n[0] for n in nexts),
        *(m for n in nexts for m in n[1:]),
    )


def solution(mesh):
    rows = P(("ctx", "tensor"), "dp", None)
    qkv = P(("dp", "ctx"), None, "tensor")
    mat = P(("dp", "ctx"), "tensor")
    norm = P(None, ("dp", "ctx"))
    qv = P(None, "tensor", ("dp", "ctx"))
    ub = P("tensor", ("dp", "ctx"))
    each = (qkv, mat, mat, mat, norm, norm, qv, ub)
    moments = tuple(s for s in each for _ in range(2))
    fused = (mesh.shape["dp"], mesh.shape["ctx"], mesh.shape["tensor"]) == (4, 4, 2)
    return jax.shard_map(
        functools.partial(body_fused if fused else body, Links(mesh)),
        mesh=mesh,
        in_specs=(rows, rows) + each + moments,
        out_specs=(rows, rows) + each + each + moments,
        check_vma=False,
    )
```

```python
import functools
import math

import jax
import jax.numpy as jnp
from jax import lax
from jax.experimental import pallas as pl
from jax.experimental.pallas import tpu as pltpu
from jax.sharding import PartitionSpec as P

HD = 64
STEP = 4
F32 = jnp.float32
BF = jnp.bfloat16

eps_norm = 1e-05
beta_one = 0.9
beta_two = 0.98
eps_adam = 1e-06
rate_qkv = 0.6
rate_proj = 1.2
rate_up = 0.1
rate_down = 0.15
rate_gains = 4.0
rate_shifts = 8.0
rate_query_bias = 20.0
rate_up_bias = 0.4
decay_rate = 0.01
root_half = 0.7071067811865476
density_scale = 0.3989422804014327
score_scale = HD ** (-0.5)
MIB = 2**20


def params(limit_mib):
    return pltpu.CompilerParams(vmem_limit_bytes=limit_mib * MIB)


def mm(a, b):
    return lax.dot_general(a, b, (((1,), (0,)), ((), ())), preferred_element_type=F32)


def mm_nt(a, b):
    return lax.dot_general(a, b, (((1,), (1,)), ((), ())), preferred_element_type=F32)


def row_mean(v):
    return jnp.mean(v, axis=-1, keepdims=True)


def normed_rows(v):
    center = v - row_mean(v)
    inv = lax.rsqrt(row_mean(center * center) + eps_norm)
    return center * inv, inv


def adam_step(current, moment_one, moment_two, gradient, rate_value, decay_value):
    one_next = beta_one * moment_one + (1.0 - beta_one) * gradient
    two_next = beta_two * moment_two + (1.0 - beta_two) * gradient * gradient
    step_ratio = (
        one_next / (1.0 - beta_one**STEP) / (jnp.sqrt(two_next / (1.0 - beta_two**STEP)) + eps_adam)
    )
    return (current - rate_value * (step_ratio + decay_value * current), one_next, two_next)


def qkv_kernel(own_ref, other_ref, w_ref, rows_ref, bias_ref, q_ref, kv_ref):
    gain, shift = rows_ref[0:1, :], rows_ref[1:2, :]
    bias_q, bias_v = bias_ref[0:1, :], bias_ref[1:2, :]
    half = own_ref.shape[0]
    width = q_ref.shape[1]
    for i, ref in enumerate((own_ref, other_ref)):
        normed, _ = normed_rows(ref[...].astype(F32))
        act = (normed * gain + shift).astype(BF)
        out = mm(act, w_ref[...])
        rows = pl.ds(i * half, half)
        q = (out[:, :width] + bias_q).astype(BF)
        q_ref[rows, :] = (q.astype(F32) * score_scale).astype(BF)
        kv_ref[rows, :width] = out[:, width : 2 * width].astype(BF)
        kv_ref[rows, width:] = (out[:, 2 * width :] + bias_v).astype(BF)


def qkv_call(own, other, weight, rows, bias):
    half, _ = own.shape
    width = weight.shape[1] // 3
    return pl.pallas_call(
        qkv_kernel,
        out_shape=(
            jax.ShapeDtypeStruct((2 * half, width), BF),
            jax.ShapeDtypeStruct((2 * half, 2 * width), BF),
        ),
        compiler_params=params(32),
        cost_estimate=pl.CostEstimate(
            flops=2 * 2 * half * weight.size, bytes_accessed=4 * MIB, transcendentals=0
        ),
        name="project_qkv",
    )(own, other, weight, rows, bias)


def head_mask(shape, h):
    lane = lax.broadcasted_iota(jnp.int32, shape, 1)
    return (lane >= HD) if h else (lane < HD)


def pick(v, h):
    return jnp.where(head_mask(v.shape, h), v, jnp.zeros_like(v))


def attend_kernel(q_ref, *refs):
    k_refs, v_refs = refs[0:4], refs[4:8]
    own_ref, send_ref, lse_ref, s_scr = refs[8:]
    half = own_ref.shape[0]
    q = q_ref[...]
    n = k_refs[0].shape[0]
    v_t = [r[...].T for r in v_refs]
    parts = []
    for h in range(2):
        qh = pick(q, h)
        tops = []
        for i in range(4):
            s = mm_nt(k_refs[i][...], qh)
            s_scr[h, pl.ds(i * n, n), :] = s
            tops.append(jnp.max(s, axis=0, keepdims=True))
        top = functools.reduce(jnp.maximum, tops)
        total = jnp.zeros_like(top)
        mix = jnp.zeros((HD, q.shape[0]), F32)
        for i in range(4):
            e = jnp.exp(s_scr[h, pl.ds(i * n, n), :] - top)
            total = total + jnp.sum(e, axis=0, keepdims=True)
            mix = mix + mm(v_t[i][h * HD : (h + 1) * HD, :], e.astype(BF))
        parts.append(mix / total)
        lse_ref[0, h : h + 1, :] = top + jnp.log(total)
    o = jnp.concatenate(parts, axis=0).T.astype(BF)
    own_ref[...] = o[:half]
    send_ref[...] = o[half:]


def attend_call(q, pieces):
    rows, width = q.shape
    pairs = width // 128
    n = pieces[0].shape[0]
    half = rows // 2
    k_spec = pl.BlockSpec((n, 128), lambda p: (0, p))
    v_spec = pl.BlockSpec((n, 128), lambda p: (0, p + pairs))
    return pl.pallas_call(
        attend_kernel,
        grid=(pairs,),
        in_specs=[pl.BlockSpec((rows, 128), lambda p: (0, p))] + [k_spec] * 4 + [v_spec] * 4,
        out_specs=[
            pl.BlockSpec((half, 128), lambda p: (0, p)),
            pl.BlockSpec((half, 128), lambda p: (0, p)),
            pl.BlockSpec((1, 2, rows), lambda p: (p, 0, 0)),
        ],
        out_shape=(
            jax.ShapeDtypeStruct((half, width), BF),
            jax.ShapeDtypeStruct((half, width), BF),
            jax.ShapeDtypeStruct((pairs, 2, rows), F32),
        ),
        scratch_shapes=[pltpu.VMEM((2, 4 * n, rows), F32)],
        compiler_params=params(40),
        cost_estimate=pl.CostEstimate(
            flops=16 * rows * 4 * n * width,
            bytes_accessed=4 * MIB,
            transcendentals=pairs * 2 * rows * 4 * n,
        ),
        name="attend",
    )(q, *pieces, *pieces)


def attend_back_kernel(*refs):
    q_ref, do_own_ref, do_got_ref, o_own_ref, o_send_ref, lse_ref = refs[:6]
    k_refs, v_refs = refs[6:10], refs[10:14]
    dq_ref = refs[14]
    dk_refs, dv_refs = refs[15:19], refs[19:23]
    q = q_ref[...]
    do = jnp.concatenate([do_own_ref[...], do_got_ref[...]], axis=0)
    o = jnp.concatenate([o_own_ref[...], o_send_ref[...]], axis=0)
    prod_t = (do.astype(F32) * o.astype(F32)).T
    q_heads = [pick(q, h) for h in range(2)]
    do_heads = [pick(do, h) for h in range(2)]
    deltas = [
        jnp.sum(prod_t[h * HD : (h + 1) * HD, :], axis=0, keepdims=True) for h in range(2)
    ]
    lses = [lse_ref[0, h : h + 1, :] for h in range(2)]
    dq_t = [jnp.zeros((HD, q.shape[0]), F32) for _ in range(2)]
    for i in range(4):
        k = k_refs[i][...]
        v = v_refs[i][...]
        k_t = k.T
        dk = jnp.zeros(k.shape, F32)
        dv = jnp.zeros(k.shape, F32)
        for h in range(2):
            p = jnp.exp(mm_nt(k, q_heads[h]) - lses[h])
            dv = dv + mm(p.astype(BF), do_heads[h])
            ds = (p * (mm_nt(v, do_heads[h]) - deltas[h])).astype(BF)
            dk = dk + mm(ds, q_heads[h])
            dq_t[h] = dq_t[h] + mm(k_t[h * HD : (h + 1) * HD, :], ds)
        dk_refs[i][...] = dk.astype(BF)
        dv_refs[i][...] = dv.astype(BF)
    dq_ref[...] = (jnp.concatenate(dq_t, axis=0).T * score_scale).astype(BF)


def attend_back_call(q, do_own, do_got, o_own, o_send, lse, pieces):
    rows, width = q.shape
    pairs = width // 128
    n = pieces[0].shape[0]
    half = rows // 2
    full = pl.BlockSpec((rows, 128), lambda p: (0, p))
    part = pl.BlockSpec((half, 128), lambda p: (0, p))
    k_spec = pl.BlockSpec((n, 128), lambda p: (0, p))
    v_spec = pl.BlockSpec((n, 128), lambda p: (0, p + pairs))
    out = pl.pallas_call(
        attend_back_kernel,
        grid=(pairs,),
        in_specs=[full, part, part, part, part, pl.BlockSpec((1, 2, rows), lambda p: (p, 0, 0))]
        + [k_spec] * 4
        + [v_spec] * 4,
        out_specs=[full] + [k_spec] * 8,
        out_shape=(jax.ShapeDtypeStruct((rows, width), BF),)
        + (jax.ShapeDtypeStruct((n, width), BF),) * 8,
        compiler_params=params(40),
        cost_estimate=pl.CostEstimate(
            flops=40 * rows * 4 * n * width,
            bytes_accessed=8 * MIB,
            transcendentals=pairs * 2 * rows * 4 * n,
        ),
        name="attend_back",
    )(q, do_own, do_got, o_own, o_send, lse, *pieces, *pieces)
    return out[0], out[1:5], out[5:9]


def ffn_kernel(clips, *refs):
    o_own, o_got = refs[0:clips], refs[clips : 2 * clips]
    x_ref, gy_ref, wo_ref, up_ref, dn_ref, b1_ref, rows_ref = refs[2 * clips : 2 * clips + 7]
    outs = refs[2 * clips + 7 :]
    y_ref, d1_ref = outs[0:2]
    do_own, do_send = outs[2 : 2 + clips], outs[2 + clips : 2 + 2 * clips]
    dup_ref, ddn_ref, dwo_ref, sums_ref, db1_ref = outs[2 + 2 * clips : 7 + 2 * clips]
    proj_scr, c_scr, ct_scr, gyt_scr, y_scr, dc_scr = outs[7 + 2 * clips :]
    half = o_own[0].shape[0]
    j = pl.program_id(0)
    gain, shift = rows_ref[0:1, :], rows_ref[1:2, :]
    bias_o, bias_2 = rows_ref[2:3, :], rows_ref[3:4, :]

    @pl.when(j == 0)
    def _():
        for i in range(clips):
            rows = pl.ds(i * half, half)
            proj = mm_nt(o_own[i][...], wo_ref[0]) + mm_nt(o_got[i][...], wo_ref[1]) + bias_o
            proj_scr[rows, :] = proj
            normed, _ = normed_rows(x_ref[rows, :].astype(F32) + proj)
            c_scr[rows, :] = (normed * gain + shift).astype(BF)
        ct_scr[...] = c_scr[...].T
        gyt_scr[...] = gy_ref[...].T
        y_scr[...] = jnp.zeros_like(y_scr)
        dc_scr[...] = jnp.zeros_like(dc_scr)

    up = up_ref[0]
    dn = dn_ref[0]
    f = mm(c_scr[...], up) + b1_ref[0]
    cdf = 0.5 * (1.0 + lax.erf(f * root_half))
    u = (f * cdf).astype(BF)
    slope = cdf + f * (density_scale * jnp.exp(-0.5 * f * f))
    df = mm(gy_ref[...], dn) * slope
    dfb = df.astype(BF)
    db1_ref[0] = jnp.sum(df, axis=0, keepdims=True)
    y_scr[...] += mm_nt(u, dn)
    dc_scr[...] += mm_nt(dfb, up)
    ddn_ref[0] = mm(gyt_scr[...], u).astype(BF)
    dup_ref[0] = mm(ct_scr[...], dfb).astype(BF)

    @pl.when(j == pl.num_programs(0) - 1)
    def _():
        sum_gain = jnp.zeros_like(gain)
        sum_dc = jnp.zeros_like(gain)
        sum_dh = jnp.zeros_like(gain)
        dwo0 = jnp.zeros(wo_ref.shape[1:], F32)
        dwo1 = jnp.zeros(wo_ref.shape[1:], F32)
        for i in range(clips):
            rows = pl.ds(i * half, half)
            proj = proj_scr[rows, :]
            normed, inv = normed_rows(x_ref[rows, :].astype(F32) + proj)
            y_ref[rows, :] = (proj + y_scr[rows, :] + bias_2).astype(BF)
            dc = dc_scr[rows, :]
            t = dc * gain
            d1 = inv * (t - row_mean(t) - normed * row_mean(t * normed))
            d1_ref[rows, :] = d1
            dh = gy_ref[rows, :].astype(F32) + d1
            dy = dh.astype(BF)
            sum_gain = sum_gain + jnp.sum(dc * normed, axis=0, keepdims=True)
            sum_dc = sum_dc + jnp.sum(dc, axis=0, keepdims=True)
            sum_dh = sum_dh + jnp.sum(dh, axis=0, keepdims=True)
            do_own[i][...] = mm(dy, wo_ref[0]).astype(BF)
            do_send[i][...] = mm(dy, wo_ref[1]).astype(BF)
            dy_t = dy.T
            dwo0 = dwo0 + mm(dy_t, o_own[i][...])
            dwo1 = dwo1 + mm(dy_t, o_got[i][...])
        dwo_ref[0] = dwo0.astype(BF)
        dwo_ref[1] = dwo1.astype(BF)
        sums_ref[0:1, :] = sum_gain
        sums_ref[1:2, :] = sum_dc
        sums_ref[2:3, :] = sum_dh
        sums_ref[3:8, :] = jnp.zeros((5, sums_ref.shape[1]), F32)


def ffn_call(o_own, o_got, x, gy, wide, b1, rows):
    clips = len(o_own)
    tokens, dim = x.shape
    half, width = o_own[0].shape
    hidden = b1.shape[1]
    block = 512
    per = hidden // block
    resident = lambda shape: pl.BlockSpec(
        shape, lambda j: (0,) * len(shape), pipeline_mode=pl.Buffered(1)
    )
    up_spec = pl.BlockSpec((1, dim, block), lambda j: (j // per, 0, j % per))
    out = pl.pallas_call(
        functools.partial(ffn_kernel, clips),
        grid=(2 * per,),
        in_specs=[resident((half, width))] * (2 * clips)
        + [
            resident((tokens, dim)),
            resident((tokens, dim)),
            pl.BlockSpec(
                (2, dim, width), lambda j: (0, 0, 2 * hidden // width), pipeline_mode=pl.Buffered(1)
            ),
            up_spec,
            pl.BlockSpec((1, dim, block), lambda j: (j // per, 0, j % per + per)),
            pl.BlockSpec((1, 1, block), lambda j: (j, 0, 0)),
            resident((8, dim)),
        ],
        out_specs=[resident((tokens, dim))] * 2
        + [resident((half, width))] * (2 * clips)
        + [
            up_spec,
            up_spec,
            resident((2, dim, width)),
            resident((8, dim)),
            pl.BlockSpec((1, 1, block), lambda j: (j, 0, 0)),
        ],
        out_shape=(
            jax.ShapeDtypeStruct((tokens, dim), BF),
            jax.ShapeDtypeStruct((tokens, dim), F32),
        )
        + (jax.ShapeDtypeStruct((half, width), BF),) * (2 * clips)
        + (
            jax.ShapeDtypeStruct((2, dim, hidden), BF),
            jax.ShapeDtypeStruct((2, dim, hidden), BF),
            jax.ShapeDtypeStruct((2, dim, width), BF),
            jax.ShapeDtypeStruct((8, dim), F32),
            jax.ShapeDtypeStruct((2 * per, 1, block), F32),
        ),
        scratch_shapes=[
            pltpu.VMEM((tokens, dim), F32),
            pltpu.VMEM((tokens, dim), BF),
            pltpu.VMEM((dim, tokens), BF),
            pltpu.VMEM((dim, tokens), BF),
            pltpu.VMEM((tokens, dim), F32),
            pltpu.VMEM((tokens, dim), F32),
        ],
        compiler_params=params(56),
        cost_estimate=pl.CostEstimate(
            flops=24 * tokens * dim * hidden, bytes_accessed=30 * MIB, transcendentals=0
        ),
        name="feed_forward",
    )(*o_own, *o_got, x, gy, wide, wide, wide, b1.reshape(2 * per, 1, block), rows)
    y, d1 = out[:2]
    do_own, do_send = out[2 : 2 + clips], out[2 + clips : 2 + 2 * clips]
    dup, ddn, dwo, sums, db1 = out[2 + 2 * clips :]
    return y, d1, do_own, do_send, dup, ddn, dwo, sums, db1.reshape(2, hidden)


def back_kernel(clips, *refs):
    own_refs, got_refs = refs[0:clips], refs[clips : 2 * clips]
    dq_refs = refs[2 * clips : 3 * clips]
    dk_refs = refs[3 * clips : 4 * clips]
    dv_refs = refs[4 * clips : 5 * clips]
    w_ref, rows_ref = refs[5 * clips : 5 * clips + 2]
    outs = refs[5 * clips + 2 :]
    da_own, da_send = outs[0:clips], outs[clips : 2 * clips]
    dw_ref, sums_ref, bias_ref = outs[2 * clips : 2 * clips + 3]
    acc_scr = outs[2 * clips + 3]
    half = own_refs[0].shape[0]
    width = dq_refs[0].shape[1]
    gain, shift = rows_ref[0:1, :], rows_ref[1:2, :]
    sum_gain = jnp.zeros_like(gain)
    sum_da = jnp.zeros_like(gain)
    sum_q = jnp.zeros((1, width), F32)
    sum_v = jnp.zeros((1, width), F32)
    for i in range(clips):
        for s, (x_ref, da_ref) in enumerate(((own_refs[i], da_own[i]), (got_refs[i], da_send[i]))):
            rows = pl.ds(s * half, half)
            normed, _ = normed_rows(x_ref[...].astype(F32))
            act = normed * gain + shift
            act_t = act.astype(BF).T
            da = jnp.zeros(act.shape, F32)
            for j, ref in enumerate((dq_refs[i], dk_refs[i], dv_refs[i])):
                g = ref[rows, :]
                cols = slice(j * width, (j + 1) * width)
                da = da + mm_nt(g, w_ref[:, cols])
                part = mm(act_t, g)
                if i == 0 and s == 0:
                    acc_scr[:, cols] = part
                else:
                    acc_scr[:, cols] += part
                if j == 0:
                    sum_q = sum_q + jnp.sum(g.astype(F32), axis=0, keepdims=True)
                if j == 2:
                    sum_v = sum_v + jnp.sum(g.astype(F32), axis=0, keepdims=True)
            da_ref[...] = da.astype(BF)
            sum_gain = sum_gain + jnp.sum(da * normed, axis=0, keepdims=True)
            sum_da = sum_da + jnp.sum(da, axis=0, keepdims=True)
    dw_ref[...] = acc_scr[...].astype(BF)
    sums_ref[0:1, :] = sum_gain
    sums_ref[1:2, :] = sum_da
    sums_ref[2:8, :] = jnp.zeros((6, sums_ref.shape[1]), F32)
    bias_ref[0:1, :] = sum_q
    bias_ref[1:2, :] = sum_v
    bias_ref[2:8, :] = jnp.zeros((6, width), F32)


def back_call(x_own, x_got, dq, dk, dv, weight, rows):
    clips = len(x_own)
    half, dim = x_own[0].shape
    width = dq[0].shape[1]
    out = pl.pallas_call(
        functools.partial(back_kernel, clips),
        out_shape=(jax.ShapeDtypeStruct((half, dim), BF),) * (2 * clips)
        + (
            jax.ShapeDtypeStruct(weight.shape, BF),
            jax.ShapeDtypeStruct((8, dim), F32),
            jax.ShapeDtypeStruct((8, width), F32),
        ),
        scratch_shapes=[pltpu.VMEM(weight.shape, F32)],
        compiler_params=params(48),
        cost_estimate=pl.CostEstimate(
            flops=8 * clips * half * weight.size, bytes_accessed=16 * MIB, transcendentals=0
        ),
        name="project_back",
    )(*x_own, *x_got, *dq, *dk, *dv, weight, rows)
    return out[:clips], out[clips : 2 * clips], out[2 * clips], out[2 * clips + 1], out[2 * clips + 2]


MESH_ID = pl.DeviceIdType.MESH


def flip(v, bit):
    step = 1 << bit
    return v + step - 2 * step * ((v // step) % 2)


def remote(src, dst, send, recv, device):
    return pltpu.make_async_remote_copy(
        src_ref=src, dst_ref=dst, send_sem=send, recv_sem=recv, device_id=device, device_id_type=MESH_ID
    )


def partners():
    d, c, t = lax.axis_index("dp"), lax.axis_index("ctx"), lax.axis_index("tensor")
    return d, c, t, {
        "x": (d, c, 1 - t),
        "z1": (d, flip(c, 0), t),
        "z2": (d, flip(c, 1), t),
        "core": (flip(d, 0), c, t),
        "y": (flip(d, 1), c, t),
        "swap": (flip(d, 0), flip(c, 1), t),
    }


def greet(devices):
    barrier = pltpu.get_barrier_semaphore()
    for device in devices:
        pl.semaphore_signal(barrier, inc=1, device_id=device, device_id_type=MESH_ID)
    pl.semaphore_wait(barrier, len(devices))


class Plan:
    def __init__(self, steps):
        self.steps = sorted(steps, key=lambda s: s[0])

    def pump(self, now):
        while self.steps and self.steps[0][0] <= now:
            self.steps.pop(0)[1]()


def pick_matrix(out_rows, per, shard):
    rows = shard * (out_rows // per)
    r = lax.broadcasted_iota(jnp.int32, (out_rows, rows), 0)
    k = lax.broadcasted_iota(jnp.int32, (out_rows, rows), 1)
    return jnp.where(k == (r // per) * shard + r % per, 1.0, 0.0).astype(BF)


def both_heads(v):
    return jnp.concatenate([pick(v, h) for h in range(2)], axis=0)


def fold_heads(v_t, rows):
    return jnp.concatenate([v_t[:HD, :rows], v_t[HD:, rows:]], axis=0).T


def attend_pair(q, kvs, s_scr):
    rows = q.shape[0]
    n = kvs[0].shape[0]
    qq = both_heads(q)
    tops = []
    for i, kv in enumerate(kvs):
        s = mm_nt(kv[:, 0:128], qq)
        s_scr[pl.ds(i * n, n), :] = s
        tops.append(jnp.max(s, axis=0, keepdims=True))
    top = functools.reduce(jnp.maximum, tops)
    e = jnp.exp(s_scr[...] - top)
    total = jnp.sum(e, axis=0, keepdims=True)
    v = jnp.concatenate([kv[:, 128:256] for kv in kvs], axis=0)
    mix = mm(v.T, e.astype(BF)) / total
    return fold_heads(mix, rows).astype(BF), top + jnp.log(total)


Y_FIRST = (2,)
SWAPS_FIRST = (0,)
PROJECT_AT = {0: (0,), 2: (1,), 4: (2,)}
POINTS = {
    "s0": (0,),
    "f1": (0,),
    "w0": (0,),
    "z0": (1,),
    "c0": (-3, 1, -1, 3),
    "p0": (6, 4),
    "u0": (6, 3, 0),
    "u1": (6,),
    "c1": (2,),
    "p1": (3, 5, 6, 4),
    "u2": (2, -2, -4),
    "u3": (3,),
    "c2": (2, 0, 1),
    "u6": (1, 4, 5),
    "u7": (6,),
    "u8": (3,),
    "g": (4, 5, 2),
    "g0": (5, 1),
    "g1": (4, 2),
    "g2": (5,),
    "g5": (6,),
}


def start_kernel(
    x_in,
    gy_in,
    qkv_in,
    wo_in,
    up_in,
    dn_in,
    gains_in,
    shifts_in,
    qv_in,
    ub_in,
    x_out,
    wf_out,
    ws_ref,
    rows_ref,
    q_out,
    kv_out,
    own_ref,
    send_ref,
    lse_ref,
    y_ref,
    d1_ref,
    do_own,
    do_send,
    up_hbm,
    dn_hbm,
    dwo_ref,
    sums_ref,
    db1_ref,
    x_home,
    gy_home,
    first,
    second,
    turn_scr,
    x_ref,
    wf_ref,
    q_ref,
    kv_ref,
    gy_ref,
    got_ref,
    s_scr,
    w_scr,
    wo_scr,
    g_scr,
    proj_scr,
    c_scr,
    ct_scr,
    gyt_scr,
    y_scr,
    dc_scr,
    b1_scr,
    local_sem,
    w_sem,
    g_sem,
    save_sem,
    swap_s,
    swap_r,
    gy_s,
    gy_r,
    xe_s,
    xe_r,
    kv_s,
    kv_r,
    oe_s,
    oe_r,
    f_s,
    f_r,
    s_s,
    s_r,
):
    clips, half, dim = x_home.shape
    shard = first.shape[0]
    chunks = second.shape[0]
    width = q_ref.shape[2]
    pairs = width // 128
    d, c, t, dev = partners()
    me = pl.multiple_of((d * 4 + c) * shard, shard)
    me_z2 = pl.multiple_of((d * 4 + flip(c, 1)) * shard, shard)
    quad = pl.multiple_of(d * 4 * shard, 4 * shard)
    quad_y = pl.multiple_of(flip(d, 1) * 4 * shard, 4 * shard)
    moves = (d % 2) != (c // 2)
    greet([dev[k] for k in ("x", "z1", "z2", "core", "y", "swap")])

    for j in range(3):
        first[:, j * width : (j + 1) * width] = qkv_in[j].astype(BF)
    turn_scr[...] = jnp.zeros_like(turn_scr)
    turn_scr[0:2, 0:shard] = gains_in[...]
    turn_scr[2:6, 0:shard] = shifts_in[...]
    turn_scr[...] = turn_scr[...].T
    for j in range(2):
        at = 8 + j * 2 * pairs
        turn_scr[0 : qv_in.shape[1], at : at + 2 * pairs] = qv_in[j]
    first[:, 3 * width :] = turn_scr[:shard].astype(BF)

    place_f = pltpu.make_async_copy(first, wf_ref.at[pl.ds(me, shard)], local_sem.at[0])
    place_s = pltpu.make_async_copy(second, ws_ref.at[:, 0, pl.ds(me, shard)], local_sem.at[1])
    place_f.start()
    keep_x = pltpu.make_async_copy(x_home, x_ref.at[0], local_sem.at[2])
    keep_gy = pltpu.make_async_copy(gy_home, gy_ref, local_sem.at[3])

    swaps = [
        remote(x_home.at[i], x_ref.at[0, i], swap_s.at[i], swap_r.at[i], dev["swap"])
        for i in range(clips)
    ]
    swap_gy = remote(gy_home, gy_ref, gy_s.at[0], gy_r.at[0], dev["swap"])

    def first_stage(i, src, rows, count, device):
        block = wf_ref.at[pl.ds(rows, count)]
        return remote(src if src is not None else block, block, f_s.at[i], f_r.at[i], device)

    f_stages = [
        [first_stage(0, first, me, shard, dev["z2"])],
        [first_stage(1, None, me, shard, dev["z1"]), first_stage(2, None, me_z2, shard, dev["z1"])],
        [first_stage(3, None, quad, 4 * shard, dev["y"])],
        [
            first_stage(4, None, quad, 4 * shard, dev["core"]),
            first_stage(5, None, quad_y, 4 * shard, dev["core"]),
        ],
    ]

    def second_stages(ch):
        def own(i, src, rows, count, device):
            block = ws_ref.at[ch, 0, pl.ds(rows, count)]
            return remote(src if src is not None else block, block, s_s.at[ch, i], s_r.at[ch, i], device)

        def both(i, rows, device):
            block = ws_ref.at[ch, :, pl.ds(rows, 4 * shard)]
            return remote(block, block, s_s.at[ch, i], s_r.at[ch, i], device)

        def over_x(i, rows):
            rows = pl.ds(rows, 4 * shard)
            return remote(
                ws_ref.at[ch, 0, rows], ws_ref.at[ch, 1, rows], s_s.at[ch, i], s_r.at[ch, i], dev["x"]
            )

        along_z = [
            [own(0, second.at[ch], me, shard, dev["z2"])],
            [own(1, None, me, shard, dev["z1"]), own(2, None, me_z2, shard, dev["z1"])],
        ]
        if ch in Y_FIRST:
            plane = [[own(4, None, quad, 4 * shard, dev["y"])], [over_x(3, quad), over_x(7, quad_y)]]
        else:
            plane = [[over_x(3, quad)], [both(4, quad, dev["y"])]]
        return along_z + plane + [[both(5, quad, dev["core"]), both(6, quad_y, dev["core"])]]

    def start(copies):
        for cp in copies:
            cp.start()

    def wait(copies):
        for cp in copies:
            cp.wait()

    s_stages = [second_stages(ch) for ch in range(chunks)]
    reached = [-1] * chunks

    def advance(point):
        for ch in POINTS.get(point, ()):
            if ch < 0:
                special[ch]()
                continue
            if reached[ch] >= len(s_stages[ch]):
                continue
            if reached[ch] >= 0:
                wait(s_stages[ch][reached[ch]])
            reached[ch] += 1
            if reached[ch] < len(s_stages[ch]):
                start(s_stages[ch][reached[ch]])
    def row_copy(j, i, src, dst, device):
        return remote(x_ref.at[src, i], x_ref.at[dst, i], xe_s.at[j, i], xe_r.at[j, i], device)

    own_x = [row_copy(0, i, 0, 1, dev["x"]) for i in range(clips)]
    own_z = [row_copy(1, i, 0, 2, dev["z1"]) for i in range(clips)]
    far_x = [row_copy(2, i, 2, 3, dev["x"]) for i in range(clips)]

    def swap_start(clip_list):
        @pl.when(moves)
        def _():
            for i in clip_list:
                swaps[i].start()

    def swap_done(i):
        @pl.when(moves)
        def _():
            swaps[i].wait()

        own_z[i].start()
        own_x[i].start()

    def far_start(i):
        own_z[i].wait()
        far_x[i].start()

    def gy_start():
        @pl.when(moves)
        def _():
            swap_gy.start()

    special = {
        -1: functools.partial(far_start, 1),
        -2: functools.partial(far_start, 2),
        -3: functools.partial(swap_done, 2),
        -4: gy_start,
    }

    start(f_stages[0])
    for i in range(clips):
        x_home[i] = x_in[i].astype(BF)
        if i in SWAPS_FIRST:
            swap_start([i])
    gy_home[...] = gy_in[...].astype(BF)
    for b in range((chunks - 1) // 2):
        cols = slice(b * second.shape[2], (b + 1) * second.shape[2])
        second[b] = up_in[:, cols].astype(BF)
        second[(chunks - 1) // 2 + b] = dn_in[:, cols].astype(BF)
    turn_scr[...] = jnp.zeros_like(turn_scr)
    turn_scr[0 : ub_in.shape[0], 0 : ub_in.shape[1]] = ub_in[...]
    second[chunks - 1, :, :width] = wo_in[...].astype(BF)
    second[chunks - 1, :, width:] = turn_scr[:shard].astype(BF)
    place_s.start()

    @pl.when(jnp.logical_not(moves))
    def _():
        keep_x.start()
        keep_gy.start()
        keep_x.wait()
        keep_gy.wait()

    place_f.wait()
    place_s.wait()
    advance("s0")
    wait(f_stages[0])
    start(f_stages[1])
    advance("f1")
    wait(f_stages[1])
    start(f_stages[2])
    swap_start([i for i in range(clips) if i not in SWAPS_FIRST])
    advance("f2")
    swap_done(0)
    advance("w0")
    wait(f_stages[2])
    start(f_stages[3])
    advance("f3")
    far_start(0)
    advance("z0")
    swap_done(1)
    advance("w1")
    wait(f_stages[3])
    advance("f4")

    extra = wf_ref[:, 3 * width : 3 * width + 128]
    rows_t = extra.astype(F32).T
    rows_ref[0:8, :] = rows_t[0:8, :]
    shards = dim // shard
    qv = mm(pick_matrix(HD, HD // shards, shard), extra).T
    biases = []
    for r in range(2):
        biases.append(
            jnp.concatenate(
                [qv[8 + r * 2 * pairs + h : 9 + r * 2 * pairs + h, :] for h in range(2 * pairs)], axis=1
            )
        )
    gain, shift = rows_t[0:1, :], rows_t[2:3, :]

    def project(i, s):
        normed, _ = normed_rows(x_ref[s, i].astype(F32))
        act = (normed * gain + shift).astype(BF)
        rows = pl.ds((s % 2) * half, half)
        if s < 2:
            out = mm(act, wf_ref[:, : 3 * width])
            q = (out[:, :width] + biases[0]).astype(BF)
            q_ref[i, rows, :] = (q.astype(F32) * score_scale).astype(BF)
            out = out[:, width:]
        else:
            out = mm(act, wf_ref[:, width : 3 * width])
        v = out[:, width:] + biases[1]
        for p in range(pairs):
            cols = slice(p * 128, (p + 1) * 128)
            kv_ref[s // 2 * 2, i, p, rows, 0:128] = out[:, cols].astype(BF)
            kv_ref[s // 2 * 2, i, p, rows, 128:256] = v[:, cols].astype(BF)

    def kv_copy(j, i):
        return remote(
            kv_ref.at[2 * j, i], kv_ref.at[2 * j + 1, i], kv_s.at[j, i], kv_r.at[j, i], dev["core"]
        )

    units = [(i, p) for i in range(clips) for p in range(pairs)]
    to_core = [[kv_copy(j, i) for j in range(2)] for i in range(clips)]

    o_copies = [
        remote(send_ref.at[i], got_ref.at[i], oe_s.at[i], oe_r.at[i], dev["x"]) for i in range(clips)
    ]

    def project_clip(i):
        project(i, 0)
        own_x[i].wait()
        project(i, 1)
        to_core[i][0].start()
        advance(f"c{i}")
        project(i, 2)
        far_x[i].wait()
        project(i, 3)
        to_core[i][1].start()
        advance(f"p{i}")

    for n, (i, p) in enumerate(units):
        for clip in PROJECT_AT.get(n, ()):
            project_clip(clip)
        if p == 0:
            wait(to_core[i])
        cols = pl.ds(p * 128, 128)
        o, lse = attend_pair(
            q_ref[i, :, cols],
            [kv_ref.at[s, i, p] for s in range(4)],
            s_scr,
        )
        own_ref[i, :, cols] = o[:half]
        send_ref[i, :, cols] = o[half:]
        lse_ref[i, p] = lse
        advance(f"u{n}")
        if p == pairs - 1:
            o_copies[i].start()

    per = (chunks - 1) // 2
    block = ws_ref.shape[3]
    tokens = clips * half
    gain, shift = rows_ref[1:2, :], rows_ref[3:4, :]
    bias_o, bias_2 = rows_ref[4:5, :], rows_ref[5:6, :]

    def finish_chunk(ch):
        while reached[ch] < len(s_stages[ch]):
            if reached[ch] >= 0:
                wait(s_stages[ch][reached[ch]])
            reached[ch] += 1
            if reached[ch] < len(s_stages[ch]):
                start(s_stages[ch][reached[ch]])

    @pl.when(moves)
    def _():
        swap_gy.wait()

    saves = [
        pltpu.make_async_copy(src, dst, save_sem.at[n])
        for n, (src, dst) in enumerate(
            ((kv_ref, kv_out), (x_ref, x_out), (wf_ref, wf_out), (q_ref, q_out))
        )
    ]
    start(saves)
    gyt_scr[...] = gy_ref[...].reshape(tokens, dim).T
    finish_chunk(2 * per)
    load_wo = pltpu.make_async_copy(ws_ref.at[2 * per], wo_scr, local_sem.at[1])
    load_wo.start()
    load_wo.wait()
    taken = pick_matrix(128, 128 // shards, shard)
    for s in range(2):
        cols = mm(taken, wo_scr[s, :, width : width + 128]).T
        for b in range(per):
            b1_scr[s * per + b] = jnp.concatenate(
                [cols[b * 4 + r : b * 4 + r + 1, :] for r in range(4)], axis=1
            )
    for i in range(clips):
        rows = pl.ds(i * half, half)
        wait([o_copies[i]])
        proj = (
            mm_nt(own_ref[i], wo_scr[0, :, :width])
            + mm_nt(got_ref[i], wo_scr[1, :, :width])
            + bias_o
        )
        proj_scr[rows, :] = proj
        normed, _ = normed_rows(x_ref[0, i].astype(F32) + proj)
        c_scr[rows, :] = (normed * gain + shift).astype(BF)
    ct_scr[...] = c_scr[...].T
    advance("g")

    def load_block(b, s, r):
        return pltpu.make_async_copy(ws_ref.at[r * per + b, s], w_scr.at[s, r], w_sem.at[s, r])

    def store_block(b, s, r):
        out = dn_hbm if r else up_hbm
        return pltpu.make_async_copy(g_scr.at[s, r], out.at[b, s], g_sem.at[s, r])

    for b in range(per):
        finish_chunk(b)
        finish_chunk(per + b)
        for s in range(2):
            start([load_block(b, s, r) for r in range(2)])
        for s in range(2):
            wait([load_block(b, s, r) for r in range(2)])
            up, dn = w_scr[s, 0], w_scr[s, 1]
            f = mm(c_scr[...], up) + b1_scr[s * per + b]
            cdf = 0.5 * (1.0 + lax.erf(f * root_half))
            u = (f * cdf).astype(BF)
            slope = cdf + f * (density_scale * jnp.exp(-0.5 * f * f))
            df = mm(gy_ref[...].reshape(tokens, dim), dn) * slope
            dfb = df.astype(BF)
            db1_ref[s * per + b] = jnp.sum(df, axis=0, keepdims=True)
            if b + s:
                y_scr[...] += mm_nt(u, dn)
                dc_scr[...] += mm_nt(dfb, up)
            else:
                y_scr[...] = mm_nt(u, dn)
                dc_scr[...] = mm_nt(dfb, up)
            if b:
                wait([store_block(b - 1, s, r) for r in range(2)])
            g_scr[s, 0] = mm(ct_scr[...], dfb).astype(BF)
            g_scr[s, 1] = mm(gyt_scr[...], u).astype(BF)
            start([store_block(b, s, r) for r in range(2)])
            advance(f"g{2 * b + s}")

    sum_gain = jnp.zeros((1, dim), F32)
    sum_dc = jnp.zeros((1, dim), F32)
    sum_dh = jnp.zeros((1, dim), F32)
    sum_gy = jnp.zeros((1, dim), F32)
    dwo = [jnp.zeros((dim, width), F32) for _ in range(2)]
    for i in range(clips):
        rows = pl.ds(i * half, half)
        proj = proj_scr[rows, :]
        normed, inv = normed_rows(x_ref[0, i].astype(F32) + proj)
        y_ref[i] = (proj + y_scr[rows, :] + bias_2).astype(BF)
        dc = dc_scr[rows, :]
        t_rows = dc * gain
        d1 = inv * (t_rows - row_mean(t_rows) - normed * row_mean(t_rows * normed))
        d1_ref[rows, :] = d1
        gy_rows = gy_ref[i].astype(F32)
        dh = gy_rows + d1
        dy = dh.astype(BF)
        sum_gain = sum_gain + jnp.sum(dc * normed, axis=0, keepdims=True)
        sum_dc = sum_dc + jnp.sum(dc, axis=0, keepdims=True)
        sum_dh = sum_dh + jnp.sum(dh, axis=0, keepdims=True)
        sum_gy = sum_gy + jnp.sum(gy_rows, axis=0, keepdims=True)
        do_own[i] = mm(dy, wo_scr[0, :, :width]).astype(BF)
        do_send[i] = mm(dy, wo_scr[1, :, :width]).astype(BF)
        dy_t = dy.T
        dwo = [dwo[0] + mm(dy_t, own_ref[i]), dwo[1] + mm(dy_t, got_ref[i])]
    for s in range(2):
        dwo_ref[s, :, :width] = dwo[s].astype(BF)
    dwo_ref[:, :, width:] = jnp.zeros((2, dim, block - width), BF)
    for r, row in enumerate((sum_gain, sum_dc, sum_dh, sum_gy)):
        sums_ref[r : r + 1, :] = row
    sums_ref[4:8, :] = jnp.zeros((4, dim), F32)
    for s in range(2):
        wait([store_block(per - 1, s, r) for r in range(2)])
    wait(saves)


def start_call(x, gy, qkv, wo, up, dn, gains, shifts, qv, ub):
    clips, half, dim = x.shape
    shard, width = wo.shape
    block = 512
    per = up.shape[1] // block
    chunks = 2 * per + 1
    pairs = width // 128
    tokens = clips * half
    columns = 3 * width + 128
    any_spec = pl.BlockSpec(memory_space=pl.ANY)
    vmem = pl.BlockSpec(memory_space=pltpu.VMEM)
    dma = pltpu.SemaphoreType.DMA
    both = lambda *shape: [dma(shape), dma(shape)]
    shaped = jax.ShapeDtypeStruct
    head = shaped((clips, half, width), BF)
    return pl.pallas_call(
        start_kernel,
        in_specs=[vmem] * 10,
        out_specs=[any_spec] * 3 + [vmem] + [any_spec] * 2 + [vmem] * 7 + [any_spec] * 2 + [vmem] * 3,
        out_shape=(
            shaped((4, clips, half, dim), BF),
            shaped((dim, columns), BF),
            shaped((chunks, 2, dim, block), BF),
            shaped((8, dim), F32),
            shaped((clips, 2 * half, width), BF),
            shaped((4, clips, pairs, 2 * half, 256), BF),
            head,
            head,
            shaped((clips, pairs, 1, 4 * half), F32),
            shaped((clips, half, dim), BF),
            shaped((tokens, dim), F32),
            head,
            head,
            shaped((per, 2, dim, block), BF),
            shaped((per, 2, dim, block), BF),
            shaped((2, dim, block), BF),
            shaped((8, dim), F32),
            shaped((2 * per, 1, block), F32),
        ),
        scratch_shapes=[
            pltpu.VMEM((clips, half, dim), BF),
            pltpu.VMEM((clips, half, dim), BF),
            pltpu.VMEM((shard, columns), BF),
            pltpu.VMEM((chunks, shard, block), BF),
            pltpu.VMEM((128, 128), F32),
            pltpu.VMEM((4, clips, half, dim), BF),
            pltpu.VMEM((dim, columns), BF),
            pltpu.VMEM((clips, 2 * half, width), BF),
            pltpu.VMEM((4, clips, pairs, 2 * half, 256), BF),
            pltpu.VMEM((clips, half, dim), BF),
            pltpu.VMEM((clips, half, width), BF),
            pltpu.VMEM((8 * half, 4 * half), F32),
            pltpu.VMEM((2, 2, dim, block), BF),
            pltpu.VMEM((2, dim, block), BF),
            pltpu.VMEM((2, 2, dim, block), BF),
            pltpu.VMEM((tokens, dim), F32),
            pltpu.VMEM((tokens, dim), BF),
            pltpu.VMEM((dim, tokens), BF),
            pltpu.VMEM((dim, tokens), BF),
            pltpu.VMEM((tokens, dim), F32),
            pltpu.VMEM((tokens, dim), F32),
            pltpu.VMEM((2 * per, 1, block), F32),
            dma((4,)),
            dma((2, 2)),
            dma((2, 2)),
            dma((4,)),
            *both(clips),
            *both(1),
            *both(3, clips),
            *both(2, clips),
            *both(clips),
            *both(6),
            *both(chunks, 8),
        ],
        compiler_params=pltpu.CompilerParams(
            collective_id=1, has_side_effects=True, vmem_limit_bytes=60 * MIB
        ),
        cost_estimate=pl.CostEstimate(
            flops=30 * 10**9, bytes_accessed=80 * MIB, transcendentals=11 * 10**6
        ),
        name="start_attend",
    )(x, gy, qkv, wo, up, dn, gains, shifts, qv, ub)


X_FIRST = (0,)
ORDER = (
    ("g", 5), ("g", 6), ("y", 0), ("g", 1), ("g", 0), ("g", 5), ("g", 4), ("g", 3),
    ("g", 6), ("u", 0), ("g", 0), ("g", 3), ("u", 1), ("u", 2), ("g", 1), ("g", 5),
    ("u", 6), ("g", 6), ("u", 3), ("b", 0), ("g", 5), ("u", 4), ("g", 6), ("u", 5),
    ("g", 2), ("g", 3), ("g", 6), ("g", 0), ("f", 0), ("g", 5), ("g", 1), ("u", 8),
    ("b", 1), ("g", 1), ("g", 4), ("e", 0), ("g", 3), ("u", 7), ("g", 0), ("g", 6),
    ("f", 1), ("g", 5), ("g", 2), ("b", 2), ("g", 0), ("g", 1), ("v", 0), ("h", 0),
    ("e", 1), ("f", 2), ("g", 3), ("g", 4), ("h", 0), ("g", 1), ("v", 0), ("v", 0),
    ("e", 2), ("h", 0), ("g", 2), ("v", 0), ("h", 0), ("g", 3), ("v", 0), ("g", 2),
    ("g", 0), ("g", 4), ("g", 2), ("v", 0), ("g", 4), ("h", 0), ("g", 2), ("g", 4),
)


def end_kernel(
    q_ref,
    kv_hbm,
    own_ref,
    send_ref,
    lse_ref,
    do_own_ref,
    do_send_ref,
    x_hbm,
    wf_hbm,
    rows_ref,
    d1_hbm,
    y_ref,
    up_hbm,
    dn_hbm,
    wo_hbm,
    sums_ref,
    db1_ref,
    yh_ref,
    dh_ref,
    g2_ref,
    g1_ref,
    vec_ref,
    kv_scr,
    x_scr,
    wf_scr,
    d1_scr,
    do_got,
    core_got,
    dq_scr,
    acc_scr,
    dw_scr,
    da_own,
    da_send,
    da_got,
    far_scr,
    far_got,
    delta_scr,
    loc_scr,
    rc_scr,
    ry_scr,
    rx_scr,
    rz1_scr,
    rz2_scr,
    c1_scr,
    y1_scr,
    p1_scr,
    q1_scr,
    vs_scr,
    vr_scr,
    kv_sem,
    in_sem,
    loc_sem,
    keep_sem,
    do_s,
    do_r,
    y_s,
    y_r,
    dc_s,
    dc_r,
    da_s,
    da_r,
    fz_s,
    fz_r,
    sw_s,
    sw_r,
    h_s,
    h_r,
    g_s,
    g_r,
    v_s,
    v_r,
):
    clips, half, width = own_ref.shape
    pairs = width // 128
    dim = rows_ref.shape[1]
    shard = g1_ref.shape[0]
    chunks = g2_ref.shape[0]
    per = (chunks - 1) // 2
    rows4 = 4 * shard
    d, c, t, dev = partners()
    moves = (d % 2) != (c // 2)
    greet([dev[k] for k in ("x", "z1", "z2", "core", "y", "swap")])

    def start(copies):
        for cp in copies:
            cp.start()

    def wait(copies):
        for cp in copies:
            cp.wait()

    units = [(i, p) for i in range(clips) for p in range(pairs)]
    do_copies = [
        remote(do_send_ref.at[i], do_got.at[i], do_s.at[i], do_r.at[i], dev["x"]) for i in range(clips)
    ]
    start(do_copies)
    loads = [
        pltpu.make_async_copy(
            kv_hbm.at[:, i, p], kv_scr.at[:, i, p], kv_sem.at[i, p]
        )
        for i, p in units
    ]
    start(loads)
    late = [
        pltpu.make_async_copy(x_hbm, x_scr, in_sem.at[0]),
        pltpu.make_async_copy(wf_hbm, wf_scr, in_sem.at[1]),
        pltpu.make_async_copy(d1_hbm, d1_scr, in_sem.at[2]),
    ]
    start(late)
    y_swap = remote(y_ref, yh_ref, y_s.at[0], y_r.at[0], dev["swap"])
    y_keep = pltpu.make_async_copy(y_ref, yh_ref, keep_sem.at[0])

    def y_start():
        @pl.when(moves)
        def _():
            y_swap.start()

        @pl.when(jnp.logical_not(moves))
        def _():
            y_keep.start()

    def grad(ch):
        if ch < per:
            return up_hbm.at[ch]
        if ch < 2 * per:
            return dn_hbm.at[ch - per]
        return wo_hbm

    def band(block):
        return pl.ds(pl.multiple_of(block * rows4, rows4), rows4)

    def strip(block):
        return pl.ds(pl.multiple_of(block * shard, shard), shard)

    mine = [d, flip(d, 1)]
    theirs = [flip(d, 0), flip(flip(d, 0), 1)]

    def g_copy(ch, k, src, dst, device):
        return remote(src, dst, g_s.at[ch, k], g_r.at[ch, k], device)

    def g_stages(ch):
        return [
            [
                g_copy(ch, k, grad(ch).at[:, band(theirs[k])], rc_scr.at[ch, k], dev["core"])
                for k in range(2)
            ],
            [
                g_copy(ch, 2, rc_scr.at[ch, 0, 1], ry_scr.at[ch, 0], dev["x"]),
                g_copy(ch, 7, rc_scr.at[ch, 1, 1], ry_scr.at[ch, 1], dev["x"]),
            ]
            if ch in X_FIRST
            else [g_copy(ch, 2, rc_scr.at[ch, 1], ry_scr.at[ch], dev["y"])],
            [g_copy(ch, 3, ry_scr.at[ch, 1], rx_scr.at[ch], dev["y" if ch in X_FIRST else "x"])],
            [
                g_copy(ch, 4, rx_scr.at[ch, strip(flip(c, 0))], rz1_scr.at[ch, 0], dev["z1"]),
                g_copy(
                    ch, 5, rx_scr.at[ch, strip(flip(flip(c, 0), 1))], rz1_scr.at[ch, 1], dev["z1"]
                ),
            ],
            [g_copy(ch, 6, rz1_scr.at[ch, 1], rz2_scr.at[ch], dev["z2"])],
        ]

    stages = [g_stages(ch) for ch in range(chunks)]
    seen = [ch for kind, ch in ORDER if kind == "g"]
    firsts = [n for n, ch in enumerate(seen) if seen[:n].count(ch) == 1]
    turns = [seen[n] for n in firsts]

    def own_loads(ch):
        slot = turns.index(ch) % 2
        return [
            pltpu.make_async_copy(
                grad(ch).at[:, band(mine[k])], loc_scr.at[slot, k], loc_sem.at[slot, k]
            )
            for k in range(2)
        ]

    reached = [-1] * chunks

    def g_step(ch):
        k = reached[ch]
        if k >= 0:
            wait(stages[ch][k])
        if k == 0:
            turn = turns.index(ch)
            wait(own_loads(ch))
            for m in range(2):
                rc_scr[ch, m] = rc_scr[ch, m] + loc_scr[turn % 2, m]
            if turn + 2 < chunks:
                start(own_loads(turns[turn + 2]))
        elif k == 1:
            if ch in X_FIRST:
                for m in range(2):
                    ry_scr[ch, m] = ry_scr[ch, m] + rc_scr[ch, m, 0]
            else:
                ry_scr[ch] = ry_scr[ch] + rc_scr[ch, 0]
        elif k == 2:
            rx_scr[ch] = rx_scr[ch] + ry_scr[ch, 0]
        elif k == 3:
            rz1_scr[ch, 0] = rz1_scr[ch, 0] + rx_scr[ch, strip(c)]
            rz1_scr[ch, 1] = rz1_scr[ch, 1] + rx_scr[ch, strip(flip(c, 1))]
        elif k == 4:
            g2_ref[ch] = rz1_scr[ch, 0].astype(F32) + rz2_scr[ch].astype(F32)
        if k + 1 < len(stages[ch]):
            start(stages[ch][k + 1])
        reached[ch] = k + 1

    start(own_loads(turns[0]))
    start(own_loads(turns[1]))

    def dkv_copies(u):
        i, p = u
        return [
            remote(
                kv_scr.at[2 * m + 1, i, p],
                core_got.at[m, i, p],
                dc_s.at[m, i, p],
                dc_r.at[m, i, p],
                dev["core"],
            )
            for m in range(2)
        ]

    to_core = [dkv_copies(u) for u in units]

    do_here = []

    def attention(n):
        i, p = units[n]
        cols = pl.ds(p * 128, 128)
        if i not in do_here:
            do_here.append(i)
            do_copies[i].wait()
        loads[n].wait()
        q = q_ref[i, :, cols]
        do = jnp.concatenate([do_own_ref[i, :, cols], do_got[i, :, cols]], axis=0)
        o = jnp.concatenate([own_ref[i, :, cols], send_ref[i, :, cols]], axis=0)
        prod_t = (do.astype(F32) * o.astype(F32)).T
        qq, dd = both_heads(q), both_heads(do)
        delta = jnp.concatenate(
            [jnp.sum(prod_t[h * HD : (h + 1) * HD, :], axis=0, keepdims=True) for h in range(2)],
            axis=1,
        )
        lse = lse_ref[i, p]
        dq_t = jnp.zeros((128, 2 * q.shape[0]), F32)
        rows = kv_scr.shape[3]
        for s in range(0, 4, 2):
            k = jnp.concatenate([kv_scr[s + m, i, p, :, 0:128] for m in range(2)], axis=0)
            v = jnp.concatenate([kv_scr[s + m, i, p, :, 128:256] for m in range(2)], axis=0)
            prob = jnp.exp(mm_nt(k, qq) - lse)
            dv = mm(prob.astype(BF), dd)
            ds = (prob * (mm_nt(v, dd) - delta)).astype(BF)
            dk = mm(ds, qq)
            dq_t = dq_t + mm(k.T, ds)
            for m in range(2):
                part = slice(m * rows, (m + 1) * rows)
                kv_scr[s + m, i, p, :, 0:128] = dk[part].astype(BF)
                kv_scr[s + m, i, p, :, 128:256] = dv[part].astype(BF)
        dq_scr[i, :, cols] = (fold_heads(dq_t, q.shape[0]) * score_scale).astype(BF)
        start(to_core[n])

    gain, shift = rows_ref[0:1, :], rows_ref[2:3, :]
    sums = {
        "gain": jnp.zeros((1, dim), F32),
        "da": jnp.zeros((1, dim), F32),
        "q": jnp.zeros((1, width), F32),
        "v": jnp.zeros((1, width), F32),
    }
    def da_x(i, j):
        return remote(da_send.at[i, j], da_got.at[i, j], da_s.at[i, j], da_r.at[i, j], dev["x"])

    da_xs = [[da_x(i, j) for j in range(2)] for i in range(clips)]
    da_zs = [remote(far_scr.at[i], far_got.at[i], fz_s.at[i], fz_r.at[i], dev["z1"]) for i in range(clips)]

    def project_back(i):
        if i == 0:
            wait(late)
        for n, u in enumerate(units):
            if u[0] == i:
                wait(to_core[n])
        for s in (3, 1, 2, 0):
            m = s // 2
            rows = pl.ds((s % 2) * half, half)
            normed, _ = normed_rows(x_scr[s, i].astype(F32))
            act_t = (normed * gain + shift).astype(BF).T
            halves = [
                kv_scr[2 * m, i, p, rows, :] + core_got[m, i, p, rows, :] for p in range(pairs)
            ]
            g = jnp.concatenate(
                ([] if m else [dq_scr[i, rows, :]])
                + [v[:, :128] for v in halves]
                + [v[:, 128:] for v in halves],
                axis=1,
            )
            cols = slice(width, 3 * width) if m else slice(0, 3 * width)
            da = mm_nt(g, wf_scr[:, cols])
            part = mm(act_t, g)
            if i == 0 and s == 3:
                acc_scr[:, :width] = jnp.zeros((dim, width), F32)
                acc_scr[:, width:] = part
            else:
                acc_scr[:, cols] += part
            total = jnp.sum(g.astype(F32), axis=0, keepdims=True)
            if m == 0:
                sums["q"] = sums["q"] + total[:, :width]
            sums["v"] = sums["v"] + total[:, total.shape[1] - width :]
            sums["gain"] = sums["gain"] + jnp.sum(da * normed, axis=0, keepdims=True)
            sums["da"] = sums["da"] + jnp.sum(da, axis=0, keepdims=True)
            if s % 2:
                da_send[i, m] = da.astype(BF)
                da_xs[i][m].start()
            elif m:
                far_scr[i] = da.astype(BF)
            else:
                da_own[i] = da

    def far_back(i):
        da_xs[i][1].wait()
        far_scr[i] = far_scr[i] + da_got[i, 1]
        da_zs[i].start()

    swaps = [
        remote(delta_scr.at[i], dh_ref.at[i], sw_s.at[i], sw_r.at[i], dev["swap"]) for i in range(clips)
    ]
    keeps = [
        pltpu.make_async_copy(delta_scr.at[i], dh_ref.at[i], keep_sem.at[1 + i]) for i in range(clips)
    ]

    def finish(i):
        da_xs[i][0].wait()
        da_zs[i].wait()
        da = da_own[i] + da_got[i, 0].astype(F32) + far_got[i].astype(F32)
        w = da * gain
        normed, inv = normed_rows(x_scr[0, i].astype(F32))
        rows = pl.ds(i * half, half)
        delta_scr[i] = (
            d1_scr[rows, :] + inv * (w - row_mean(w) - normed * row_mean(w * normed))
        ).astype(BF)

        @pl.when(moves)
        def _():
            swaps[i].start()

        @pl.when(jnp.logical_not(moves))
        def _():
            keeps[i].start()

    def h_copy(k, src, dst, device):
        return remote(src, dst, h_s.at[k], h_r.at[k], device)

    h_stages = [
        [h_copy(k, dw_scr.at[band(theirs[k])], c1_scr.at[k], dev["core"]) for k in range(2)],
        [h_copy(2, c1_scr.at[1], y1_scr, dev["y"])],
        [
            h_copy(3, y1_scr.at[strip(flip(c, 0))], p1_scr.at[0], dev["z1"]),
            h_copy(4, y1_scr.at[strip(flip(flip(c, 0), 1))], p1_scr.at[1], dev["z1"]),
        ],
        [h_copy(5, p1_scr.at[1], q1_scr, dev["z2"])],
    ]
    h_reached = [-1]

    def h_step():
        k = h_reached[0]
        if k < 0:
            dw_scr[...] = acc_scr[...].astype(BF)
        else:
            wait(h_stages[k])
        if k == 0:
            for m in range(2):
                c1_scr[m] = c1_scr[m] + dw_scr[band(mine[m]), :]
        elif k == 1:
            y1_scr[...] = y1_scr[...] + c1_scr[0]
        elif k == 2:
            p1_scr[0] = p1_scr[0] + y1_scr[strip(c), :]
            p1_scr[1] = p1_scr[1] + y1_scr[strip(flip(c, 1)), :]
        elif k == 3:
            g1_ref[...] = p1_scr[0].astype(F32) + q1_scr[...].astype(F32)
        if k + 1 < len(h_stages):
            start(h_stages[k + 1])
        h_reached[0] = k + 1

    def small_sums():
        zero = jnp.zeros((1, dim), F32)
        shared = [
            sums["gain"],
            sums_ref[0:1, :],
            sums["da"],
            sums_ref[1:2, :],
            sums_ref[2:3, :],
            sums_ref[3:4, :],
        ]
        ub = [
            jnp.concatenate([db1_ref[s * per + b] for b in range(per)], axis=1) for s in range(2)
        ]
        for r, row in enumerate(shared):
            vs_scr[0, r : r + 1, :] = row
            vs_scr[1, r : r + 1, :] = row
        vs_scr[0, 6:7, :] = jnp.concatenate([sums["q"], sums["v"]], axis=1)
        vs_scr[1, 6:7, :] = zero
        vs_scr[0, 7:8, :] = zero
        vs_scr[1, 7:8, :] = zero
        vs_scr[0, 10:16, :] = jnp.zeros((6, dim), F32)
        vs_scr[1, 10:16, :] = jnp.zeros((6, dim), F32)
        for s in range(2):
            vs_scr[s, 8:9, :] = ub[s][:, :dim]
            vs_scr[s, 9:10, :] = ub[s][:, dim:]
    v_devices = ("x", "core", "y", "z1", "z2")

    def v_copy(k):
        src = vs_scr.at[1] if k == 0 else vs_scr.at[0] if k == 1 else vr_scr.at[k - 1]
        return remote(src, vr_scr.at[k], v_s.at[k], v_r.at[k], dev[v_devices[k]])

    v_copies = [v_copy(k) for k in range(len(v_devices))]

    v_reached = [-1]

    def v_step():
        k = v_reached[0]
        if k < 0:
            small_sums()
        else:
            v_copies[k].wait()
        if k == 0:
            vs_scr[0] = vs_scr[0] + vr_scr[0]
        elif k == 1:
            vr_scr[1] = vr_scr[1] + vs_scr[0]
        elif k > 1:
            vr_scr[k] = vr_scr[k] + vr_scr[k - 1]
        if k + 1 < len(v_devices):
            v_copies[k + 1].start()
        else:
            vec_ref[...] = vr_scr[k]
        v_reached[0] = k + 1

    steps = {
        "y": lambda n: y_start(),
        "u": attention,
        "b": project_back,
        "f": far_back,
        "e": finish,
        "g": g_step,
        "h": lambda n: h_step(),
        "v": lambda n: v_step(),
    }
    for kind, n in ORDER:
        steps[kind](n)

    @pl.when(moves)
    def _():
        y_swap.wait()
        wait(swaps)

    @pl.when(jnp.logical_not(moves))
    def _():
        y_keep.wait()
        wait(keeps)


def end_call(q, kv, own, send, lse, do_own, do_send, x, wf, rows, d1, y, up, dn, wo, sums, db1):
    clips, half, width = own.shape
    pairs = width // 128
    dim = rows.shape[1]
    shard = dim // 16
    per, _, _, block = up.shape
    chunks = 2 * per + 1
    any_spec = pl.BlockSpec(memory_space=pl.ANY)
    vmem = pl.BlockSpec(memory_space=pltpu.VMEM)
    dma = pltpu.SemaphoreType.DMA
    rows4 = 4 * shard
    both = lambda *shape: [dma(shape), dma(shape)]
    return pl.pallas_call(
        end_kernel,
        in_specs=[vmem, any_spec, vmem, vmem, vmem, vmem, vmem, any_spec, any_spec, vmem]
        + [any_spec, vmem]
        + [any_spec] * 3
        + [vmem, vmem],
        out_specs=[any_spec, any_spec, vmem, vmem, vmem],
        out_shape=(
            jax.ShapeDtypeStruct((clips, half, dim), BF),
            jax.ShapeDtypeStruct((clips, half, dim), BF),
            jax.ShapeDtypeStruct((chunks, shard, block), F32),
            jax.ShapeDtypeStruct((shard, 3 * width), F32),
            jax.ShapeDtypeStruct((16, dim), F32),
        ),
        scratch_shapes=[
            pltpu.VMEM(kv.shape, BF),
            pltpu.VMEM(x.shape, BF),
            pltpu.VMEM(wf.shape, BF),
            pltpu.VMEM(d1.shape, F32),
            pltpu.VMEM(do_send.shape, BF),
            pltpu.VMEM((2, clips, pairs, 2 * half, 256), BF),
            pltpu.VMEM(q.shape, BF),
            pltpu.VMEM((dim, 3 * width), F32),
            pltpu.VMEM((dim, 3 * width), BF),
            pltpu.VMEM((clips, half, dim), F32),
            pltpu.VMEM((clips, 2, half, dim), BF),
            pltpu.VMEM((clips, 2, half, dim), BF),
            pltpu.VMEM((clips, half, dim), BF),
            pltpu.VMEM((clips, half, dim), BF),
            pltpu.VMEM((clips, half, dim), BF),
            pltpu.VMEM((2, 2, 2, rows4, block), BF),
            pltpu.VMEM((chunks, 2, 2, rows4, block), BF),
            pltpu.VMEM((chunks, 2, rows4, block), BF),
            pltpu.VMEM((chunks, rows4, block), BF),
            pltpu.VMEM((chunks, 2, shard, block), BF),
            pltpu.VMEM((chunks, shard, block), BF),
            pltpu.VMEM((2, rows4, 3 * width), BF),
            pltpu.VMEM((rows4, 3 * width), BF),
            pltpu.VMEM((2, shard, 3 * width), BF),
            pltpu.VMEM((shard, 3 * width), BF),
            pltpu.VMEM((2, 16, dim), F32),
            pltpu.VMEM((5, 16, dim), F32),
            dma((clips, pairs)),
            dma((3,)),
            dma((2, 2)),
            dma((1 + clips,)),
            *both(clips),
            *both(1),
            *both(2, clips, pairs),
            *both(clips, 2),
            *both(clips),
            *both(clips),
            *both(6),
            *both(chunks, 8),
            *both(5),
        ],
        compiler_params=pltpu.CompilerParams(
            collective_id=2, has_side_effects=True, vmem_limit_bytes=62 * MIB
        ),
        cost_estimate=pl.CostEstimate(
            flops=20 * 10**9, bytes_accessed=40 * MIB, transcendentals=11 * 10**6
        ),
        name="attend_back_end",
    )(q, kv, own, send, lse, do_own, do_send, x, wf, rows, d1, y, up, dn, wo, sums, db1)


def update_kernel(rates, *refs):
    g1_ref, g2_ref, vec_ref = refs[0:3]
    params, firsts, seconds = refs[3:11], refs[11:27:2], refs[12:27:2]
    grads, news, firsts_next, seconds_next = refs[27:35], refs[35:43], refs[43:59:2], refs[44:59:2]
    qkv, proj, up, down, gains, shifts, qv, ub = range(8)
    shard, width = params[proj].shape
    per = (g2_ref.shape[0] - 1) // 2
    block = g2_ref.shape[2]
    dim = vec_ref.shape[1]
    me = lax.axis_index("dp") * lax.axis_size("ctx") + lax.axis_index("ctx")

    def write(n, at, g):
        rate, decay = rates[n]
        new, one, two = adam_step(params[n][at], firsts[n][at], seconds[n][at], g, rate, decay)
        grads[n][at] = g
        news[n][at] = new
        firsts_next[n][at] = one
        seconds_next[n][at] = two

    everything = slice(None)
    for j in range(3):
        write(qkv, j, g1_ref[:, j * width : (j + 1) * width])
    for b in range(per):
        cols = (everything, slice(b * block, (b + 1) * block))
        write(up, cols, g2_ref[b])
        write(down, cols, g2_ref[per + b])
    write(proj, (everything, everything), g2_ref[2 * per, :, :width])

    def front(per_device):
        return pltpu.roll(vec_ref[...], lax.rem(dim - me * per_device, dim), 1)

    rows = front(shard)
    write(gains, (everything, everything), rows[0:2, :shard])
    write(shifts, (everything, everything), rows[2:6, :shard])
    cols = params[qv].shape[1]
    heads = params[qv].shape[2]
    rows = front(cols)
    for j in range(2):
        parts = [rows[6:7, (j * heads + h) * HD : (j * heads + h) * HD + 128] for h in range(heads - 1)]
        last = rows[6:7, (j * heads + heads - 2) * HD : (j * heads + heads) * HD]
        parts.append(pltpu.roll(last, HD, 1))
        square = jnp.concatenate(parts + [jnp.zeros((128 - heads, 128), F32)], axis=0).T
        write(qv, j, square[:cols, :heads])
    cols, lines = params[ub].shape
    rows = front(cols)
    each = dim // 128
    parts = [
        rows[8 + r // each : 9 + r // each, (r % each) * 128 : (r % each + 1) * 128]
        for r in range(lines)
    ]
    square = jnp.concatenate(parts + [jnp.zeros((128 - lines, 128), F32)], axis=0).T
    write(ub, (everything, everything), square[:cols, :lines])


def update_call(g1, g2, vec, params, moments, rates):
    shapes = [jax.ShapeDtypeStruct(p.shape, F32) for p in params]
    vmem = pl.BlockSpec(memory_space=pltpu.VMEM)
    out = shapes + shapes + [s for s in shapes for _ in range(2)]
    return pl.pallas_call(
        functools.partial(update_kernel, rates),
        in_specs=[vmem] * 27,
        out_specs=[vmem] * 32,
        out_shape=out,
        compiler_params=pltpu.CompilerParams(vmem_limit_bytes=48 * MIB),
        cost_estimate=pl.CostEstimate(flops=10**7, bytes_accessed=8 * MIB, transcendentals=10**6),
        name="update",
    )(g1, g2, vec, *params, *moments)


class Links:
    def __init__(self, mesh):
        self.dp = mesh.shape["dp"]
        self.ctx = mesh.shape["ctx"]
        self.tensor = mesh.shape["tensor"]
        self.dp_bits = self.dp.bit_length() - 1
        self.ctx_bits = self.ctx.bit_length() - 1

    def flat(self, d, c, t):
        return (d * self.ctx + c) * self.tensor + t

    def move(self, value, partner):
        pairs = []
        for d in range(self.dp):
            for c in range(self.ctx):
                for t in range(self.tensor):
                    other = partner(d, c, t)
                    if other != (d, c, t):
                        pairs.append((self.flat(d, c, t), self.flat(*other)))
        return lax.ppermute(value, ("dp", "ctx", "tensor"), pairs)

    def across_x(self, value):
        return self.move(value, lambda d, c, t: (d, c, t ^ 1))

    def across_core(self, value):
        return self.move(value, lambda d, c, t: (d ^ 1, c, t))

    def across_z(self, value):
        return self.move(value, lambda d, c, t: (d, c ^ 1, t))

    def stays(self):
        d, c = lax.axis_index("dp"), lax.axis_index("ctx")
        return (d % 2) == (c // (self.ctx // 2))

    def swap(self, value):
        half = self.ctx // 2
        moved = self.move(
            value,
            lambda d, c, t: (d, c, t) if d % 2 == c // half else (d ^ 1, c ^ half, t),
        )
        return jnp.where(self.stays(), value, moved)

    def stages(self):
        out = []
        for bit in reversed(range(self.ctx_bits)):
            out.append(("ctx", bit, self.ctx_bits - 1 - bit))
        for bit in reversed(range(self.dp_bits)):
            out.append(("dp", bit, self.dp_bits - 1 - bit))
        return out

    def step(self, value, axis, bit):
        if axis == "ctx":
            return self.move(value, lambda d, c, t: (d, c ^ (1 << bit), t))
        return self.move(value, lambda d, c, t: (d ^ (1 << bit), c, t))

    def side(self, axis, bit):
        return (lax.axis_index(axis) // (1 << bit)) % 2

    def gather(self, value, both):
        shape = value.shape
        lead = 0
        for axis, bit, place in self.stages():
            if axis == "dp" and both and not lead:
                value = jnp.stack([value, self.across_x(value)])
                lead = 1
            got = self.step(value, axis, bit)
            low = self.side(axis, bit) == 0
            value = jnp.stack(
                [jnp.where(low, value, got), jnp.where(low, got, value)], axis=lead + place
            )
        shards = self.dp * self.ctx
        return value.reshape((2,) * lead + (shards * shape[0],) + shape[1:])

    def scatter(self, value, both):
        lead = 1 if both else 0
        rest = value.shape[lead + 1 :]
        value = value.reshape(
            value.shape[:lead] + (2,) * (self.dp_bits + self.ctx_bits) + rest
        )
        for axis, bit, place in reversed(self.stages()):
            if axis == "ctx" and lead:
                value = value[0] + self.across_x(value[1])
                lead = 0
            side = self.side(axis, bit)
            keep = lax.dynamic_index_in_dim(value, side, lead + place, keepdims=False)
            give = lax.dynamic_index_in_dim(value, 1 - side, lead + place, keepdims=False)
            value = keep + self.step(give, axis, bit)
        return value


def body(links, *args):
    (
        block_input,
        out_cotangent,
        qkv_weight,
        proj_weight,
        up_weight,
        down_weight,
        norm_gains,
        shift_terms,
        qv_bias,
        up_bias,
        qkv_first,
        qkv_second,
        proj_first,
        proj_second,
        up_first,
        up_second,
        down_first,
        down_second,
        gains_first,
        gains_second,
        shifts_first,
        shifts_second,
        qv_bias_first,
        qv_bias_second,
        up_bias_first,
        up_bias_second,
    ) = args
    half, clips, dim = block_input.shape
    shard = qkv_weight.shape[0]
    shards = dim // shard
    width = qkv_weight.shape[2]
    hidden = up_weight.shape[1]
    heads = width // HD

    x_home = jnp.transpose(block_input, (1, 0, 2)).astype(BF)
    gy_home = jnp.transpose(out_cotangent, (1, 0, 2)).astype(BF)
    x = links.swap(x_home)
    x_own = [x[i] for i in range(clips)]
    x_got = [links.across_x(v) for v in x_own]

    def lanes(parts):
        flat = jnp.concatenate([p.astype(BF).reshape(-1) for p in parts])
        return jnp.pad(flat, (0, shard * 128 - flat.size)).reshape(shard, 128)

    first = jnp.concatenate(
        [qkv_weight.reshape(shard, 3 * width).astype(BF), lanes([norm_gains, shift_terms, qv_bias])],
        axis=1,
    )
    second = jnp.concatenate(
        [up_weight.astype(BF), down_weight.astype(BF), proj_weight.astype(BF), lanes([up_bias])],
        axis=1,
    )
    first = links.gather(first, False)
    second = links.gather(second, True)
    w_qkv = first[:, : 3 * width]
    small = first[:, 3 * width :].reshape(shards, shard * 128)
    n_g, n_s = 2 * shard, 4 * shard
    gains = jnp.transpose(small[:, :n_g].reshape(shards, 2, shard), (1, 0, 2)).reshape(2, dim)
    shifts = jnp.transpose(
        small[:, n_g : n_g + n_s].reshape(shards, 4, shard), (1, 0, 2)
    ).reshape(4, dim)
    qv_cols = qv_bias.shape[2]
    biases = jnp.transpose(
        small[:, n_g + n_s : n_g + n_s + qv_bias.size].reshape(shards, 2, heads, qv_cols),
        (1, 2, 0, 3),
    ).reshape(2, width)
    ub_rows, ub_cols = up_bias.shape
    b1 = jnp.transpose(
        second[:, :, 2 * hidden + width :]
        .reshape(2, shards, shard * 128)[:, :, : up_bias.size]
        .reshape(2, shards, ub_rows, ub_cols),
        (0, 2, 1, 3),
    ).reshape(2, hidden)
    gains, shifts, biases, b1 = (v.astype(F32) for v in (gains, shifts, biases, b1))
    zero4 = jnp.zeros((4, dim), F32)
    rows_one = jnp.concatenate([gains[0:1], shifts[0:1], zero4, zero4[:2]])
    rows_two = jnp.concatenate([gains[1:2], shifts[1:4], zero4])
    biases = jnp.concatenate([biases, jnp.zeros((6, width), F32)])

    q, pieces, o_own, o_send, o_got, lse = [], [], [], [], [], []
    for i in range(clips):
        q_i, kv = qkv_call(x_own[i], x_got[i], w_qkv, rows_one, biases)
        kv_z = links.across_z(kv)
        kv_c = links.across_core(kv)
        kv_d = links.across_core(kv_z)
        q.append(q_i)
        pieces.append((kv, kv_c, kv_z, kv_d))
    gy = links.swap(gy_home)
    for i in range(clips):
        own, send, lse_i = attend_call(q[i], pieces[i])
        o_own.append(own)
        o_send.append(send)
        o_got.append(links.across_x(send))
        lse.append(lse_i)

    tokens = clips * half
    y, d1, do_own, do_send, d_up, d_down, d_proj, sums_two, d_b1 = ffn_call(
        o_own, o_got, x.reshape(tokens, dim), gy.reshape(tokens, dim), second, b1, rows_two
    )
    y_home = links.swap(y.reshape(clips, half, dim))
    block_output = block_input + jnp.transpose(y_home, (1, 0, 2)).astype(F32)

    grads_two = jnp.concatenate([d_up, d_down, d_proj], axis=2)
    grads_two = links.scatter(grads_two.reshape(2, shards, shard, -1), True)

    dq, dk, dv = [], [], []
    do_got = [links.across_x(v) for v in do_send]
    for i in range(clips):
        dq_i, dks, dvs = attend_back_call(
            q[i], do_own[i], do_got[i], o_own[i], o_send[i], lse[i], pieces[i]
        )
        dq.append(dq_i)
        for parts, out in ((dks, dk), (dvs, dv)):
            mine, core, z, diag = parts
            mine = mine + links.across_core(core)
            z = z + links.across_core(diag)
            out.append(mine + links.across_z(z))
    da_own, da_send, d_qkv, sums_one, sums_bias = back_call(
        x_own, x_got, dq, dk, dv, w_qkv, rows_one
    )
    grads_one = links.scatter(d_qkv.reshape(shards, shard, 3 * width), False)
    d1 = d1.reshape(clips, half, dim)
    deltas = []
    for i in range(clips):
        da = da_own[i].astype(F32) + links.across_x(da_send[i]).astype(F32)
        normed, inv = normed_rows(x_own[i].astype(F32))
        w = da * gains[0]
        deltas.append(
            (d1[i] + inv * (w - row_mean(w) - normed * row_mean(w * normed))).astype(BF)
        )
    delta_home = links.swap(jnp.stack(deltas))
    input_grad = out_cotangent + jnp.transpose(delta_home, (1, 0, 2)).astype(F32)

    cot_sum = jnp.sum(out_cotangent, axis=(0, 1))[None]
    both = jnp.concatenate(
        [sums_one[0:1], sums_two[0:1], sums_one[1:2], sums_two[1:2], sums_two[2:3], cot_sum]
    )
    both = jnp.transpose(both.reshape(6, shards, shard), (1, 0, 2)).reshape(shards, 6 * shard)
    ub = jnp.transpose(d_b1.reshape(2, ub_rows, shards, ub_cols), (0, 2, 1, 3)).reshape(
        2, shards, up_bias.size
    )
    crossed = links.across_x(jnp.concatenate([both, ub[1]], axis=1))
    qv = jnp.transpose(
        sums_bias[0:2].reshape(2, heads, shards, qv_cols), (2, 0, 1, 3)
    ).reshape(shards, qv_bias.size)
    vec = jnp.concatenate([jnp.concatenate([both, ub[0]], axis=1) + crossed, qv], axis=1)
    vec = links.scatter(vec, False)
    gains_grad = vec[:n_g].reshape(2, shard)
    shifts_grad = vec[n_g : n_g + n_s].reshape(4, shard)
    up_bias_grad = vec[6 * shard : 6 * shard + up_bias.size].reshape(up_bias.shape)
    qv_bias_grad = vec[6 * shard + up_bias.size :].reshape(qv_bias.shape)

    qkv_grad = grads_one.astype(F32).reshape(qkv_weight.shape)
    grads_two = grads_two.astype(F32)
    up_grad = grads_two[:, :hidden]
    down_grad = grads_two[:, hidden : 2 * hidden]
    proj_grad = grads_two[:, 2 * hidden :]

    qkv_next = adam_step(qkv_weight, qkv_first, qkv_second, qkv_grad, rate_qkv, decay_rate)
    proj_next = adam_step(proj_weight, proj_first, proj_second, proj_grad, rate_proj, decay_rate)
    up_next = adam_step(up_weight, up_first, up_second, up_grad, rate_up, decay_rate)
    down_next = adam_step(down_weight, down_first, down_second, down_grad, rate_down, decay_rate)
    gains_next = adam_step(norm_gains, gains_first, gains_second, gains_grad, rate_gains, 0.0)
    shifts_next = adam_step(shift_terms, shifts_first, shifts_second, shifts_grad, rate_shifts, 0.0)
    qv_next = adam_step(qv_bias, qv_bias_first, qv_bias_second, qv_bias_grad, rate_query_bias, 0.0)
    ub_next = adam_step(up_bias, up_bias_first, up_bias_second, up_bias_grad, rate_up_bias, 0.0)
    nexts = (qkv_next, proj_next, up_next, down_next, gains_next, shifts_next, qv_next, ub_next)
    return (
        block_output,
        input_grad,
        qkv_grad,
        proj_grad,
        up_grad,
        down_grad,
        gains_grad,
        shifts_grad,
        qv_bias_grad,
        up_bias_grad,
        *(n[0] for n in nexts),
        *(m for n in nexts for m in n[1:]),
    )


def body_fused(links, *args):
    block_input, out_cotangent = args[0:2]
    moments = args[10:]

    orders = ((1, 0, 2), (0, 1), (0, 1), (0, 1), (0, 1), (0, 1), (0, 2, 1), (1, 0))
    backs = ((1, 0, 2), (0, 1), (0, 1), (0, 1), (0, 1), (0, 1), (0, 2, 1), (1, 0))
    turned = [jnp.transpose(v, o) for v, o in zip(args[2:10], orders)]
    x, wf, _, rows, q, kv, own, send, lse, y, d1, do_own, do_send, up, dn, wo, sums, db1 = start_call(
        jnp.transpose(block_input, (1, 0, 2)), jnp.transpose(out_cotangent, (1, 0, 2)), *turned
    )
    y_home, delta_home, g2, g1, vec = end_call(
        q,
        kv,
        own,
        send,
        lse,
        do_own,
        do_send,
        x,
        wf,
        rows,
        d1,
        y,
        up,
        dn,
        wo,
        sums,
        db1,
    )
    block_output = block_input + jnp.transpose(y_home, (1, 0, 2)).astype(F32)
    input_grad = out_cotangent + jnp.transpose(delta_home, (1, 0, 2)).astype(F32)

    rates = (
        (rate_qkv, decay_rate),
        (rate_proj, decay_rate),
        (rate_up, decay_rate),
        (rate_down, decay_rate),
        (rate_gains, 0.0),
        (rate_shifts, 0.0),
        (rate_query_bias, 0.0),
        (rate_up_bias, 0.0),
    )
    turned_moments = [jnp.transpose(v, orders[n // 2]) for n, v in enumerate(moments)]
    out = update_call(g1, g2, vec, turned, turned_moments, rates)
    places = list(range(8)) * 2 + [n // 2 for n in range(16)]
    return (block_output, input_grad, *(jnp.transpose(v, backs[n]) for v, n in zip(out, places)))


def solution(mesh):
    rows = P(("ctx", "tensor"), "dp", None)
    qkv = P(("dp", "ctx"), None, "tensor")
    mat = P(("dp", "ctx"), "tensor")
    norm = P(None, ("dp", "ctx"))
    qv = P(None, "tensor", ("dp", "ctx"))
    ub = P("tensor", ("dp", "ctx"))
    each = (qkv, mat, mat, mat, norm, norm, qv, ub)
    moments = tuple(s for s in each for _ in range(2))
    fused = (mesh.shape["dp"], mesh.shape["ctx"], mesh.shape["tensor"]) == (4, 4, 2)
    return jax.shard_map(
        functools.partial(body_fused if fused else body, Links(mesh)),
        mesh=mesh,
        in_specs=(rows, rows) + each + moments,
        out_specs=(rows, rows) + each + each + moments,
        check_vma=False,
    )
```

```python
import functools
import math

import jax
import jax.numpy as jnp
from jax import lax
from jax.experimental import pallas as pl
from jax.experimental.pallas import tpu as pltpu
from jax.sharding import PartitionSpec as P

HD = 64
STEP = 4
F32 = jnp.float32
BF = jnp.bfloat16

eps_norm = 1e-05
beta_one = 0.9
beta_two = 0.98
eps_adam = 1e-06
rate_qkv = 0.6
rate_proj = 1.2
rate_up = 0.1
rate_down = 0.15
rate_gains = 4.0
rate_shifts = 8.0
rate_query_bias = 20.0
rate_up_bias = 0.4
decay_rate = 0.01
root_half = 0.7071067811865476
density_scale = 0.3989422804014327
score_scale = HD ** (-0.5)
MIB = 2**20


def params(limit_mib):
    return pltpu.CompilerParams(vmem_limit_bytes=limit_mib * MIB)


def mm(a, b):
    return lax.dot_general(a, b, (((1,), (0,)), ((), ())), preferred_element_type=F32)


def mm_nt(a, b):
    return lax.dot_general(a, b, (((1,), (1,)), ((), ())), preferred_element_type=F32)


def row_mean(v):
    return jnp.mean(v, axis=-1, keepdims=True)


def normed_rows(v):
    center = v - row_mean(v)
    inv = lax.rsqrt(row_mean(center * center) + eps_norm)
    return center * inv, inv


def adam_step(current, moment_one, moment_two, gradient, rate_value, decay_value):
    one_next = beta_one * moment_one + (1.0 - beta_one) * gradient
    two_next = beta_two * moment_two + (1.0 - beta_two) * gradient * gradient
    step_ratio = (
        one_next / (1.0 - beta_one**STEP) / (jnp.sqrt(two_next / (1.0 - beta_two**STEP)) + eps_adam)
    )
    return (current - rate_value * (step_ratio + decay_value * current), one_next, two_next)


def qkv_kernel(own_ref, other_ref, w_ref, rows_ref, bias_ref, q_ref, kv_ref):
    gain, shift = rows_ref[0:1, :], rows_ref[1:2, :]
    bias_q, bias_v = bias_ref[0:1, :], bias_ref[1:2, :]
    half = own_ref.shape[0]
    width = q_ref.shape[1]
    for i, ref in enumerate((own_ref, other_ref)):
        normed, _ = normed_rows(ref[...].astype(F32))
        act = (normed * gain + shift).astype(BF)
        out = mm(act, w_ref[...])
        rows = pl.ds(i * half, half)
        q = (out[:, :width] + bias_q).astype(BF)
        q_ref[rows, :] = (q.astype(F32) * score_scale).astype(BF)
        kv_ref[rows, :width] = out[:, width : 2 * width].astype(BF)
        kv_ref[rows, width:] = (out[:, 2 * width :] + bias_v).astype(BF)


def qkv_call(own, other, weight, rows, bias):
    half, _ = own.shape
    width = weight.shape[1] // 3
    return pl.pallas_call(
        qkv_kernel,
        out_shape=(
            jax.ShapeDtypeStruct((2 * half, width), BF),
            jax.ShapeDtypeStruct((2 * half, 2 * width), BF),
        ),
        compiler_params=params(32),
        cost_estimate=pl.CostEstimate(
            flops=2 * 2 * half * weight.size, bytes_accessed=4 * MIB, transcendentals=0
        ),
        name="project_qkv",
    )(own, other, weight, rows, bias)


def head_mask(shape, h):
    lane = lax.broadcasted_iota(jnp.int32, shape, 1)
    return (lane >= HD) if h else (lane < HD)


def pick(v, h):
    return jnp.where(head_mask(v.shape, h), v, jnp.zeros_like(v))


def attend_kernel(q_ref, *refs):
    k_refs, v_refs = refs[0:4], refs[4:8]
    own_ref, send_ref, lse_ref, s_scr = refs[8:]
    half = own_ref.shape[0]
    q = q_ref[...]
    n = k_refs[0].shape[0]
    v_t = [r[...].T for r in v_refs]
    parts = []
    for h in range(2):
        qh = pick(q, h)
        tops = []
        for i in range(4):
            s = mm_nt(k_refs[i][...], qh)
            s_scr[h, pl.ds(i * n, n), :] = s
            tops.append(jnp.max(s, axis=0, keepdims=True))
        top = functools.reduce(jnp.maximum, tops)
        total = jnp.zeros_like(top)
        mix = jnp.zeros((HD, q.shape[0]), F32)
        for i in range(4):
            e = jnp.exp(s_scr[h, pl.ds(i * n, n), :] - top)
            total = total + jnp.sum(e, axis=0, keepdims=True)
            mix = mix + mm(v_t[i][h * HD : (h + 1) * HD, :], e.astype(BF))
        parts.append(mix / total)
        lse_ref[0, h : h + 1, :] = top + jnp.log(total)
    o = jnp.concatenate(parts, axis=0).T.astype(BF)
    own_ref[...] = o[:half]
    send_ref[...] = o[half:]


def attend_call(q, pieces):
    rows, width = q.shape
    pairs = width // 128
    n = pieces[0].shape[0]
    half = rows // 2
    k_spec = pl.BlockSpec((n, 128), lambda p: (0, p))
    v_spec = pl.BlockSpec((n, 128), lambda p: (0, p + pairs))
    return pl.pallas_call(
        attend_kernel,
        grid=(pairs,),
        in_specs=[pl.BlockSpec((rows, 128), lambda p: (0, p))] + [k_spec] * 4 + [v_spec] * 4,
        out_specs=[
            pl.BlockSpec((half, 128), lambda p: (0, p)),
            pl.BlockSpec((half, 128), lambda p: (0, p)),
            pl.BlockSpec((1, 2, rows), lambda p: (p, 0, 0)),
        ],
        out_shape=(
            jax.ShapeDtypeStruct((half, width), BF),
            jax.ShapeDtypeStruct((half, width), BF),
            jax.ShapeDtypeStruct((pairs, 2, rows), F32),
        ),
        scratch_shapes=[pltpu.VMEM((2, 4 * n, rows), F32)],
        compiler_params=params(40),
        cost_estimate=pl.CostEstimate(
            flops=16 * rows * 4 * n * width,
            bytes_accessed=4 * MIB,
            transcendentals=pairs * 2 * rows * 4 * n,
        ),
        name="attend",
    )(q, *pieces, *pieces)


def attend_back_kernel(*refs):
    q_ref, do_own_ref, do_got_ref, o_own_ref, o_send_ref, lse_ref = refs[:6]
    k_refs, v_refs = refs[6:10], refs[10:14]
    dq_ref = refs[14]
    dk_refs, dv_refs = refs[15:19], refs[19:23]
    q = q_ref[...]
    do = jnp.concatenate([do_own_ref[...], do_got_ref[...]], axis=0)
    o = jnp.concatenate([o_own_ref[...], o_send_ref[...]], axis=0)
    prod_t = (do.astype(F32) * o.astype(F32)).T
    q_heads = [pick(q, h) for h in range(2)]
    do_heads = [pick(do, h) for h in range(2)]
    deltas = [
        jnp.sum(prod_t[h * HD : (h + 1) * HD, :], axis=0, keepdims=True) for h in range(2)
    ]
    lses = [lse_ref[0, h : h + 1, :] for h in range(2)]
    dq_t = [jnp.zeros((HD, q.shape[0]), F32) for _ in range(2)]
    for i in range(4):
        k = k_refs[i][...]
        v = v_refs[i][...]
        k_t = k.T
        dk = jnp.zeros(k.shape, F32)
        dv = jnp.zeros(k.shape, F32)
        for h in range(2):
            p = jnp.exp(mm_nt(k, q_heads[h]) - lses[h])
            dv = dv + mm(p.astype(BF), do_heads[h])
            ds = (p * (mm_nt(v, do_heads[h]) - deltas[h])).astype(BF)
            dk = dk + mm(ds, q_heads[h])
            dq_t[h] = dq_t[h] + mm(k_t[h * HD : (h + 1) * HD, :], ds)
        dk_refs[i][...] = dk.astype(BF)
        dv_refs[i][...] = dv.astype(BF)
    dq_ref[...] = (jnp.concatenate(dq_t, axis=0).T * score_scale).astype(BF)


def attend_back_call(q, do_own, do_got, o_own, o_send, lse, pieces):
    rows, width = q.shape
    pairs = width // 128
    n = pieces[0].shape[0]
    half = rows // 2
    full = pl.BlockSpec((rows, 128), lambda p: (0, p))
    part = pl.BlockSpec((half, 128), lambda p: (0, p))
    k_spec = pl.BlockSpec((n, 128), lambda p: (0, p))
    v_spec = pl.BlockSpec((n, 128), lambda p: (0, p + pairs))
    out = pl.pallas_call(
        attend_back_kernel,
        grid=(pairs,),
        in_specs=[full, part, part, part, part, pl.BlockSpec((1, 2, rows), lambda p: (p, 0, 0))]
        + [k_spec] * 4
        + [v_spec] * 4,
        out_specs=[full] + [k_spec] * 8,
        out_shape=(jax.ShapeDtypeStruct((rows, width), BF),)
        + (jax.ShapeDtypeStruct((n, width), BF),) * 8,
        compiler_params=params(40),
        cost_estimate=pl.CostEstimate(
            flops=40 * rows * 4 * n * width,
            bytes_accessed=8 * MIB,
            transcendentals=pairs * 2 * rows * 4 * n,
        ),
        name="attend_back",
    )(q, do_own, do_got, o_own, o_send, lse, *pieces, *pieces)
    return out[0], out[1:5], out[5:9]


def ffn_kernel(clips, *refs):
    o_own, o_got = refs[0:clips], refs[clips : 2 * clips]
    x_ref, gy_ref, wo_ref, up_ref, dn_ref, b1_ref, rows_ref = refs[2 * clips : 2 * clips + 7]
    outs = refs[2 * clips + 7 :]
    y_ref, d1_ref = outs[0:2]
    do_own, do_send = outs[2 : 2 + clips], outs[2 + clips : 2 + 2 * clips]
    dup_ref, ddn_ref, dwo_ref, sums_ref, db1_ref = outs[2 + 2 * clips : 7 + 2 * clips]
    proj_scr, c_scr, ct_scr, gyt_scr, y_scr, dc_scr = outs[7 + 2 * clips :]
    half = o_own[0].shape[0]
    j = pl.program_id(0)
    gain, shift = rows_ref[0:1, :], rows_ref[1:2, :]
    bias_o, bias_2 = rows_ref[2:3, :], rows_ref[3:4, :]

    @pl.when(j == 0)
    def _():
        for i in range(clips):
            rows = pl.ds(i * half, half)
            proj = mm_nt(o_own[i][...], wo_ref[0]) + mm_nt(o_got[i][...], wo_ref[1]) + bias_o
            proj_scr[rows, :] = proj
            normed, _ = normed_rows(x_ref[rows, :].astype(F32) + proj)
            c_scr[rows, :] = (normed * gain + shift).astype(BF)
        ct_scr[...] = c_scr[...].T
        gyt_scr[...] = gy_ref[...].T
        y_scr[...] = jnp.zeros_like(y_scr)
        dc_scr[...] = jnp.zeros_like(dc_scr)

    up = up_ref[0]
    dn = dn_ref[0]
    f = mm(c_scr[...], up) + b1_ref[0]
    cdf = 0.5 * (1.0 + lax.erf(f * root_half))
    u = (f * cdf).astype(BF)
    slope = cdf + f * (density_scale * jnp.exp(-0.5 * f * f))
    df = mm(gy_ref[...], dn) * slope
    dfb = df.astype(BF)
    db1_ref[0] = jnp.sum(df, axis=0, keepdims=True)
    y_scr[...] += mm_nt(u, dn)
    dc_scr[...] += mm_nt(dfb, up)
    ddn_ref[0] = mm(gyt_scr[...], u).astype(BF)
    dup_ref[0] = mm(ct_scr[...], dfb).astype(BF)

    @pl.when(j == pl.num_programs(0) - 1)
    def _():
        sum_gain = jnp.zeros_like(gain)
        sum_dc = jnp.zeros_like(gain)
        sum_dh = jnp.zeros_like(gain)
        dwo0 = jnp.zeros(wo_ref.shape[1:], F32)
        dwo1 = jnp.zeros(wo_ref.shape[1:], F32)
        for i in range(clips):
            rows = pl.ds(i * half, half)
            proj = proj_scr[rows, :]
            normed, inv = normed_rows(x_ref[rows, :].astype(F32) + proj)
            y_ref[rows, :] = (proj + y_scr[rows, :] + bias_2).astype(BF)
            dc = dc_scr[rows, :]
            t = dc * gain
            d1 = inv * (t - row_mean(t) - normed * row_mean(t * normed))
            d1_ref[rows, :] = d1
            dh = gy_ref[rows, :].astype(F32) + d1
            dy = dh.astype(BF)
            sum_gain = sum_gain + jnp.sum(dc * normed, axis=0, keepdims=True)
            sum_dc = sum_dc + jnp.sum(dc, axis=0, keepdims=True)
            sum_dh = sum_dh + jnp.sum(dh, axis=0, keepdims=True)
            do_own[i][...] = mm(dy, wo_ref[0]).astype(BF)
            do_send[i][...] = mm(dy, wo_ref[1]).astype(BF)
            dy_t = dy.T
            dwo0 = dwo0 + mm(dy_t, o_own[i][...])
            dwo1 = dwo1 + mm(dy_t, o_got[i][...])
        dwo_ref[0] = dwo0.astype(BF)
        dwo_ref[1] = dwo1.astype(BF)
        sums_ref[0:1, :] = sum_gain
        sums_ref[1:2, :] = sum_dc
        sums_ref[2:3, :] = sum_dh
        sums_ref[3:8, :] = jnp.zeros((5, sums_ref.shape[1]), F32)


def ffn_call(o_own, o_got, x, gy, wide, b1, rows):
    clips = len(o_own)
    tokens, dim = x.shape
    half, width = o_own[0].shape
    hidden = b1.shape[1]
    block = 512
    per = hidden // block
    resident = lambda shape: pl.BlockSpec(
        shape, lambda j: (0,) * len(shape), pipeline_mode=pl.Buffered(1)
    )
    up_spec = pl.BlockSpec((1, dim, block), lambda j: (j // per, 0, j % per))
    out = pl.pallas_call(
        functools.partial(ffn_kernel, clips),
        grid=(2 * per,),
        in_specs=[resident((half, width))] * (2 * clips)
        + [
            resident((tokens, dim)),
            resident((tokens, dim)),
            pl.BlockSpec(
                (2, dim, width), lambda j: (0, 0, 2 * hidden // width), pipeline_mode=pl.Buffered(1)
            ),
            up_spec,
            pl.BlockSpec((1, dim, block), lambda j: (j // per, 0, j % per + per)),
            pl.BlockSpec((1, 1, block), lambda j: (j, 0, 0)),
            resident((8, dim)),
        ],
        out_specs=[resident((tokens, dim))] * 2
        + [resident((half, width))] * (2 * clips)
        + [
            up_spec,
            up_spec,
            resident((2, dim, width)),
            resident((8, dim)),
            pl.BlockSpec((1, 1, block), lambda j: (j, 0, 0)),
        ],
        out_shape=(
            jax.ShapeDtypeStruct((tokens, dim), BF),
            jax.ShapeDtypeStruct((tokens, dim), F32),
        )
        + (jax.ShapeDtypeStruct((half, width), BF),) * (2 * clips)
        + (
            jax.ShapeDtypeStruct((2, dim, hidden), BF),
            jax.ShapeDtypeStruct((2, dim, hidden), BF),
            jax.ShapeDtypeStruct((2, dim, width), BF),
            jax.ShapeDtypeStruct((8, dim), F32),
            jax.ShapeDtypeStruct((2 * per, 1, block), F32),
        ),
        scratch_shapes=[
            pltpu.VMEM((tokens, dim), F32),
            pltpu.VMEM((tokens, dim), BF),
            pltpu.VMEM((dim, tokens), BF),
            pltpu.VMEM((dim, tokens), BF),
            pltpu.VMEM((tokens, dim), F32),
            pltpu.VMEM((tokens, dim), F32),
        ],
        compiler_params=params(56),
        cost_estimate=pl.CostEstimate(
            flops=24 * tokens * dim * hidden, bytes_accessed=30 * MIB, transcendentals=0
        ),
        name="feed_forward",
    )(*o_own, *o_got, x, gy, wide, wide, wide, b1.reshape(2 * per, 1, block), rows)
    y, d1 = out[:2]
    do_own, do_send = out[2 : 2 + clips], out[2 + clips : 2 + 2 * clips]
    dup, ddn, dwo, sums, db1 = out[2 + 2 * clips :]
    return y, d1, do_own, do_send, dup, ddn, dwo, sums, db1.reshape(2, hidden)


def back_kernel(clips, *refs):
    own_refs, got_refs = refs[0:clips], refs[clips : 2 * clips]
    dq_refs = refs[2 * clips : 3 * clips]
    dk_refs = refs[3 * clips : 4 * clips]
    dv_refs = refs[4 * clips : 5 * clips]
    w_ref, rows_ref = refs[5 * clips : 5 * clips + 2]
    outs = refs[5 * clips + 2 :]
    da_own, da_send = outs[0:clips], outs[clips : 2 * clips]
    dw_ref, sums_ref, bias_ref = outs[2 * clips : 2 * clips + 3]
    acc_scr = outs[2 * clips + 3]
    half = own_refs[0].shape[0]
    width = dq_refs[0].shape[1]
    gain, shift = rows_ref[0:1, :], rows_ref[1:2, :]
    sum_gain = jnp.zeros_like(gain)
    sum_da = jnp.zeros_like(gain)
    sum_q = jnp.zeros((1, width), F32)
    sum_v = jnp.zeros((1, width), F32)
    for i in range(clips):
        for s, (x_ref, da_ref) in enumerate(((own_refs[i], da_own[i]), (got_refs[i], da_send[i]))):
            rows = pl.ds(s * half, half)
            normed, _ = normed_rows(x_ref[...].astype(F32))
            act = normed * gain + shift
            act_t = act.astype(BF).T
            da = jnp.zeros(act.shape, F32)
            for j, ref in enumerate((dq_refs[i], dk_refs[i], dv_refs[i])):
                g = ref[rows, :]
                cols = slice(j * width, (j + 1) * width)
                da = da + mm_nt(g, w_ref[:, cols])
                part = mm(act_t, g)
                if i == 0 and s == 0:
                    acc_scr[:, cols] = part
                else:
                    acc_scr[:, cols] += part
                if j == 0:
                    sum_q = sum_q + jnp.sum(g.astype(F32), axis=0, keepdims=True)
                if j == 2:
                    sum_v = sum_v + jnp.sum(g.astype(F32), axis=0, keepdims=True)
            da_ref[...] = da.astype(BF)
            sum_gain = sum_gain + jnp.sum(da * normed, axis=0, keepdims=True)
            sum_da = sum_da + jnp.sum(da, axis=0, keepdims=True)
    dw_ref[...] = acc_scr[...].astype(BF)
    sums_ref[0:1, :] = sum_gain
    sums_ref[1:2, :] = sum_da
    sums_ref[2:8, :] = jnp.zeros((6, sums_ref.shape[1]), F32)
    bias_ref[0:1, :] = sum_q
    bias_ref[1:2, :] = sum_v
    bias_ref[2:8, :] = jnp.zeros((6, width), F32)


def back_call(x_own, x_got, dq, dk, dv, weight, rows):
    clips = len(x_own)
    half, dim = x_own[0].shape
    width = dq[0].shape[1]
    out = pl.pallas_call(
        functools.partial(back_kernel, clips),
        out_shape=(jax.ShapeDtypeStruct((half, dim), BF),) * (2 * clips)
        + (
            jax.ShapeDtypeStruct(weight.shape, BF),
            jax.ShapeDtypeStruct((8, dim), F32),
            jax.ShapeDtypeStruct((8, width), F32),
        ),
        scratch_shapes=[pltpu.VMEM(weight.shape, F32)],
        compiler_params=params(48),
        cost_estimate=pl.CostEstimate(
            flops=8 * clips * half * weight.size, bytes_accessed=16 * MIB, transcendentals=0
        ),
        name="project_back",
    )(*x_own, *x_got, *dq, *dk, *dv, weight, rows)
    return out[:clips], out[clips : 2 * clips], out[2 * clips], out[2 * clips + 1], out[2 * clips + 2]


MESH_ID = pl.DeviceIdType.MESH


def flip(v, bit):
    step = 1 << bit
    return v + step - 2 * step * ((v // step) % 2)


def remote(src, dst, send, recv, device):
    return pltpu.make_async_remote_copy(
        src_ref=src, dst_ref=dst, send_sem=send, recv_sem=recv, device_id=device, device_id_type=MESH_ID
    )


def partners():
    d, c, t = lax.axis_index("dp"), lax.axis_index("ctx"), lax.axis_index("tensor")
    return d, c, t, {
        "x": (d, c, 1 - t),
        "z1": (d, flip(c, 0), t),
        "z2": (d, flip(c, 1), t),
        "core": (flip(d, 0), c, t),
        "y": (flip(d, 1), c, t),
        "swap": (flip(d, 0), flip(c, 1), t),
    }


def greet(devices):
    barrier = pltpu.get_barrier_semaphore()
    for device in devices:
        pl.semaphore_signal(barrier, inc=1, device_id=device, device_id_type=MESH_ID)
    pl.semaphore_wait(barrier, len(devices))


class Plan:
    def __init__(self, steps):
        self.steps = sorted(steps, key=lambda s: s[0])

    def pump(self, now):
        while self.steps and self.steps[0][0] <= now:
            self.steps.pop(0)[1]()


def pick_matrix(out_rows, per, shard):
    rows = shard * (out_rows // per)
    r = lax.broadcasted_iota(jnp.int32, (out_rows, rows), 0)
    k = lax.broadcasted_iota(jnp.int32, (out_rows, rows), 1)
    return jnp.where(k == (r // per) * shard + r % per, 1.0, 0.0).astype(BF)


def both_heads(v):
    return jnp.concatenate([pick(v, h) for h in range(2)], axis=0)


def fold_heads(v_t, rows):
    return jnp.concatenate([v_t[:HD, :rows], v_t[HD:, rows:]], axis=0).T


def attend_pair(q, kvs, s_scr):
    rows = q.shape[0]
    n = kvs[0].shape[0]
    qq = both_heads(q)
    tops = []
    for i, kv in enumerate(kvs):
        s = mm_nt(kv[:, 0:128], qq)
        s_scr[pl.ds(i * n, n), :] = s
        tops.append(jnp.max(s, axis=0, keepdims=True))
    top = functools.reduce(jnp.maximum, tops)
    e = jnp.exp(s_scr[...] - top)
    total = jnp.sum(e, axis=0, keepdims=True)
    v = jnp.concatenate([kv[:, 128:256] for kv in kvs], axis=0)
    mix = mm(v.T, e.astype(BF)) / total
    return fold_heads(mix, rows).astype(BF), top + jnp.log(total)


Y_FIRST = (2,)
SWAPS_FIRST = (0,)
PROJECT_AT = {0: (0,), 2: (1,), 4: (2,)}
POINTS = {
    "s0": (0,),
    "f1": (0,),
    "w0": (0,),
    "z0": (1,),
    "c0": (-3, 1, -1, 3),
    "p0": (6, 4),
    "u0": (6, 3, 0),
    "u1": (6,),
    "c1": (2,),
    "p1": (3, 5, 6, 4),
    "u2": (2, -2, -4),
    "u3": (3,),
    "c2": (2, 0, 1),
    "u6": (1, 4, 5),
    "u7": (6,),
    "u8": (3,),
    "g": (4, 5, 2),
    "g0": (5, 1),
    "g1": (4, 2),
    "g2": (5,),
    "g5": (6,),
}


def start_kernel(
    x_hbm,
    gy_hbm,
    qkv_in,
    wo_in,
    up_in,
    dn_in,
    gains_in,
    shifts_in,
    qv_in,
    ub_in,
    x_out,
    wf_out,
    ws_ref,
    rows_ref,
    q_out,
    kv_out,
    own_ref,
    send_ref,
    lse_ref,
    y_ref,
    d1_ref,
    do_own,
    do_send,
    up_hbm,
    dn_hbm,
    dwo_ref,
    sums_ref,
    db1_ref,
    x_in,
    gy_in,
    x_home,
    gy_home,
    first,
    second,
    turn_scr,
    x_ref,
    wf_ref,
    q_ref,
    kv_ref,
    gy_ref,
    got_ref,
    s_scr,
    w_scr,
    wo_scr,
    g_scr,
    proj_scr,
    c_scr,
    ct_scr,
    gyt_scr,
    y_scr,
    dc_scr,
    b1_scr,
    local_sem,
    load_sem,
    w_sem,
    g_sem,
    save_sem,
    swap_s,
    swap_r,
    gy_s,
    gy_r,
    xe_s,
    xe_r,
    kv_s,
    kv_r,
    oe_s,
    oe_r,
    f_s,
    f_r,
    s_s,
    s_r,
):
    clips, half, dim = x_home.shape
    shard = first.shape[0]
    chunks = second.shape[0]
    width = q_ref.shape[2]
    pairs = width // 128
    d, c, t, dev = partners()
    me = pl.multiple_of((d * 4 + c) * shard, shard)
    me_z2 = pl.multiple_of((d * 4 + flip(c, 1)) * shard, shard)
    quad = pl.multiple_of(d * 4 * shard, 4 * shard)
    quad_y = pl.multiple_of(flip(d, 1) * 4 * shard, 4 * shard)
    moves = (d % 2) != (c // 2)
    x_loads = [
        pltpu.make_async_copy(x_hbm.at[i], x_in.at[i], load_sem.at[i]) for i in range(clips)
    ]
    gy_load = pltpu.make_async_copy(gy_hbm, gy_in, load_sem.at[clips])
    for cp in x_loads:
        cp.start()
    gy_load.start()
    greet([dev[k] for k in ("x", "z1", "z2", "core", "y", "swap")])

    for j in range(3):
        first[:, j * width : (j + 1) * width] = qkv_in[j].astype(BF)
    turn_scr[...] = jnp.zeros_like(turn_scr)
    turn_scr[0:2, 0:shard] = gains_in[...]
    turn_scr[2:6, 0:shard] = shifts_in[...]
    turn_scr[...] = turn_scr[...].T
    for j in range(2):
        at = 8 + j * 2 * pairs
        turn_scr[0 : qv_in.shape[1], at : at + 2 * pairs] = qv_in[j]
    first[:, 3 * width :] = turn_scr[:shard].astype(BF)

    place_f = pltpu.make_async_copy(first, wf_ref.at[pl.ds(me, shard)], local_sem.at[0])
    place_s = pltpu.make_async_copy(second, ws_ref.at[:, 0, pl.ds(me, shard)], local_sem.at[1])
    place_f.start()
    keep_x = pltpu.make_async_copy(x_home, x_ref.at[0], local_sem.at[2])
    keep_gy = pltpu.make_async_copy(gy_home, gy_ref, local_sem.at[3])

    swaps = [
        remote(x_home.at[i], x_ref.at[0, i], swap_s.at[i], swap_r.at[i], dev["swap"])
        for i in range(clips)
    ]
    swap_gy = remote(gy_home, gy_ref, gy_s.at[0], gy_r.at[0], dev["swap"])

    def first_stage(i, src, rows, count, device):
        block = wf_ref.at[pl.ds(rows, count)]
        return remote(src if src is not None else block, block, f_s.at[i], f_r.at[i], device)

    f_stages = [
        [first_stage(0, first, me, shard, dev["z2"])],
        [first_stage(1, None, me, shard, dev["z1"]), first_stage(2, None, me_z2, shard, dev["z1"])],
        [first_stage(3, None, quad, 4 * shard, dev["y"])],
        [
            first_stage(4, None, quad, 4 * shard, dev["core"]),
            first_stage(5, None, quad_y, 4 * shard, dev["core"]),
        ],
    ]

    def second_stages(ch):
        def own(i, src, rows, count, device):
            block = ws_ref.at[ch, 0, pl.ds(rows, count)]
            return remote(src if src is not None else block, block, s_s.at[ch, i], s_r.at[ch, i], device)

        def both(i, rows, device):
            block = ws_ref.at[ch, :, pl.ds(rows, 4 * shard)]
            return remote(block, block, s_s.at[ch, i], s_r.at[ch, i], device)

        def over_x(i, rows):
            rows = pl.ds(rows, 4 * shard)
            return remote(
                ws_ref.at[ch, 0, rows], ws_ref.at[ch, 1, rows], s_s.at[ch, i], s_r.at[ch, i], dev["x"]
            )

        along_z = [
            [own(0, second.at[ch], me, shard, dev["z2"])],
            [own(1, None, me, shard, dev["z1"]), own(2, None, me_z2, shard, dev["z1"])],
        ]
        if ch in Y_FIRST:
            plane = [[own(4, None, quad, 4 * shard, dev["y"])], [over_x(3, quad), over_x(7, quad_y)]]
        else:
            plane = [[over_x(3, quad)], [both(4, quad, dev["y"])]]
        return along_z + plane + [[both(5, quad, dev["core"]), both(6, quad_y, dev["core"])]]

    def start(copies):
        for cp in copies:
            cp.start()

    def wait(copies):
        for cp in copies:
            cp.wait()

    s_stages = [second_stages(ch) for ch in range(chunks)]
    reached = [-1] * chunks

    def advance(point):
        for ch in POINTS.get(point, ()):
            if ch < 0:
                special[ch]()
                continue
            if reached[ch] >= len(s_stages[ch]):
                continue
            if reached[ch] >= 0:
                wait(s_stages[ch][reached[ch]])
            reached[ch] += 1
            if reached[ch] < len(s_stages[ch]):
                start(s_stages[ch][reached[ch]])
    def row_copy(j, i, src, dst, device):
        return remote(x_ref.at[src, i], x_ref.at[dst, i], xe_s.at[j, i], xe_r.at[j, i], device)

    own_x = [row_copy(0, i, 0, 1, dev["x"]) for i in range(clips)]
    own_z = [row_copy(1, i, 0, 2, dev["z1"]) for i in range(clips)]
    far_x = [row_copy(2, i, 2, 3, dev["x"]) for i in range(clips)]

    def swap_start(clip_list):
        @pl.when(moves)
        def _():
            for i in clip_list:
                swaps[i].start()

    def swap_done(i):
        @pl.when(moves)
        def _():
            swaps[i].wait()

        own_z[i].start()
        own_x[i].start()

    def far_start(i):
        own_z[i].wait()
        far_x[i].start()

    def gy_start():
        @pl.when(moves)
        def _():
            swap_gy.start()

    special = {
        -1: functools.partial(far_start, 1),
        -2: functools.partial(far_start, 2),
        -3: functools.partial(swap_done, 2),
        -4: gy_start,
    }

    start(f_stages[0])
    for i in range(clips):
        x_loads[i].wait()
        x_home[i] = x_in[i].astype(BF)
        if i in SWAPS_FIRST:
            swap_start([i])
    gy_load.wait()
    gy_home[...] = gy_in[...].astype(BF)
    for b in range((chunks - 1) // 2):
        cols = slice(b * second.shape[2], (b + 1) * second.shape[2])
        second[b] = up_in[:, cols].astype(BF)
        second[(chunks - 1) // 2 + b] = dn_in[:, cols].astype(BF)
    turn_scr[...] = jnp.zeros_like(turn_scr)
    turn_scr[0 : ub_in.shape[0], 0 : ub_in.shape[1]] = ub_in[...]
    second[chunks - 1, :, :width] = wo_in[...].astype(BF)
    second[chunks - 1, :, width:] = turn_scr[:shard].astype(BF)
    place_s.start()

    @pl.when(jnp.logical_not(moves))
    def _():
        keep_x.start()
        keep_gy.start()
        keep_x.wait()
        keep_gy.wait()

    place_f.wait()
    place_s.wait()
    advance("s0")
    wait(f_stages[0])
    start(f_stages[1])
    advance("f1")
    wait(f_stages[1])
    start(f_stages[2])
    swap_start([i for i in range(clips) if i not in SWAPS_FIRST])
    advance("f2")
    swap_done(0)
    advance("w0")
    wait(f_stages[2])
    start(f_stages[3])
    advance("f3")
    far_start(0)
    advance("z0")
    swap_done(1)
    advance("w1")
    wait(f_stages[3])
    advance("f4")

    extra = wf_ref[:, 3 * width : 3 * width + 128]
    rows_t = extra.astype(F32).T
    rows_ref[0:8, :] = rows_t[0:8, :]
    shards = dim // shard
    qv = mm(pick_matrix(HD, HD // shards, shard), extra).T
    biases = []
    for r in range(2):
        biases.append(
            jnp.concatenate(
                [qv[8 + r * 2 * pairs + h : 9 + r * 2 * pairs + h, :] for h in range(2 * pairs)], axis=1
            )
        )
    gain, shift = rows_t[0:1, :], rows_t[2:3, :]

    def project(i, s):
        normed, _ = normed_rows(x_ref[s, i].astype(F32))
        act = (normed * gain + shift).astype(BF)
        rows = pl.ds((s % 2) * half, half)
        if s < 2:
            out = mm(act, wf_ref[:, : 3 * width])
            q = (out[:, :width] + biases[0]).astype(BF)
            q_ref[i, rows, :] = (q.astype(F32) * score_scale).astype(BF)
            out = out[:, width:]
        else:
            out = mm(act, wf_ref[:, width : 3 * width])
        v = out[:, width:] + biases[1]
        for p in range(pairs):
            cols = slice(p * 128, (p + 1) * 128)
            kv_ref[s // 2 * 2, i, p, rows, 0:128] = out[:, cols].astype(BF)
            kv_ref[s // 2 * 2, i, p, rows, 128:256] = v[:, cols].astype(BF)

    def kv_copy(j, i):
        return remote(
            kv_ref.at[2 * j, i], kv_ref.at[2 * j + 1, i], kv_s.at[j, i], kv_r.at[j, i], dev["core"]
        )

    units = [(i, p) for i in range(clips) for p in range(pairs)]
    to_core = [[kv_copy(j, i) for j in range(2)] for i in range(clips)]

    o_copies = [
        remote(send_ref.at[i], got_ref.at[i], oe_s.at[i], oe_r.at[i], dev["x"]) for i in range(clips)
    ]

    def project_clip(i):
        project(i, 0)
        own_x[i].wait()
        project(i, 1)
        to_core[i][0].start()
        advance(f"c{i}")
        project(i, 2)
        far_x[i].wait()
        project(i, 3)
        to_core[i][1].start()
        advance(f"p{i}")

    for n, (i, p) in enumerate(units):
        for clip in PROJECT_AT.get(n, ()):
            project_clip(clip)
        if p == 0:
            wait(to_core[i])
        cols = pl.ds(p * 128, 128)
        o, lse = attend_pair(
            q_ref[i, :, cols],
            [kv_ref.at[s, i, p] for s in range(4)],
            s_scr,
        )
        own_ref[i, :, cols] = o[:half]
        send_ref[i, :, cols] = o[half:]
        lse_ref[i, p] = lse
        advance(f"u{n}")
        if p == pairs - 1:
            o_copies[i].start()

    per = (chunks - 1) // 2
    block = ws_ref.shape[3]
    tokens = clips * half
    gain, shift = rows_ref[1:2, :], rows_ref[3:4, :]
    bias_o, bias_2 = rows_ref[4:5, :], rows_ref[5:6, :]

    def finish_chunk(ch):
        while reached[ch] < len(s_stages[ch]):
            if reached[ch] >= 0:
                wait(s_stages[ch][reached[ch]])
            reached[ch] += 1
            if reached[ch] < len(s_stages[ch]):
                start(s_stages[ch][reached[ch]])

    @pl.when(moves)
    def _():
        swap_gy.wait()

    saves = [
        pltpu.make_async_copy(src, dst, save_sem.at[n])
        for n, (src, dst) in enumerate(
            ((kv_ref, kv_out), (x_ref, x_out), (wf_ref, wf_out), (q_ref, q_out))
        )
    ]
    start(saves)
    gyt_scr[...] = gy_ref[...].reshape(tokens, dim).T
    finish_chunk(2 * per)
    load_wo = pltpu.make_async_copy(ws_ref.at[2 * per], wo_scr, local_sem.at[1])
    load_wo.start()
    load_wo.wait()
    taken = pick_matrix(128, 128 // shards, shard)
    for s in range(2):
        cols = mm(taken, wo_scr[s, :, width : width + 128]).T
        for b in range(per):
            b1_scr[s * per + b] = jnp.concatenate(
                [cols[b * 4 + r : b * 4 + r + 1, :] for r in range(4)], axis=1
            )
    for i in range(clips):
        rows = pl.ds(i * half, half)
        wait([o_copies[i]])
        proj = (
            mm_nt(own_ref[i], wo_scr[0, :, :width])
            + mm_nt(got_ref[i], wo_scr[1, :, :width])
            + bias_o
        )
        proj_scr[rows, :] = proj
        normed, _ = normed_rows(x_ref[0, i].astype(F32) + proj)
        c_scr[rows, :] = (normed * gain + shift).astype(BF)
    ct_scr[...] = c_scr[...].T
    advance("g")

    def load_block(b, s, r):
        return pltpu.make_async_copy(ws_ref.at[r * per + b, s], w_scr.at[s, r], w_sem.at[s, r])

    def store_block(b, s, r):
        out = dn_hbm if r else up_hbm
        return pltpu.make_async_copy(g_scr.at[s, r], out.at[b, s], g_sem.at[s, r])

    for b in range(per):
        finish_chunk(b)
        finish_chunk(per + b)
        for s in range(2):
            start([load_block(b, s, r) for r in range(2)])
        for s in range(2):
            wait([load_block(b, s, r) for r in range(2)])
            up, dn = w_scr[s, 0], w_scr[s, 1]
            f = mm(c_scr[...], up) + b1_scr[s * per + b]
            cdf = 0.5 * (1.0 + lax.erf(f * root_half))
            u = (f * cdf).astype(BF)
            slope = cdf + f * (density_scale * jnp.exp(-0.5 * f * f))
            df = mm(gy_ref[...].reshape(tokens, dim), dn) * slope
            dfb = df.astype(BF)
            db1_ref[s * per + b] = jnp.sum(df, axis=0, keepdims=True)
            if b + s:
                y_scr[...] += mm_nt(u, dn)
                dc_scr[...] += mm_nt(dfb, up)
            else:
                y_scr[...] = mm_nt(u, dn)
                dc_scr[...] = mm_nt(dfb, up)
            if b:
                wait([store_block(b - 1, s, r) for r in range(2)])
            g_scr[s, 0] = mm(ct_scr[...], dfb).astype(BF)
            g_scr[s, 1] = mm(gyt_scr[...], u).astype(BF)
            start([store_block(b, s, r) for r in range(2)])
            advance(f"g{2 * b + s}")

    sum_gain = jnp.zeros((1, dim), F32)
    sum_dc = jnp.zeros((1, dim), F32)
    sum_dh = jnp.zeros((1, dim), F32)
    sum_gy = jnp.zeros((1, dim), F32)
    dwo = [jnp.zeros((dim, width), F32) for _ in range(2)]
    for i in range(clips):
        rows = pl.ds(i * half, half)
        proj = proj_scr[rows, :]
        normed, inv = normed_rows(x_ref[0, i].astype(F32) + proj)
        y_ref[i] = (proj + y_scr[rows, :] + bias_2).astype(BF)
        dc = dc_scr[rows, :]
        t_rows = dc * gain
        d1 = inv * (t_rows - row_mean(t_rows) - normed * row_mean(t_rows * normed))
        d1_ref[rows, :] = d1
        gy_rows = gy_ref[i].astype(F32)
        dh = gy_rows + d1
        dy = dh.astype(BF)
        sum_gain = sum_gain + jnp.sum(dc * normed, axis=0, keepdims=True)
        sum_dc = sum_dc + jnp.sum(dc, axis=0, keepdims=True)
        sum_dh = sum_dh + jnp.sum(dh, axis=0, keepdims=True)
        sum_gy = sum_gy + jnp.sum(gy_rows, axis=0, keepdims=True)
        do_own[i] = mm(dy, wo_scr[0, :, :width]).astype(BF)
        do_send[i] = mm(dy, wo_scr[1, :, :width]).astype(BF)
        dy_t = dy.T
        dwo = [dwo[0] + mm(dy_t, own_ref[i]), dwo[1] + mm(dy_t, got_ref[i])]
    for s in range(2):
        dwo_ref[s, :, :width] = dwo[s].astype(BF)
    dwo_ref[:, :, width:] = jnp.zeros((2, dim, block - width), BF)
    for r, row in enumerate((sum_gain, sum_dc, sum_dh, sum_gy)):
        sums_ref[r : r + 1, :] = row
    sums_ref[4:8, :] = jnp.zeros((4, dim), F32)
    for s in range(2):
        wait([store_block(per - 1, s, r) for r in range(2)])
    wait(saves)


def start_call(x, gy, qkv, wo, up, dn, gains, shifts, qv, ub):
    clips, half, dim = x.shape
    shard, width = wo.shape
    block = 512
    per = up.shape[1] // block
    chunks = 2 * per + 1
    pairs = width // 128
    tokens = clips * half
    columns = 3 * width + 128
    any_spec = pl.BlockSpec(memory_space=pl.ANY)
    vmem = pl.BlockSpec(memory_space=pltpu.VMEM)
    dma = pltpu.SemaphoreType.DMA
    both = lambda *shape: [dma(shape), dma(shape)]
    shaped = jax.ShapeDtypeStruct
    head = shaped((clips, half, width), BF)
    return pl.pallas_call(
        start_kernel,
        in_specs=[any_spec] * 2 + [vmem] * 8,
        out_specs=[any_spec] * 3 + [vmem] + [any_spec] * 2 + [vmem] * 7 + [any_spec] * 2 + [vmem] * 3,
        out_shape=(
            shaped((4, clips, half, dim), BF),
            shaped((dim, columns), BF),
            shaped((chunks, 2, dim, block), BF),
            shaped((8, dim), F32),
            shaped((clips, 2 * half, width), BF),
            shaped((4, clips, pairs, 2 * half, 256), BF),
            head,
            head,
            shaped((clips, pairs, 1, 4 * half), F32),
            shaped((clips, half, dim), BF),
            shaped((tokens, dim), F32),
            head,
            head,
            shaped((per, 2, dim, block), BF),
            shaped((per, 2, dim, block), BF),
            shaped((2, dim, block), BF),
            shaped((8, dim), F32),
            shaped((2 * per, 1, block), F32),
        ),
        scratch_shapes=[
            pltpu.VMEM((clips, half, dim), F32),
            pltpu.VMEM((clips, half, dim), F32),
            pltpu.VMEM((clips, half, dim), BF),
            pltpu.VMEM((clips, half, dim), BF),
            pltpu.VMEM((shard, columns), BF),
            pltpu.VMEM((chunks, shard, block), BF),
            pltpu.VMEM((128, 128), F32),
            pltpu.VMEM((4, clips, half, dim), BF),
            pltpu.VMEM((dim, columns), BF),
            pltpu.VMEM((clips, 2 * half, width), BF),
            pltpu.VMEM((4, clips, pairs, 2 * half, 256), BF),
            pltpu.VMEM((clips, half, dim), BF),
            pltpu.VMEM((clips, half, width), BF),
            pltpu.VMEM((8 * half, 4 * half), F32),
            pltpu.VMEM((2, 2, dim, block), BF),
            pltpu.VMEM((2, dim, block), BF),
            pltpu.VMEM((2, 2, dim, block), BF),
            pltpu.VMEM((tokens, dim), F32),
            pltpu.VMEM((tokens, dim), BF),
            pltpu.VMEM((dim, tokens), BF),
            pltpu.VMEM((dim, tokens), BF),
            pltpu.VMEM((tokens, dim), F32),
            pltpu.VMEM((tokens, dim), F32),
            pltpu.VMEM((2 * per, 1, block), F32),
            dma((4,)),
            dma((clips + 1,)),
            dma((2, 2)),
            dma((2, 2)),
            dma((4,)),
            *both(clips),
            *both(1),
            *both(3, clips),
            *both(2, clips),
            *both(clips),
            *both(6),
            *both(chunks, 8),
        ],
        compiler_params=pltpu.CompilerParams(
            collective_id=1, has_side_effects=True, vmem_limit_bytes=60 * MIB
        ),
        cost_estimate=pl.CostEstimate(
            flops=30 * 10**9, bytes_accessed=80 * MIB, transcendentals=11 * 10**6
        ),
        name="start_attend",
    )(x, gy, qkv, wo, up, dn, gains, shifts, qv, ub)


X_FIRST = (0,)
ORDER = (
    ("g", 5), ("g", 6), ("y", 0), ("g", 1), ("g", 0), ("g", 5), ("g", 4), ("g", 3),
    ("g", 6), ("u", 0), ("g", 0), ("g", 3), ("u", 1), ("u", 2), ("g", 1), ("g", 5),
    ("u", 6), ("g", 6), ("u", 3), ("b", 0), ("g", 5), ("u", 4), ("g", 6), ("u", 5),
    ("g", 2), ("g", 3), ("g", 6), ("g", 0), ("f", 0), ("g", 5), ("g", 1), ("u", 8),
    ("b", 1), ("g", 1), ("g", 4), ("e", 0), ("g", 3), ("u", 7), ("g", 0), ("g", 6),
    ("f", 1), ("g", 5), ("g", 2), ("b", 2), ("g", 0), ("g", 1), ("v", 0), ("h", 0),
    ("e", 1), ("f", 2), ("g", 3), ("g", 4), ("h", 0), ("g", 1), ("v", 0), ("v", 0),
    ("e", 2), ("h", 0), ("g", 2), ("v", 0), ("h", 0), ("g", 3), ("v", 0), ("g", 2),
    ("g", 0), ("g", 4), ("g", 2), ("v", 0), ("g", 4), ("h", 0), ("g", 2), ("g", 4),
)


def end_kernel(
    q_ref,
    kv_hbm,
    own_ref,
    send_ref,
    lse_ref,
    do_own_ref,
    do_send_ref,
    x_hbm,
    wf_hbm,
    rows_ref,
    d1_hbm,
    y_ref,
    up_hbm,
    dn_hbm,
    wo_hbm,
    sums_ref,
    db1_ref,
    yh_ref,
    dh_ref,
    g2_ref,
    g1_ref,
    vec_ref,
    kv_scr,
    x_scr,
    wf_scr,
    d1_scr,
    do_got,
    core_got,
    dq_scr,
    acc_scr,
    dw_scr,
    da_own,
    da_send,
    da_got,
    far_scr,
    far_got,
    delta_scr,
    loc_scr,
    rc_scr,
    ry_scr,
    rx_scr,
    rz1_scr,
    rz2_scr,
    c1_scr,
    y1_scr,
    p1_scr,
    q1_scr,
    vs_scr,
    vr_scr,
    kv_sem,
    in_sem,
    loc_sem,
    keep_sem,
    do_s,
    do_r,
    y_s,
    y_r,
    dc_s,
    dc_r,
    da_s,
    da_r,
    fz_s,
    fz_r,
    sw_s,
    sw_r,
    h_s,
    h_r,
    g_s,
    g_r,
    v_s,
    v_r,
):
    clips, half, width = own_ref.shape
    pairs = width // 128
    dim = rows_ref.shape[1]
    shard = g1_ref.shape[0]
    chunks = g2_ref.shape[0]
    per = (chunks - 1) // 2
    rows4 = 4 * shard
    d, c, t, dev = partners()
    moves = (d % 2) != (c // 2)
    greet([dev[k] for k in ("x", "z1", "z2", "core", "y", "swap")])

    def start(copies):
        for cp in copies:
            cp.start()

    def wait(copies):
        for cp in copies:
            cp.wait()

    units = [(i, p) for i in range(clips) for p in range(pairs)]
    do_copies = [
        remote(do_send_ref.at[i], do_got.at[i], do_s.at[i], do_r.at[i], dev["x"]) for i in range(clips)
    ]
    start(do_copies)
    loads = [
        pltpu.make_async_copy(
            kv_hbm.at[:, i, p], kv_scr.at[:, i, p], kv_sem.at[i, p]
        )
        for i, p in units
    ]
    start(loads)
    late = [
        pltpu.make_async_copy(x_hbm, x_scr, in_sem.at[0]),
        pltpu.make_async_copy(wf_hbm, wf_scr, in_sem.at[1]),
        pltpu.make_async_copy(d1_hbm, d1_scr, in_sem.at[2]),
    ]
    start(late)
    y_swap = remote(y_ref, yh_ref, y_s.at[0], y_r.at[0], dev["swap"])
    y_keep = pltpu.make_async_copy(y_ref, yh_ref, keep_sem.at[0])

    def y_start():
        @pl.when(moves)
        def _():
            y_swap.start()

        @pl.when(jnp.logical_not(moves))
        def _():
            y_keep.start()

    def grad(ch):
        if ch < per:
            return up_hbm.at[ch]
        if ch < 2 * per:
            return dn_hbm.at[ch - per]
        return wo_hbm

    def band(block):
        return pl.ds(pl.multiple_of(block * rows4, rows4), rows4)

    def strip(block):
        return pl.ds(pl.multiple_of(block * shard, shard), shard)

    mine = [d, flip(d, 1)]
    theirs = [flip(d, 0), flip(flip(d, 0), 1)]

    def g_copy(ch, k, src, dst, device):
        return remote(src, dst, g_s.at[ch, k], g_r.at[ch, k], device)

    def g_stages(ch):
        return [
            [
                g_copy(ch, k, grad(ch).at[:, band(theirs[k])], rc_scr.at[ch, k], dev["core"])
                for k in range(2)
            ],
            [
                g_copy(ch, 2, rc_scr.at[ch, 0, 1], ry_scr.at[ch, 0], dev["x"]),
                g_copy(ch, 7, rc_scr.at[ch, 1, 1], ry_scr.at[ch, 1], dev["x"]),
            ]
            if ch in X_FIRST
            else [g_copy(ch, 2, rc_scr.at[ch, 1], ry_scr.at[ch], dev["y"])],
            [g_copy(ch, 3, ry_scr.at[ch, 1], rx_scr.at[ch], dev["y" if ch in X_FIRST else "x"])],
            [
                g_copy(ch, 4, rx_scr.at[ch, strip(flip(c, 0))], rz1_scr.at[ch, 0], dev["z1"]),
                g_copy(
                    ch, 5, rx_scr.at[ch, strip(flip(flip(c, 0), 1))], rz1_scr.at[ch, 1], dev["z1"]
                ),
            ],
            [g_copy(ch, 6, rz1_scr.at[ch, 1], rz2_scr.at[ch], dev["z2"])],
        ]

    stages = [g_stages(ch) for ch in range(chunks)]
    seen = [ch for kind, ch in ORDER if kind == "g"]
    firsts = [n for n, ch in enumerate(seen) if seen[:n].count(ch) == 1]
    turns = [seen[n] for n in firsts]

    def own_loads(ch):
        slot = turns.index(ch) % 2
        return [
            pltpu.make_async_copy(
                grad(ch).at[:, band(mine[k])], loc_scr.at[slot, k], loc_sem.at[slot, k]
            )
            for k in range(2)
        ]

    reached = [-1] * chunks

    def g_step(ch):
        k = reached[ch]
        if k >= 0:
            wait(stages[ch][k])
        if k == 0:
            turn = turns.index(ch)
            wait(own_loads(ch))
            for m in range(2):
                rc_scr[ch, m] = rc_scr[ch, m] + loc_scr[turn % 2, m]
            if turn + 2 < chunks:
                start(own_loads(turns[turn + 2]))
        elif k == 1:
            if ch in X_FIRST:
                for m in range(2):
                    ry_scr[ch, m] = ry_scr[ch, m] + rc_scr[ch, m, 0]
            else:
                ry_scr[ch] = ry_scr[ch] + rc_scr[ch, 0]
        elif k == 2:
            rx_scr[ch] = rx_scr[ch] + ry_scr[ch, 0]
        elif k == 3:
            rz1_scr[ch, 0] = rz1_scr[ch, 0] + rx_scr[ch, strip(c)]
            rz1_scr[ch, 1] = rz1_scr[ch, 1] + rx_scr[ch, strip(flip(c, 1))]
        elif k == 4:
            g2_ref[ch] = rz1_scr[ch, 0].astype(F32) + rz2_scr[ch].astype(F32)
        if k + 1 < len(stages[ch]):
            start(stages[ch][k + 1])
        reached[ch] = k + 1

    start(own_loads(turns[0]))
    start(own_loads(turns[1]))

    def dkv_copies(u):
        i, p = u
        return [
            remote(
                kv_scr.at[2 * m + 1, i, p],
                core_got.at[m, i, p],
                dc_s.at[m, i, p],
                dc_r.at[m, i, p],
                dev["core"],
            )
            for m in range(2)
        ]

    to_core = [dkv_copies(u) for u in units]

    do_here = []

    def attention(n):
        i, p = units[n]
        cols = pl.ds(p * 128, 128)
        if i not in do_here:
            do_here.append(i)
            do_copies[i].wait()
        loads[n].wait()
        q = q_ref[i, :, cols]
        do = jnp.concatenate([do_own_ref[i, :, cols], do_got[i, :, cols]], axis=0)
        o = jnp.concatenate([own_ref[i, :, cols], send_ref[i, :, cols]], axis=0)
        prod_t = (do.astype(F32) * o.astype(F32)).T
        qq, dd = both_heads(q), both_heads(do)
        delta = jnp.concatenate(
            [jnp.sum(prod_t[h * HD : (h + 1) * HD, :], axis=0, keepdims=True) for h in range(2)],
            axis=1,
        )
        lse = lse_ref[i, p]
        dq_t = jnp.zeros((128, 2 * q.shape[0]), F32)
        rows = kv_scr.shape[3]
        for s in range(0, 4, 2):
            k = jnp.concatenate([kv_scr[s + m, i, p, :, 0:128] for m in range(2)], axis=0)
            v = jnp.concatenate([kv_scr[s + m, i, p, :, 128:256] for m in range(2)], axis=0)
            prob = jnp.exp(mm_nt(k, qq) - lse)
            dv = mm(prob.astype(BF), dd)
            ds = (prob * (mm_nt(v, dd) - delta)).astype(BF)
            dk = mm(ds, qq)
            dq_t = dq_t + mm(k.T, ds)
            for m in range(2):
                part = slice(m * rows, (m + 1) * rows)
                kv_scr[s + m, i, p, :, 0:128] = dk[part].astype(BF)
                kv_scr[s + m, i, p, :, 128:256] = dv[part].astype(BF)
        dq_scr[i, :, cols] = (fold_heads(dq_t, q.shape[0]) * score_scale).astype(BF)
        start(to_core[n])

    gain, shift = rows_ref[0:1, :], rows_ref[2:3, :]
    sums = {
        "gain": jnp.zeros((1, dim), F32),
        "da": jnp.zeros((1, dim), F32),
        "q": jnp.zeros((1, width), F32),
        "v": jnp.zeros((1, width), F32),
    }
    def da_x(i, j):
        return remote(da_send.at[i, j], da_got.at[i, j], da_s.at[i, j], da_r.at[i, j], dev["x"])

    da_xs = [[da_x(i, j) for j in range(2)] for i in range(clips)]
    da_zs = [remote(far_scr.at[i], far_got.at[i], fz_s.at[i], fz_r.at[i], dev["z1"]) for i in range(clips)]

    def project_back(i):
        if i == 0:
            wait(late)
        for n, u in enumerate(units):
            if u[0] == i:
                wait(to_core[n])
        for s in (3, 1, 2, 0):
            m = s // 2
            rows = pl.ds((s % 2) * half, half)
            normed, _ = normed_rows(x_scr[s, i].astype(F32))
            act_t = (normed * gain + shift).astype(BF).T
            halves = [
                kv_scr[2 * m, i, p, rows, :] + core_got[m, i, p, rows, :] for p in range(pairs)
            ]
            g = jnp.concatenate(
                ([] if m else [dq_scr[i, rows, :]])
                + [v[:, :128] for v in halves]
                + [v[:, 128:] for v in halves],
                axis=1,
            )
            cols = slice(width, 3 * width) if m else slice(0, 3 * width)
            da = mm_nt(g, wf_scr[:, cols])
            part = mm(act_t, g)
            if i == 0 and s == 3:
                acc_scr[:, :width] = jnp.zeros((dim, width), F32)
                acc_scr[:, width:] = part
            else:
                acc_scr[:, cols] += part
            total = jnp.sum(g.astype(F32), axis=0, keepdims=True)
            if m == 0:
                sums["q"] = sums["q"] + total[:, :width]
            sums["v"] = sums["v"] + total[:, total.shape[1] - width :]
            sums["gain"] = sums["gain"] + jnp.sum(da * normed, axis=0, keepdims=True)
            sums["da"] = sums["da"] + jnp.sum(da, axis=0, keepdims=True)
            if s % 2:
                da_send[i, m] = da.astype(BF)
                da_xs[i][m].start()
            elif m:
                far_scr[i] = da.astype(BF)
            else:
                da_own[i] = da

    def far_back(i):
        da_xs[i][1].wait()
        far_scr[i] = far_scr[i] + da_got[i, 1]
        da_zs[i].start()

    swaps = [
        remote(delta_scr.at[i], dh_ref.at[i], sw_s.at[i], sw_r.at[i], dev["swap"]) for i in range(clips)
    ]
    keeps = [
        pltpu.make_async_copy(delta_scr.at[i], dh_ref.at[i], keep_sem.at[1 + i]) for i in range(clips)
    ]

    def finish(i):
        da_xs[i][0].wait()
        da_zs[i].wait()
        da = da_own[i] + da_got[i, 0].astype(F32) + far_got[i].astype(F32)
        w = da * gain
        normed, inv = normed_rows(x_scr[0, i].astype(F32))
        rows = pl.ds(i * half, half)
        delta_scr[i] = (
            d1_scr[rows, :] + inv * (w - row_mean(w) - normed * row_mean(w * normed))
        ).astype(BF)

        @pl.when(moves)
        def _():
            swaps[i].start()

        @pl.when(jnp.logical_not(moves))
        def _():
            keeps[i].start()

    def h_copy(k, src, dst, device):
        return remote(src, dst, h_s.at[k], h_r.at[k], device)

    h_stages = [
        [h_copy(k, dw_scr.at[band(theirs[k])], c1_scr.at[k], dev["core"]) for k in range(2)],
        [h_copy(2, c1_scr.at[1], y1_scr, dev["y"])],
        [
            h_copy(3, y1_scr.at[strip(flip(c, 0))], p1_scr.at[0], dev["z1"]),
            h_copy(4, y1_scr.at[strip(flip(flip(c, 0), 1))], p1_scr.at[1], dev["z1"]),
        ],
        [h_copy(5, p1_scr.at[1], q1_scr, dev["z2"])],
    ]
    h_reached = [-1]

    def h_step():
        k = h_reached[0]
        if k < 0:
            dw_scr[...] = acc_scr[...].astype(BF)
        else:
            wait(h_stages[k])
        if k == 0:
            for m in range(2):
                c1_scr[m] = c1_scr[m] + dw_scr[band(mine[m]), :]
        elif k == 1:
            y1_scr[...] = y1_scr[...] + c1_scr[0]
        elif k == 2:
            p1_scr[0] = p1_scr[0] + y1_scr[strip(c), :]
            p1_scr[1] = p1_scr[1] + y1_scr[strip(flip(c, 1)), :]
        elif k == 3:
            g1_ref[...] = p1_scr[0].astype(F32) + q1_scr[...].astype(F32)
        if k + 1 < len(h_stages):
            start(h_stages[k + 1])
        h_reached[0] = k + 1

    def small_sums():
        zero = jnp.zeros((1, dim), F32)
        shared = [
            sums["gain"],
            sums_ref[0:1, :],
            sums["da"],
            sums_ref[1:2, :],
            sums_ref[2:3, :],
            sums_ref[3:4, :],
        ]
        ub = [
            jnp.concatenate([db1_ref[s * per + b] for b in range(per)], axis=1) for s in range(2)
        ]
        for r, row in enumerate(shared):
            vs_scr[0, r : r + 1, :] = row
            vs_scr[1, r : r + 1, :] = row
        vs_scr[0, 6:7, :] = jnp.concatenate([sums["q"], sums["v"]], axis=1)
        vs_scr[1, 6:7, :] = zero
        vs_scr[0, 7:8, :] = zero
        vs_scr[1, 7:8, :] = zero
        vs_scr[0, 10:16, :] = jnp.zeros((6, dim), F32)
        vs_scr[1, 10:16, :] = jnp.zeros((6, dim), F32)
        for s in range(2):
            vs_scr[s, 8:9, :] = ub[s][:, :dim]
            vs_scr[s, 9:10, :] = ub[s][:, dim:]
    v_devices = ("x", "core", "y", "z1", "z2")

    def v_copy(k):
        src = vs_scr.at[1] if k == 0 else vs_scr.at[0] if k == 1 else vr_scr.at[k - 1]
        return remote(src, vr_scr.at[k], v_s.at[k], v_r.at[k], dev[v_devices[k]])

    v_copies = [v_copy(k) for k in range(len(v_devices))]

    v_reached = [-1]

    def v_step():
        k = v_reached[0]
        if k < 0:
            small_sums()
        else:
            v_copies[k].wait()
        if k == 0:
            vs_scr[0] = vs_scr[0] + vr_scr[0]
        elif k == 1:
            vr_scr[1] = vr_scr[1] + vs_scr[0]
        elif k > 1:
            vr_scr[k] = vr_scr[k] + vr_scr[k - 1]
        if k + 1 < len(v_devices):
            v_copies[k + 1].start()
        else:
            vec_ref[...] = vr_scr[k]
        v_reached[0] = k + 1

    steps = {
        "y": lambda n: y_start(),
        "u": attention,
        "b": project_back,
        "f": far_back,
        "e": finish,
        "g": g_step,
        "h": lambda n: h_step(),
        "v": lambda n: v_step(),
    }
    for kind, n in ORDER:
        steps[kind](n)

    @pl.when(moves)
    def _():
        y_swap.wait()
        wait(swaps)

    @pl.when(jnp.logical_not(moves))
    def _():
        y_keep.wait()
        wait(keeps)


def end_call(q, kv, own, send, lse, do_own, do_send, x, wf, rows, d1, y, up, dn, wo, sums, db1):
    clips, half, width = own.shape
    pairs = width // 128
    dim = rows.shape[1]
    shard = dim // 16
    per, _, _, block = up.shape
    chunks = 2 * per + 1
    any_spec = pl.BlockSpec(memory_space=pl.ANY)
    vmem = pl.BlockSpec(memory_space=pltpu.VMEM)
    dma = pltpu.SemaphoreType.DMA
    rows4 = 4 * shard
    both = lambda *shape: [dma(shape), dma(shape)]
    return pl.pallas_call(
        end_kernel,
        in_specs=[vmem, any_spec, vmem, vmem, vmem, vmem, vmem, any_spec, any_spec, vmem]
        + [any_spec, vmem]
        + [any_spec] * 3
        + [vmem, vmem],
        out_specs=[any_spec, any_spec, vmem, vmem, vmem],
        out_shape=(
            jax.ShapeDtypeStruct((clips, half, dim), BF),
            jax.ShapeDtypeStruct((clips, half, dim), BF),
            jax.ShapeDtypeStruct((chunks, shard, block), F32),
            jax.ShapeDtypeStruct((shard, 3 * width), F32),
            jax.ShapeDtypeStruct((16, dim), F32),
        ),
        scratch_shapes=[
            pltpu.VMEM(kv.shape, BF),
            pltpu.VMEM(x.shape, BF),
            pltpu.VMEM(wf.shape, BF),
            pltpu.VMEM(d1.shape, F32),
            pltpu.VMEM(do_send.shape, BF),
            pltpu.VMEM((2, clips, pairs, 2 * half, 256), BF),
            pltpu.VMEM(q.shape, BF),
            pltpu.VMEM((dim, 3 * width), F32),
            pltpu.VMEM((dim, 3 * width), BF),
            pltpu.VMEM((clips, half, dim), F32),
            pltpu.VMEM((clips, 2, half, dim), BF),
            pltpu.VMEM((clips, 2, half, dim), BF),
            pltpu.VMEM((clips, half, dim), BF),
            pltpu.VMEM((clips, half, dim), BF),
            pltpu.VMEM((clips, half, dim), BF),
            pltpu.VMEM((2, 2, 2, rows4, block), BF),
            pltpu.VMEM((chunks, 2, 2, rows4, block), BF),
            pltpu.VMEM((chunks, 2, rows4, block), BF),
            pltpu.VMEM((chunks, rows4, block), BF),
            pltpu.VMEM((chunks, 2, shard, block), BF),
            pltpu.VMEM((chunks, shard, block), BF),
            pltpu.VMEM((2, rows4, 3 * width), BF),
            pltpu.VMEM((rows4, 3 * width), BF),
            pltpu.VMEM((2, shard, 3 * width), BF),
            pltpu.VMEM((shard, 3 * width), BF),
            pltpu.VMEM((2, 16, dim), F32),
            pltpu.VMEM((5, 16, dim), F32),
            dma((clips, pairs)),
            dma((3,)),
            dma((2, 2)),
            dma((1 + clips,)),
            *both(clips),
            *both(1),
            *both(2, clips, pairs),
            *both(clips, 2),
            *both(clips),
            *both(clips),
            *both(6),
            *both(chunks, 8),
            *both(5),
        ],
        compiler_params=pltpu.CompilerParams(
            collective_id=2, has_side_effects=True, vmem_limit_bytes=62 * MIB
        ),
        cost_estimate=pl.CostEstimate(
            flops=20 * 10**9, bytes_accessed=40 * MIB, transcendentals=11 * 10**6
        ),
        name="attend_back_end",
    )(q, kv, own, send, lse, do_own, do_send, x, wf, rows, d1, y, up, dn, wo, sums, db1)


def update_kernel(rates, *refs):
    g1_ref, g2_ref, vec_ref = refs[0:3]
    params, firsts, seconds = refs[3:11], refs[11:27:2], refs[12:27:2]
    grads, news, firsts_next, seconds_next = refs[27:35], refs[35:43], refs[43:59:2], refs[44:59:2]
    qkv, proj, up, down, gains, shifts, qv, ub = range(8)
    shard, width = params[proj].shape
    per = (g2_ref.shape[0] - 1) // 2
    block = g2_ref.shape[2]
    dim = vec_ref.shape[1]
    me = lax.axis_index("dp") * lax.axis_size("ctx") + lax.axis_index("ctx")

    def write(n, at, g):
        rate, decay = rates[n]
        new, one, two = adam_step(params[n][at], firsts[n][at], seconds[n][at], g, rate, decay)
        grads[n][at] = g
        news[n][at] = new
        firsts_next[n][at] = one
        seconds_next[n][at] = two

    everything = slice(None)
    for j in range(3):
        write(qkv, j, g1_ref[:, j * width : (j + 1) * width])
    for b in range(per):
        cols = (everything, slice(b * block, (b + 1) * block))
        write(up, cols, g2_ref[b])
        write(down, cols, g2_ref[per + b])
    write(proj, (everything, everything), g2_ref[2 * per, :, :width])

    def front(per_device):
        return pltpu.roll(vec_ref[...], lax.rem(dim - me * per_device, dim), 1)

    rows = front(shard)
    write(gains, (everything, everything), rows[0:2, :shard])
    write(shifts, (everything, everything), rows[2:6, :shard])
    cols = params[qv].shape[1]
    heads = params[qv].shape[2]
    rows = front(cols)
    for j in range(2):
        parts = [rows[6:7, (j * heads + h) * HD : (j * heads + h) * HD + 128] for h in range(heads - 1)]
        last = rows[6:7, (j * heads + heads - 2) * HD : (j * heads + heads) * HD]
        parts.append(pltpu.roll(last, HD, 1))
        square = jnp.concatenate(parts + [jnp.zeros((128 - heads, 128), F32)], axis=0).T
        write(qv, j, square[:cols, :heads])
    cols, lines = params[ub].shape
    rows = front(cols)
    each = dim // 128
    parts = [
        rows[8 + r // each : 9 + r // each, (r % each) * 128 : (r % each + 1) * 128]
        for r in range(lines)
    ]
    square = jnp.concatenate(parts + [jnp.zeros((128 - lines, 128), F32)], axis=0).T
    write(ub, (everything, everything), square[:cols, :lines])


def update_call(g1, g2, vec, params, moments, rates):
    shapes = [jax.ShapeDtypeStruct(p.shape, F32) for p in params]
    vmem = pl.BlockSpec(memory_space=pltpu.VMEM)
    out = shapes + shapes + [s for s in shapes for _ in range(2)]
    return pl.pallas_call(
        functools.partial(update_kernel, rates),
        in_specs=[vmem] * 27,
        out_specs=[vmem] * 32,
        out_shape=out,
        compiler_params=pltpu.CompilerParams(vmem_limit_bytes=48 * MIB),
        cost_estimate=pl.CostEstimate(flops=10**7, bytes_accessed=8 * MIB, transcendentals=10**6),
        name="update",
    )(g1, g2, vec, *params, *moments)


class Links:
    def __init__(self, mesh):
        self.dp = mesh.shape["dp"]
        self.ctx = mesh.shape["ctx"]
        self.tensor = mesh.shape["tensor"]
        self.dp_bits = self.dp.bit_length() - 1
        self.ctx_bits = self.ctx.bit_length() - 1

    def flat(self, d, c, t):
        return (d * self.ctx + c) * self.tensor + t

    def move(self, value, partner):
        pairs = []
        for d in range(self.dp):
            for c in range(self.ctx):
                for t in range(self.tensor):
                    other = partner(d, c, t)
                    if other != (d, c, t):
                        pairs.append((self.flat(d, c, t), self.flat(*other)))
        return lax.ppermute(value, ("dp", "ctx", "tensor"), pairs)

    def across_x(self, value):
        return self.move(value, lambda d, c, t: (d, c, t ^ 1))

    def across_core(self, value):
        return self.move(value, lambda d, c, t: (d ^ 1, c, t))

    def across_z(self, value):
        return self.move(value, lambda d, c, t: (d, c ^ 1, t))

    def stays(self):
        d, c = lax.axis_index("dp"), lax.axis_index("ctx")
        return (d % 2) == (c // (self.ctx // 2))

    def swap(self, value):
        half = self.ctx // 2
        moved = self.move(
            value,
            lambda d, c, t: (d, c, t) if d % 2 == c // half else (d ^ 1, c ^ half, t),
        )
        return jnp.where(self.stays(), value, moved)

    def stages(self):
        out = []
        for bit in reversed(range(self.ctx_bits)):
            out.append(("ctx", bit, self.ctx_bits - 1 - bit))
        for bit in reversed(range(self.dp_bits)):
            out.append(("dp", bit, self.dp_bits - 1 - bit))
        return out

    def step(self, value, axis, bit):
        if axis == "ctx":
            return self.move(value, lambda d, c, t: (d, c ^ (1 << bit), t))
        return self.move(value, lambda d, c, t: (d ^ (1 << bit), c, t))

    def side(self, axis, bit):
        return (lax.axis_index(axis) // (1 << bit)) % 2

    def gather(self, value, both):
        shape = value.shape
        lead = 0
        for axis, bit, place in self.stages():
            if axis == "dp" and both and not lead:
                value = jnp.stack([value, self.across_x(value)])
                lead = 1
            got = self.step(value, axis, bit)
            low = self.side(axis, bit) == 0
            value = jnp.stack(
                [jnp.where(low, value, got), jnp.where(low, got, value)], axis=lead + place
            )
        shards = self.dp * self.ctx
        return value.reshape((2,) * lead + (shards * shape[0],) + shape[1:])

    def scatter(self, value, both):
        lead = 1 if both else 0
        rest = value.shape[lead + 1 :]
        value = value.reshape(
            value.shape[:lead] + (2,) * (self.dp_bits + self.ctx_bits) + rest
        )
        for axis, bit, place in reversed(self.stages()):
            if axis == "ctx" and lead:
                value = value[0] + self.across_x(value[1])
                lead = 0
            side = self.side(axis, bit)
            keep = lax.dynamic_index_in_dim(value, side, lead + place, keepdims=False)
            give = lax.dynamic_index_in_dim(value, 1 - side, lead + place, keepdims=False)
            value = keep + self.step(give, axis, bit)
        return value


def body(links, *args):
    (
        block_input,
        out_cotangent,
        qkv_weight,
        proj_weight,
        up_weight,
        down_weight,
        norm_gains,
        shift_terms,
        qv_bias,
        up_bias,
        qkv_first,
        qkv_second,
        proj_first,
        proj_second,
        up_first,
        up_second,
        down_first,
        down_second,
        gains_first,
        gains_second,
        shifts_first,
        shifts_second,
        qv_bias_first,
        qv_bias_second,
        up_bias_first,
        up_bias_second,
    ) = args
    half, clips, dim = block_input.shape
    shard = qkv_weight.shape[0]
    shards = dim // shard
    width = qkv_weight.shape[2]
    hidden = up_weight.shape[1]
    heads = width // HD

    x_home = jnp.transpose(block_input, (1, 0, 2)).astype(BF)
    gy_home = jnp.transpose(out_cotangent, (1, 0, 2)).astype(BF)
    x = links.swap(x_home)
    x_own = [x[i] for i in range(clips)]
    x_got = [links.across_x(v) for v in x_own]

    def lanes(parts):
        flat = jnp.concatenate([p.astype(BF).reshape(-1) for p in parts])
        return jnp.pad(flat, (0, shard * 128 - flat.size)).reshape(shard, 128)

    first = jnp.concatenate(
        [qkv_weight.reshape(shard, 3 * width).astype(BF), lanes([norm_gains, shift_terms, qv_bias])],
        axis=1,
    )
    second = jnp.concatenate(
        [up_weight.astype(BF), down_weight.astype(BF), proj_weight.astype(BF), lanes([up_bias])],
        axis=1,
    )
    first = links.gather(first, False)
    second = links.gather(second, True)
    w_qkv = first[:, : 3 * width]
    small = first[:, 3 * width :].reshape(shards, shard * 128)
    n_g, n_s = 2 * shard, 4 * shard
    gains = jnp.transpose(small[:, :n_g].reshape(shards, 2, shard), (1, 0, 2)).reshape(2, dim)
    shifts = jnp.transpose(
        small[:, n_g : n_g + n_s].reshape(shards, 4, shard), (1, 0, 2)
    ).reshape(4, dim)
    qv_cols = qv_bias.shape[2]
    biases = jnp.transpose(
        small[:, n_g + n_s : n_g + n_s + qv_bias.size].reshape(shards, 2, heads, qv_cols),
        (1, 2, 0, 3),
    ).reshape(2, width)
    ub_rows, ub_cols = up_bias.shape
    b1 = jnp.transpose(
        second[:, :, 2 * hidden + width :]
        .reshape(2, shards, shard * 128)[:, :, : up_bias.size]
        .reshape(2, shards, ub_rows, ub_cols),
        (0, 2, 1, 3),
    ).reshape(2, hidden)
    gains, shifts, biases, b1 = (v.astype(F32) for v in (gains, shifts, biases, b1))
    zero4 = jnp.zeros((4, dim), F32)
    rows_one = jnp.concatenate([gains[0:1], shifts[0:1], zero4, zero4[:2]])
    rows_two = jnp.concatenate([gains[1:2], shifts[1:4], zero4])
    biases = jnp.concatenate([biases, jnp.zeros((6, width), F32)])

    q, pieces, o_own, o_send, o_got, lse = [], [], [], [], [], []
    for i in range(clips):
        q_i, kv = qkv_call(x_own[i], x_got[i], w_qkv, rows_one, biases)
        kv_z = links.across_z(kv)
        kv_c = links.across_core(kv)
        kv_d = links.across_core(kv_z)
        q.append(q_i)
        pieces.append((kv, kv_c, kv_z, kv_d))
    gy = links.swap(gy_home)
    for i in range(clips):
        own, send, lse_i = attend_call(q[i], pieces[i])
        o_own.append(own)
        o_send.append(send)
        o_got.append(links.across_x(send))
        lse.append(lse_i)

    tokens = clips * half
    y, d1, do_own, do_send, d_up, d_down, d_proj, sums_two, d_b1 = ffn_call(
        o_own, o_got, x.reshape(tokens, dim), gy.reshape(tokens, dim), second, b1, rows_two
    )
    y_home = links.swap(y.reshape(clips, half, dim))
    block_output = block_input + jnp.transpose(y_home, (1, 0, 2)).astype(F32)

    grads_two = jnp.concatenate([d_up, d_down, d_proj], axis=2)
    grads_two = links.scatter(grads_two.reshape(2, shards, shard, -1), True)

    dq, dk, dv = [], [], []
    do_got = [links.across_x(v) for v in do_send]
    for i in range(clips):
        dq_i, dks, dvs = attend_back_call(
            q[i], do_own[i], do_got[i], o_own[i], o_send[i], lse[i], pieces[i]
        )
        dq.append(dq_i)
        for parts, out in ((dks, dk), (dvs, dv)):
            mine, core, z, diag = parts
            mine = mine + links.across_core(core)
            z = z + links.across_core(diag)
            out.append(mine + links.across_z(z))
    da_own, da_send, d_qkv, sums_one, sums_bias = back_call(
        x_own, x_got, dq, dk, dv, w_qkv, rows_one
    )
    grads_one = links.scatter(d_qkv.reshape(shards, shard, 3 * width), False)
    d1 = d1.reshape(clips, half, dim)
    deltas = []
    for i in range(clips):
        da = da_own[i].astype(F32) + links.across_x(da_send[i]).astype(F32)
        normed, inv = normed_rows(x_own[i].astype(F32))
        w = da * gains[0]
        deltas.append(
            (d1[i] + inv * (w - row_mean(w) - normed * row_mean(w * normed))).astype(BF)
        )
    delta_home = links.swap(jnp.stack(deltas))
    input_grad = out_cotangent + jnp.transpose(delta_home, (1, 0, 2)).astype(F32)

    cot_sum = jnp.sum(out_cotangent, axis=(0, 1))[None]
    both = jnp.concatenate(
        [sums_one[0:1], sums_two[0:1], sums_one[1:2], sums_two[1:2], sums_two[2:3], cot_sum]
    )
    both = jnp.transpose(both.reshape(6, shards, shard), (1, 0, 2)).reshape(shards, 6 * shard)
    ub = jnp.transpose(d_b1.reshape(2, ub_rows, shards, ub_cols), (0, 2, 1, 3)).reshape(
        2, shards, up_bias.size
    )
    crossed = links.across_x(jnp.concatenate([both, ub[1]], axis=1))
    qv = jnp.transpose(
        sums_bias[0:2].reshape(2, heads, shards, qv_cols), (2, 0, 1, 3)
    ).reshape(shards, qv_bias.size)
    vec = jnp.concatenate([jnp.concatenate([both, ub[0]], axis=1) + crossed, qv], axis=1)
    vec = links.scatter(vec, False)
    gains_grad = vec[:n_g].reshape(2, shard)
    shifts_grad = vec[n_g : n_g + n_s].reshape(4, shard)
    up_bias_grad = vec[6 * shard : 6 * shard + up_bias.size].reshape(up_bias.shape)
    qv_bias_grad = vec[6 * shard + up_bias.size :].reshape(qv_bias.shape)

    qkv_grad = grads_one.astype(F32).reshape(qkv_weight.shape)
    grads_two = grads_two.astype(F32)
    up_grad = grads_two[:, :hidden]
    down_grad = grads_two[:, hidden : 2 * hidden]
    proj_grad = grads_two[:, 2 * hidden :]

    qkv_next = adam_step(qkv_weight, qkv_first, qkv_second, qkv_grad, rate_qkv, decay_rate)
    proj_next = adam_step(proj_weight, proj_first, proj_second, proj_grad, rate_proj, decay_rate)
    up_next = adam_step(up_weight, up_first, up_second, up_grad, rate_up, decay_rate)
    down_next = adam_step(down_weight, down_first, down_second, down_grad, rate_down, decay_rate)
    gains_next = adam_step(norm_gains, gains_first, gains_second, gains_grad, rate_gains, 0.0)
    shifts_next = adam_step(shift_terms, shifts_first, shifts_second, shifts_grad, rate_shifts, 0.0)
    qv_next = adam_step(qv_bias, qv_bias_first, qv_bias_second, qv_bias_grad, rate_query_bias, 0.0)
    ub_next = adam_step(up_bias, up_bias_first, up_bias_second, up_bias_grad, rate_up_bias, 0.0)
    nexts = (qkv_next, proj_next, up_next, down_next, gains_next, shifts_next, qv_next, ub_next)
    return (
        block_output,
        input_grad,
        qkv_grad,
        proj_grad,
        up_grad,
        down_grad,
        gains_grad,
        shifts_grad,
        qv_bias_grad,
        up_bias_grad,
        *(n[0] for n in nexts),
        *(m for n in nexts for m in n[1:]),
    )


def body_fused(links, *args):
    block_input, out_cotangent = args[0:2]
    moments = args[10:]

    orders = ((1, 0, 2), (0, 1), (0, 1), (0, 1), (0, 1), (0, 1), (0, 2, 1), (1, 0))
    backs = ((1, 0, 2), (0, 1), (0, 1), (0, 1), (0, 1), (0, 1), (0, 2, 1), (1, 0))
    turned = [jnp.transpose(v, o) for v, o in zip(args[2:10], orders)]
    x, wf, _, rows, q, kv, own, send, lse, y, d1, do_own, do_send, up, dn, wo, sums, db1 = start_call(
        jnp.transpose(block_input, (1, 0, 2)), jnp.transpose(out_cotangent, (1, 0, 2)), *turned
    )
    y_home, delta_home, g2, g1, vec = end_call(
        q,
        kv,
        own,
        send,
        lse,
        do_own,
        do_send,
        x,
        wf,
        rows,
        d1,
        y,
        up,
        dn,
        wo,
        sums,
        db1,
    )
    block_output = block_input + jnp.transpose(y_home, (1, 0, 2)).astype(F32)
    input_grad = out_cotangent + jnp.transpose(delta_home, (1, 0, 2)).astype(F32)

    rates = (
        (rate_qkv, decay_rate),
        (rate_proj, decay_rate),
        (rate_up, decay_rate),
        (rate_down, decay_rate),
        (rate_gains, 0.0),
        (rate_shifts, 0.0),
        (rate_query_bias, 0.0),
        (rate_up_bias, 0.0),
    )
    turned_moments = [jnp.transpose(v, orders[n // 2]) for n, v in enumerate(moments)]
    out = update_call(g1, g2, vec, turned, turned_moments, rates)
    places = list(range(8)) * 2 + [n // 2 for n in range(16)]
    return (block_output, input_grad, *(jnp.transpose(v, backs[n]) for v, n in zip(out, places)))


def solution(mesh):
    rows = P(("ctx", "tensor"), "dp", None)
    qkv = P(("dp", "ctx"), None, "tensor")
    mat = P(("dp", "ctx"), "tensor")
    norm = P(None, ("dp", "ctx"))
    qv = P(None, "tensor", ("dp", "ctx"))
    ub = P("tensor", ("dp", "ctx"))
    each = (qkv, mat, mat, mat, norm, norm, qv, ub)
    moments = tuple(s for s in each for _ in range(2))
    fused = (mesh.shape["dp"], mesh.shape["ctx"], mesh.shape["tensor"]) == (4, 4, 2)
    return jax.shard_map(
        functools.partial(body_fused if fused else body, Links(mesh)),
        mesh=mesh,
        in_specs=(rows, rows) + each + moments,
        out_specs=(rows, rows) + each + each + moments,
        check_vma=False,
    )
```
